32 devices in a mesh: gx: 8 (over z, y), gy: 4 (over x, core).
Axes of the slice: x: 2, y: 2, z: 4, core: 2. Of those that a mesh axis runs over, the one named last changes fastest.
Arguments:
- bus_start: float32 [4, 524288], P(None, ('gx', 'gy')), may hold values from -6 to 6
- bus_target: float32 [4, 524288], P(None, ('gx', 'gy')), may hold values from -6 to 6
- bus_weight: float32 [4, 524288], P(None, ('gx', 'gy')), may hold values from 0.25 to 4
- inner_ends: int32 [2, 655360], P(None, ('gx', 'gy')), may hold values from 0 to 16383, as said below
- cross_from: int32 [131072], P(('gx', 'gy')), may hold values from 0 to 16383, as said below
- boundary_lists: int32 [32, 4096], P(('gx', 'gy')), may hold values from 0 to 16383, as said below
- kkt_map: float32 [8, 8, 786432], P(None, None, ('gx', 'gy'))
- active_set: int32 [8, 786432], P(None, ('gx', 'gy')), may hold values 0 or 1
- limits: float32 [8, 786432], P(None, ('gx', 'gy')), may hold values from -3 to 3
- penalty_level: int32 [786432], P(('gx', 'gy')), may hold values from 1 to 8
- hv_bus: int32 [1024], P(('gx', 'gy')), may hold values from 0 to 16383
- hv_partner: int32 [1024], P(('gx', 'gy')), may hold values from 0 to 1023, as said below
- hv_level: int32 [1024], P(('gx', 'gy')), may hold values from 1 to 8
Outputs:
- bus_state: float32 [4, 524288], P(None, ('gx', 'gy'))
- branch_dual: float32 [8, 786432], P(None, ('gx', 'gy'))
- hv_dual: float32 [1024], P(('gx', 'gy'))
The draws below stay inside these ranges and needn't reach their ends.
Inputs may be any that keep to these rules, and one draw needn't show every extreme that they name: `inner_ends`: local bus indices; both ends of a device's interior branch j lie in its cluster j // 320, that is among local buses 256 * (j // 320) to 256 * (j // 320) + 255. `cross_from`: local bus index; a device's crossing branch j has its own end in its cluster j // 64, that is among local buses 256 * (j // 64) to 256 * (j // 64) + 255. `hv_bus`: local bus index on the terminal's own device. `hv_partner`: links pair terminals: the partner of a terminal's partner is the terminal itself, and it lies on another device; two devices share either no link or exactly 2 links. `boundary_lists`: within a row all entries are distinct local bus indices; position i of each list lies in cluster i // 16, that is among local buses 256 * (i // 16) to 256 * (i // 16) + 255.
All inputs are finite; a program needn't handle non-finite values. No bound on the sum of `active_set` on one device may be relied on, other than what follows from the above.
Results may differ from the reference program's by a relative error of at most 0.000052.
Values sent between devices are 32-bit elements; how exact they have to be, the bound alone decides.
No kernel may reach another device: no remote copies, remote signals or barrier semaphores. Data moves between devices by JAX's collectives and lax.ppermute only.
A program may use at most 128 MiB of HBM per device.

```python
import math
import jax
import jax.numpy as jnp
from jax import lax

C = 4
K = 8
BLK = 256
BUS_DEV = 16384
NBD = 1024
CROSS = 4096
BR_IN = 20480
BR = 24576
TILES = 32
CAP = 2
HV_DEV = 32
ITERS = 2
N_GX = 8
N_GY = 4


def draw_inner_ends(key, part):
    local = jnp.arange(TILES * BR_IN, dtype=jnp.int32) % BR_IN
    cluster = local // (BR_IN // (BUS_DEV // BLK))
    offsets = jax.random.randint(jax.random.fold_in(key, 17), (2, TILES * BR_IN), 0, BLK, dtype=jnp.int32)
    return (cluster[None, :] * BLK + offsets).astype(jnp.int32)


def draw_cross_from(key, part):
    local = jnp.arange(TILES * CROSS, dtype=jnp.int32) % CROSS
    cluster = local // (CROSS // (BUS_DEV // BLK))
    offsets = jax.random.randint(jax.random.fold_in(key, 19), (TILES * CROSS,), 0, BLK, dtype=jnp.int32)
    return (cluster * BLK + offsets).astype(jnp.int32)


def draw_boundary_lists(key, part):
    cluster_count = BUS_DEV // BLK
    per_list = NBD // cluster_count
    tile_keys = jax.random.split(jax.random.fold_in(key, 3), TILES * cluster_count)
    chosen = jax.vmap(lambda single: jax.random.permutation(single, BLK)[:4 * per_list])(tile_keys)
    chosen = chosen.reshape(TILES, cluster_count, 4, per_list)
    base = (jnp.arange(cluster_count, dtype=jnp.int32) * BLK)[None, :, None, None]
    placed = (chosen + base).transpose(0, 2, 1, 3)
    return placed.reshape(TILES, 4 * NBD).astype(jnp.int32)


def draw_kkt_map(key, part):
    first_key, second_key = jax.random.split(jax.random.fold_in(key, 5))
    count = TILES * BR
    diagonal = jax.random.uniform(first_key, (K, count), jnp.float32, 0.4, 0.8)
    outside = jax.random.uniform(second_key, (K, K, count), jnp.float32, -0.07, 0.07)
    identity = jnp.eye(K, dtype=jnp.float32)[:, :, None]
    return outside * (1.0 - identity) + identity * diagonal[:, None, :]


def draw_hv_partner(key, part):
    first_key, second_key = jax.random.split(jax.random.fold_in(key, 11))
    xor_masks = jax.random.permutation(first_key, TILES - 1)[:HV_DEV // CAP] + 1
    tile_keys = jax.random.split(second_key, TILES)
    position = jax.vmap(lambda single: jax.random.permutation(single, HV_DEV))(tile_keys)
    inverse = jnp.argsort(position, axis=1, stable=True)
    device = jnp.arange(TILES, dtype=jnp.int32)[:, None]
    rounds = inverse // CAP
    partner_dev = jnp.bitwise_xor(device, xor_masks[rounds].astype(jnp.int32))
    landing = position[partner_dev, inverse]
    return (partner_dev * HV_DEV + landing).reshape(-1).astype(jnp.int32)


def with_ends(result, rng, least, largest):
    place = [jax.random.randint(jax.random.fold_in(rng, axis), (), 0, length) for axis, length in enumerate(result.shape)]
    main_axis = result.shape.index(max(result.shape))
    next_to = place[:main_axis] + [(place[main_axis] + 1) % result.shape[main_axis]] + place[main_axis + 1:]
    return result.at[tuple(place)].set(least).at[tuple(next_to)].set(largest)


def shard_levels(key, dims, cuts, least, high):
    def one(dim, shards_of):
        draws = jax.random.uniform(jax.random.fold_in(jax.random.fold_in(key, 6), dim), (shards_of,), jnp.float32, least / len(cuts), high / len(cuts))
        return jnp.repeat(jnp.exp(draws), dims[dim] // shards_of).reshape((-1,) + (1,) * (len(dims) - dim - 1))

    factor_of = one(*cuts[0])
    for cut in cuts[1:]:
        factor_of = factor_of * one(*cut)
    return factor_of


def gaussian(key, dims, deviation, limit, cuts=(), kind=jnp.bfloat16):
    entries = deviation * jax.random.normal(key, dims, jnp.float32)
    if cuts:
        entries = entries * shard_levels(key, dims, cuts, -0.22, 0.18)
    return jnp.clip(entries, -limit, limit).astype(kind)


def setup_inputs(seed: int = 0) -> dict:
    streams_of = jax.random.split(jax.random.key(seed), 14)
    return {
        "bus_start": gaussian(streams_of[0], (C, TILES * BUS_DEV), 1.0, 6.0, ((1, 32),), jnp.float32),
        "bus_target": gaussian(streams_of[1], (C, TILES * BUS_DEV), 1.0, 6.0, ((1, 32),), jnp.float32),
        "bus_weight": jnp.clip(jnp.exp(math.log(4.0) - 2.7725887 * jax.random.uniform(streams_of[2], (C, TILES * BUS_DEV), jnp.float32) ** shard_levels(streams_of[2], (C, TILES * BUS_DEV), ((1, 32),), -0.2, 0.2)), 0.25, 4.0),
        "inner_ends": draw_inner_ends(jax.random.fold_in(streams_of[13], 71), 0),
        "cross_from": draw_cross_from(jax.random.fold_in(streams_of[13], 71), 0),
        "boundary_lists": draw_boundary_lists(jax.random.fold_in(streams_of[13], 71), 0),
        "kkt_map": draw_kkt_map(jax.random.fold_in(streams_of[13], 71), 0),
        "active_set": with_ends((jax.random.randint(streams_of[7], (K, TILES * BR), 0, 8) < 1).astype(jnp.int32), jax.random.fold_in(streams_of[7], 1), 0, 1),
        "limits": gaussian(streams_of[8], (K, TILES * BR), 0.5, 3.0, ((1, 32),), jnp.float32),
        "penalty_level": with_ends(jax.random.randint(streams_of[9], (TILES * BR,), 1, 9), jax.random.fold_in(streams_of[9], 1), 1, 8).astype(jnp.int32),
        "hv_bus": with_ends(jax.random.randint(streams_of[10], (TILES * HV_DEV,), 0, BUS_DEV), jax.random.fold_in(streams_of[10], 1), 0, BUS_DEV - 1).astype(jnp.int32),
        "hv_partner": draw_hv_partner(jax.random.fold_in(streams_of[13], 71), 0),
        "hv_level": with_ends(jax.random.randint(streams_of[12], (TILES * HV_DEV,), 1, 9), jax.random.fold_in(streams_of[12], 1), 1, 8).astype(jnp.int32),
    }


def relax(ends_block, dual_block, kkt_block, active_block, limit_block, penalty_block):
    target = ends_block - dual_block / penalty_block[None, :]
    solved = kkt_block[:, 0, :] * target[0][None, :]
    for column in range(1, target.shape[0]):
        solved = solved + kkt_block[:, column, :] * target[column][None, :]
    return jnp.where(active_block == 1, limit_block, solved)


def moved(blocks, grid_axis, offset):
    tile_grid = blocks.reshape((N_GX, N_GY) + blocks.shape[1:])
    length = tile_grid.shape[grid_axis]
    zeros_rim = jnp.zeros_like(lax.slice_in_dim(tile_grid, 0, 1, axis=grid_axis))
    if offset == 1:
        shifted = jnp.concatenate([zeros_rim, lax.slice_in_dim(tile_grid, 0, length - 1, axis=grid_axis)], axis=grid_axis)
    else:
        shifted = jnp.concatenate([lax.slice_in_dim(tile_grid, 1, length, axis=grid_axis), zeros_rim], axis=grid_axis)
    return shifted.reshape(blocks.shape)


def ghosts(bus_now, list_rows):
    blocks = jax.vmap(lambda single, indices: single[:, indices])(bus_now, list_rows)
    pieces = [moved(blocks[:, :, 0], 0, 1), moved(blocks[:, :, 1], 0, -1),
              moved(blocks[:, :, 2], 1, 1), moved(blocks[:, :, 3], 1, -1)]
    return jnp.concatenate(pieces, axis=2)


def accumulate(end_terms, penalty, from_index, to_index, hv_bus, hv_terms, hv_penalty):
    width_all = BUS_DEV + CROSS
    sums = jnp.zeros((C, width_all), jnp.float32).at[:, from_index].add(end_terms[:C]).at[:, to_index].add(end_terms[C:])
    weight_row = jnp.zeros((width_all,), jnp.float32).at[from_index].add(penalty).at[to_index].add(penalty)
    own_sums = sums[:, :BUS_DEV].at[2, hv_bus].add(hv_terms)
    own_weight = jnp.broadcast_to(weight_row[None, :BUS_DEV], (C, BUS_DEV)).at[2, hv_bus].add(hv_penalty)
    far_pack = jnp.concatenate([sums[:, BUS_DEV:], weight_row[None, BUS_DEV:]], axis=0)
    return own_sums, own_weight, far_pack


def reference(bus_start, bus_target, bus_weight, inner_ends, cross_from, boundary_lists, kkt_map, active_set, limits, penalty_level, hv_bus, hv_partner, hv_level):
    tile_count = N_GX * N_GY

    def by_tile(values_in):
        return values_in.reshape(values_in.shape[0], tile_count, -1).transpose(1, 0, 2)

    def by_branch(values_in):
        return values_in.transpose(1, 0, 2).reshape(values_in.shape[1], -1)

    bus_now = by_tile(bus_start)
    prior_sum = by_tile(bus_weight * bus_target)
    weight_tiles = by_tile(bus_weight)
    list_rows = boundary_lists.reshape(tile_count, 4, NBD)
    inner_tile = by_tile(inner_ends)
    crossing = cross_from.reshape(tile_count, CROSS)
    from_index = jnp.concatenate([inner_tile[:, 0], crossing], axis=1)
    ghost_index = jnp.broadcast_to(BUS_DEV + jnp.arange(CROSS, dtype=jnp.int32), (tile_count, CROSS))
    to_index = jnp.concatenate([inner_tile[:, 1], ghost_index], axis=1)
    penalty = 0.25 * penalty_level.astype(jnp.float32)
    tile_penalty = penalty.reshape(tile_count, BR)
    hv_penalty = 0.25 * hv_level.astype(jnp.float32)
    hv_tiles = hv_bus.reshape(tile_count, HV_DEV)

    def ends_of(bus_now, ghost_now):
        extended = jnp.concatenate([bus_now, ghost_now], axis=2)
        picker = jax.vmap(lambda single, first_end, second: jnp.concatenate([single[:, first_end], single[:, second]], axis=0))
        return by_branch(picker(extended, from_index, to_index))

    def bus_power(bus_now):
        return jax.vmap(lambda single, indices: single[2, indices])(bus_now, hv_tiles).reshape(-1)

    duals = jnp.zeros((K, tile_count * BR), jnp.float32)
    hv_duals = jnp.zeros((tile_count * HV_DEV,), jnp.float32)
    ghost_now = ghosts(bus_now, list_rows)
    ends = ends_of(bus_now, ghost_now)
    for iteration in range(ITERS):
        branch_flow = relax(ends, duals, kkt_map, active_set, limits, penalty)
        hv_value = bus_power(bus_now) - hv_duals / hv_penalty
        far_value = hv_value[hv_partner]
        far_penalty = hv_penalty[hv_partner]
        hv_flow = (hv_penalty * hv_value - far_penalty * far_value) / (hv_penalty + far_penalty)
        end_terms = penalty[None, :] * branch_flow + duals
        tile_terms = end_terms.reshape(K, tile_count, BR).transpose(1, 0, 2)
        hv_terms = (hv_penalty * hv_flow + hv_duals).reshape(tile_count, HV_DEV)
        own_sums, own_weight, far_pack = jax.vmap(accumulate)(tile_terms, tile_penalty, from_index, to_index, hv_tiles, hv_terms, hv_penalty.reshape(tile_count, HV_DEV))
        partial_value = prior_sum + own_sums
        partial_weight = weight_tiles + own_weight
        back_cat = jnp.concatenate([moved(far_pack[:, :, 0:NBD], 0, -1), moved(far_pack[:, :, NBD:2 * NBD], 0, 1),
                                    moved(far_pack[:, :, 2 * NBD:3 * NBD], 1, -1), moved(far_pack[:, :, 3 * NBD:], 1, 1)], axis=2)
        arriving = jax.vmap(lambda indices, values: jnp.zeros((C + 1, BUS_DEV), jnp.float32).at[:, indices].set(values))(boundary_lists, back_cat)
        bus_now = (partial_value + arriving[:, :C]) / (partial_weight + arriving[:, C:])
        ghost_now = ghosts(bus_now, list_rows)
        ends = ends_of(bus_now, ghost_now)
        duals = duals + penalty[None, :] * (branch_flow - ends)
        hv_duals = hv_duals + hv_penalty * (hv_flow - bus_power(bus_now))
    return bus_now.transpose(1, 0, 2).reshape(C, -1), duals, hv_duals
```

```python
import functools

import jax
import jax.numpy as jnp
from jax import lax
from jax.experimental import pallas as pl
from jax.experimental.pallas import tpu as pltpu
from jax.sharding import PartitionSpec as P

F32 = jnp.float32
BF16 = jnp.bfloat16
BLK = 256
LANES = 128
GROUP = 8
PAIR = 2 * BLK
STATIC_ROWS = 25


def swapped(value, axis, first):
    count = lax.axis_size(axis)
    moves = []
    for low in range(first, count - 1, 2):
        moves += [(low, low + 1), (low + 1, low)]
    return lax.ppermute(value, axis, moves)


def to_all(rows):
    return lax.all_to_all(rows, ("gx", "gy"), split_axis=0, concat_axis=0, tiled=True)


def take_lanes(table, lane):
    return jnp.take_along_axis(table, lane, axis=1, mode="promise_in_bounds")


def pick(tables, index, tiles):
    lane, tile = (index & (LANES - 1), index >> 7)
    found = None
    for h in tiles:
        got = take_lanes(tables[h], lane)
        found = got if found is None else jnp.where(tile == h, got, found)
    return found


def spread8(row, rows=8):
    return jnp.broadcast_to(row, (rows, row.shape[-1]))


def one_hot(index, sublane):
    low = spread8(index & (LANES - 1), 16).astype(F32).astype(BF16)
    column = jnp.concatenate([low] * (LANES // 16), axis=0)
    return jnp.where(column == sublane, jnp.ones((), BF16), jnp.zeros((), BF16))


def contract(left, right):
    return lax.dot_general(
        left.astype(BF16), right, (((1,), (1,)), ((), ())), preferred_element_type=F32
    )


def halves(values):
    high = values.astype(BF16).astype(F32)
    return high, values - high


def sublanes():
    return lax.broadcasted_iota(jnp.int32, (LANES, LANES), 0).astype(F32).astype(BF16)


def folded(first, second, distance, mask):
    return jnp.where(
        mask,
        first + pltpu.roll(first, 8 - distance, 0),
        second + pltpu.roll(second, distance, 0),
    )


def product(kkt_ref, cols, target):
    row = lax.broadcasted_iota(jnp.int32, (8, LANES), 0)
    terms = [kkt_ref[8 * i : 8 * i + 8, cols] * target for i in range(8)]
    upper = row < 4
    quads = [
        jnp.where(upper, terms[i], terms[i + 4]) + pltpu.roll(jnp.where(upper, terms[i + 4], terms[i]), 4, 0)
        for i in range(4)
    ]
    even_two = (row & 2) == 0
    twos = [folded(quads[i], quads[i + 2], 2, even_two) for i in range(2)]
    return folded(twos[0], twos[1], 1, (row & 1) == 0)


def doubled(block):
    return block if block.shape[0] == 8 else jnp.concatenate([block, block], axis=0)


def tiles_of(states):
    return [states[:, h * LANES : (h + 1) * LANES] for h in range(states.shape[1] // LANES)]


def inner_ends_of(tables, index_ref, base, cols, t, upper):
    near = index_ref[0:1, cols] - base
    far = index_ref[1:2, cols] - base
    tiles = (0, 1) if t < 2 else (2, 3) if t > 2 else (0, 1, 2, 3)
    both = jnp.where(upper, spread8(near), spread8(far))
    return pick(tables, both, tiles), near, far, tiles


def inner_kernel(first, *refs):
    if first:
        s_ref, index_ref, kkt_ref, act_ref, lim_ref, lev_ref, y_ref, acc_ref, w_ref = refs
    else:
        s_ref, index_ref, kkt_ref, act_ref, lim_ref, lev_ref, old_ref, y_ref, acc_ref = refs
    step = pl.program_id(0)
    states = doubled(s_ref[...])
    upper = lax.broadcasted_iota(jnp.int32, (8, LANES), 0) < 4
    row16 = lax.broadcasted_iota(jnp.int32, (16, LANES), 0)
    sublane = sublanes()
    width = states.shape[1]
    per_pair = kkt_ref.shape[1] // (width // PAIR)
    for p in range(width // PAIR):
        tables = tiles_of(states[:, p * PAIR : (p + 1) * PAIR])
        base = step * width + p * PAIR
        sums = [jnp.zeros((8, LANES), F32)] * 4
        weights = jnp.zeros((16, LANES), F32)
        for t in range(per_pair // LANES):
            cols = slice(p * per_pair + t * LANES, p * per_pair + (t + 1) * LANES)
            ends, near, far, tiles = inner_ends_of(tables, index_ref, base, cols, t, upper)
            penalty = 0.25 * lev_ref[0:1, cols].astype(F32)
            if first:
                scaled, target = (None, ends)
            else:
                scaled = old_ref[:, cols] - ends
                target = ends - scaled
            flows = product(kkt_ref, cols, target)
            flows = jnp.where(act_ref[:, cols] == 1, lim_ref[:, cols], flows)
            y = flows if first else flows + scaled
            y_ref[:, cols] = y
            high, low = halves(spread8(penalty) * y)
            from_part = jnp.where(upper, high, pltpu.roll(low, 4, 0))
            to_part = jnp.where(upper, pltpu.roll(high, 4, 0), low)
            near_tile, far_tile = (spread8(near >> 7), spread8(far >> 7))
            left = [
                jnp.concatenate(
                    [
                        jnp.where(near_tile == h, from_part, 0.0),
                        jnp.where(far_tile == h, to_part, 0.0),
                    ],
                    axis=1,
                )
                for h in tiles
            ]
            if first:
                level = spread8(penalty, 16)
                left.append(
                    jnp.concatenate(
                        [
                            jnp.where(spread8(near >> 7, 16) == row16, level, 0.0),
                            jnp.where(spread8(far >> 7, 16) == row16, level, 0.0),
                        ],
                        axis=1,
                    )
                )
            right = jnp.concatenate([one_hot(near, sublane), one_hot(far, sublane)], axis=1)
            out = contract(jnp.concatenate(left, axis=0), right)
            for place, h in enumerate(tiles):
                sums[h] = sums[h] + out[8 * place : 8 * place + 8]
            if first:
                weights = weights + out[8 * len(tiles) :]
        for h in range(4):
            spot = slice(p * PAIR + h * LANES, p * PAIR + (h + 1) * LANES)
            acc_ref[:, spot] = sums[h]
            if first:
                w_ref[0:1, spot] = weights[h : h + 1]


def list_picks(tables, list_ref, step, base, upper):
    count = list_ref.shape[1] // 4
    places = [
        list_ref[0:1, pl.ds(pl.multiple_of(k * count + step * LANES, LANES), LANES)] - base
        for k in range(4)
    ]
    picks = []
    for k in (0, 2):
        both = jnp.where(upper, spread8(places[k]), spread8(places[k + 1]))
        picks.append(pick(tables, both, range(len(tables))))
    return places, picks


def even_sides():
    return lax.axis_index("gx") % 2 == 0, lax.axis_index("gy") % 2 == 0


def slots(outs, step, per_list_steps):
    even_x, even_y = even_sides()
    block = step // per_list_steps
    wanted = (
        jnp.where(even_x, 1, 0),
        jnp.where(even_x, 0, 1),
        jnp.where(even_y, 3, 2),
        jnp.where(even_y, 2, 3),
    )
    return [(ref, block == want) for ref, want in zip(outs, wanted)]


def write_ghosts(outs, picks, step):
    even_x, even_y = even_sides()
    spot = pl.ds(pl.multiple_of(step * LANES, LANES), LANES)
    for out_even, out_odd, even, both in (
        (outs[0], outs[1], even_x, picks[0]),
        (outs[2], outs[3], even_y, picks[1]),
    ):
        out_even[0:4, spot] = jnp.where(even, both[:4], both[4:])
        out_odd[0:4, spot] = jnp.where(even, both[4:], both[:4])


def cross_spot(step, per_list_steps, t, width):
    start = (step % per_list_steps) * width + t * LANES
    return pl.ds(pl.multiple_of(start, LANES), LANES)


def hv_states(s_ref, hv_bus_ref, work_ref):
    lane = lax.broadcasted_iota(jnp.int32, (1, LANES), 1)

    def body(t, carry):
        bus = hv_bus_ref[t]
        start = pl.multiple_of((bus >> 7) * LANES, LANES)
        row = s_ref[2:3, pl.ds(start, LANES)]
        work_ref[pl.ds(t, 1), :] = jnp.where(lane == (bus & (LANES - 1)), row, 0.0)
        return carry

    lax.fori_loop(0, work_ref.shape[0], body, 0, unroll=8)
    return jnp.broadcast_to(jnp.sum(work_ref[...], axis=1, keepdims=True), work_ref.shape)


def hv_penalties(level_ref, work_ref):
    def body(t, carry):
        work_ref[pl.ds(t, 1), :] = jnp.full((1, LANES), level_ref[t], jnp.int32).astype(F32) * 0.25
        return carry

    lax.fori_loop(0, work_ref.shape[0], body, 0, unroll=8)
    return work_ref[...]


def as_row(values, width, offset):
    count = values.shape[0]
    wide = jnp.broadcast_to(values[:, :1], (count, width))
    lane = lax.broadcasted_iota(jnp.int32, (count, width), 1)
    own = lax.broadcasted_iota(jnp.int32, (count, width), 0)
    return jnp.sum(jnp.where(lane == own + offset, wide, 0.0), axis=0, keepdims=True)


def write_hv(out_ref, values, penalties):
    width = out_ref.shape[-1]
    row = as_row(values, width, 0) + as_row(penalties, width, values.shape[0])
    out_ref[...] = jnp.broadcast_to(row, out_ref.shape)


def start_kernel(
    bus_ref, level_ref, s_ref, list_ref, from_ref, kkt_ref, act_ref, lim_ref, lev_ref,
    xe_ref, xo_ref, ye_ref, yo_ref, z_ref, hv_ref, hv_own_ref, work_ref, turn_ref,
):
    step = pl.program_id(0)
    width = s_ref.shape[1] // pl.num_programs(0)
    outs = (xe_ref, xo_ref, ye_ref, yo_ref)
    upper = lax.broadcasted_iota(jnp.int32, (8, LANES), 0) < 4

    @pl.when(step == 0)
    def _():
        values = hv_states(s_ref, bus_ref, work_ref)
        hv_own_ref[...] = values
        penalties = hv_penalties(level_ref, work_ref)
        write_hv(hv_ref, values, penalties)

    base = step * width
    states = doubled(s_ref[:, pl.ds(pl.multiple_of(base, width), width)])
    tables = tiles_of(states)
    _, picks = list_picks(tables, list_ref, step, base, upper)
    z_ref[0:8, :] = picks[0]
    z_ref[8:16, :] = picks[1]
    write_ghosts(outs, picks, step)
    cross = from_ref.shape[1]
    per_list_steps = xe_ref.shape[1] // cross
    found = []
    for t in range(cross // LANES):
        cols = slice(t * LANES, (t + 1) * LANES)
        index = spread8(from_ref[0:1, cols] - (base + t * PAIR))
        ends = pick(tables[4 * t : 4 * t + 4], index, range(4))
        fixed = act_ref[:, cols] == 1
        part = jnp.where(fixed, lim_ref[:, cols], product(kkt_ref, cols, jnp.where(upper, ends, 0.0)))
        for i in range(8):
            turn_ref[64 * t + 8 * i : 64 * t + 8 * i + 8, :] = kkt_ref[8 * i : 8 * i + 8, cols]
        block = [
            jnp.where(fixed, 0.0, turn_ref[pl.ds(64 * t + 4 + j, 8, stride=8), :])[4:] for j in range(4)
        ]
        found.append((part[4:], block, 0.25 * lev_ref[0:1, cols].astype(F32)))
    for ref, here in slots(outs, step, per_list_steps):

        @pl.when(here)
        def _():
            for t, (part, block, penalty) in enumerate(found):
                spot = cross_spot(step, per_list_steps, t, cross)
                ref[4:8, spot] = part
                for j in range(4):
                    ref[8 + 4 * j : 12 + 4 * j, spot] = block[j]
                ref[24:25, spot] = penalty


def far_hv(first, bus_ref, partner_ref, level_ref, all_ref, own, scaled, sum_ref, weight_ref, work_ref, pen_ref):
    count = work_ref.shape[0]
    width = all_ref.shape[-1]
    lane = lax.broadcasted_iota(jnp.int32, (1, LANES), 1)
    wide = lax.broadcasted_iota(jnp.int32, (1, width), 1)

    def fetch(t, carry):
        partner = partner_ref[t]
        device, place = (partner // count, partner % count)
        row = all_ref[pl.ds(device, 1), :]
        value = jnp.sum(jnp.where(wide == place, row, 0.0), axis=1, keepdims=True)
        weight = jnp.sum(jnp.where(wide == place + count, row, 0.0), axis=1, keepdims=True)
        work_ref[pl.ds(t, 1), :] = jnp.broadcast_to(value, (1, LANES))
        pen_ref[pl.ds(t, 1), :] = jnp.broadcast_to(weight, (1, LANES))
        return carry

    lax.fori_loop(0, count, fetch, 0, unroll=8)
    far_value = work_ref[...]
    far_penalty = pen_ref[...]
    penalty = hv_penalties(level_ref, pen_ref)
    flow = (penalty * own - far_penalty * far_value) / (penalty + far_penalty)
    y = flow if first else flow + scaled
    work_ref[...] = penalty * y
    sum_ref[...] = jnp.zeros_like(sum_ref)
    if first:
        weight_ref[...] = jnp.zeros_like(weight_ref)

    def place_terms(t, carry):
        bus = bus_ref[t]
        spot = pl.ds(pl.multiple_of((bus >> 7) * LANES, LANES), LANES)
        here = lane == (bus & (LANES - 1))
        sum_ref[0:1, spot] += jnp.where(here, work_ref[pl.ds(t, 1), :], 0.0)
        if first:
            weight_ref[0:1, spot] += jnp.where(here, pen_ref[pl.ds(t, 1), :], 0.0)
        return carry

    lax.fori_loop(0, count, place_terms, 0, unroll=8)
    return penalty, y


def outer_kernel(first, *refs):
    if first:
        (
            bus_ref, partner_ref, level_ref, all_ref, own_ref, xe, xo, ye, yo, acc_ref, weight_in_ref,
            s_ref, list_ref, from_ref, kkt_ref, act_ref, lim_ref, lev_ref, z_ref, target_ref, prior_ref,
            new_ref, inv_ref, oxe, oxo, oye, oyo, yc_ref, ym_ref, zn_ref, hv_ref, hv_scaled_ref, hv_own_ref,
            sum_ref, hv_weight_ref, work_ref, pen_ref, hold_ref,
        ) = refs
        now = (xe, xo, ye, yo)
        scaled_ref = None
    else:
        (
            bus_ref, partner_ref, level_ref, all_ref, own_ref, scaled_ref, xe, xo, ye, yo, nxe, nxo, nye, nyo,
            acc_ref, inv_ref, s_ref, list_ref, from_ref, kkt_ref, act_ref, lim_ref, lev_ref, z_ref, yc_old_ref,
            ym_old_ref, target_ref, prior_ref,
            new_ref, state_ref, oxe, oxo, oye, oyo, yc_ref, hv_dual_ref,
            sum_ref, work_ref, pen_ref, hold_ref,
        ) = refs
        now = (nxe, nxo, nye, nyo)
        hv_weight_ref = None
    fixed_parts = (xe, xo, ye, yo)
    outs = (oxe, oxo, oye, oyo)
    step = pl.program_id(0)
    width = s_ref.shape[1]
    upper = lax.broadcasted_iota(jnp.int32, (8, LANES), 0) < 4
    row8 = lax.broadcasted_iota(jnp.int32, (8, LANES), 0)
    row16 = lax.broadcasted_iota(jnp.int32, (16, LANES), 0)
    power = (row8 == 2) | (row8 == 6)
    sublane = sublanes()
    even_x, even_y = even_sides()

    @pl.when(step == 0)
    def _():
        scaled = None if first else scaled_ref[...]
        _, y = far_hv(
            first, bus_ref, partner_ref, level_ref, all_ref, own_ref[...], scaled, sum_ref, hv_weight_ref,
            work_ref, pen_ref,
        )
        hold_ref[...] = y

    base = step * width
    tables = tiles_of(doubled(s_ref[...]))
    cross = from_ref.shape[1]
    per_list_steps = xe.shape[1] // cross
    block = step // per_list_steps
    places, _ = (
        [
            list_ref[0:1, pl.ds(pl.multiple_of(k * (list_ref.shape[1] // 4) + step * LANES, LANES), LANES)] - base
            for k in range(4)
        ],
        None,
    )
    sums = [None] * len(tables)
    weights = [None] * len(tables)

    use_even = jnp.where(even_x, block == 1, block == 0) | (jnp.where(even_y, block == 3, block == 2))
    along_x = block < 2
    outputs = []
    for t in range(cross // LANES):
        cols = slice(t * LANES, (t + 1) * LANES)
        spot = cross_spot(step, per_list_steps, t, cross)
        ghost = jnp.where(
            along_x,
            jnp.where(use_even, now[0][0:4, spot], now[1][0:4, spot]),
            jnp.where(use_even, now[2][0:4, spot], now[3][0:4, spot]),
        )
        near = from_ref[0:1, cols] - (base + t * PAIR)
        ends = pick(tables[4 * t : 4 * t + 4], spread8(near), range(4))
        ends = jnp.where(upper, ends, doubled(ghost))
        penalty = 0.25 * lev_ref[0:1, cols].astype(F32)
        if first:
            scaled, target = (None, ends)
        else:
            scaled = yc_old_ref[:, cols] - ends
            target = ends - scaled
        flows = product(kkt_ref, cols, target)
        flows = jnp.where(act_ref[:, cols] == 1, lim_ref[:, cols], flows)
        y = flows if first else flows + scaled
        yc_ref[:, cols] = y
        outputs.append(y)
        high, low = halves(spread8(penalty) * y)
        part = jnp.where(upper, high, pltpu.roll(low, 4, 0))
        tile = spread8(near >> 7)
        left = [jnp.where(tile == h, part, 0.0) for h in range(4)]
        if first:
            left.append(jnp.where(spread8(near >> 7, 16) == row16, spread8(penalty, 16), 0.0))
        out = contract(jnp.concatenate(left, axis=0), one_hot(near, sublane))
        for h in range(4):
            sums[4 * t + h] = out[8 * h : 8 * h + 8]
            if first:
                weights[4 * t + h] = out[32 + h : 33 + h]

    spot = pl.ds(pl.multiple_of(step * LANES, LANES), LANES)
    lefts, rights = ([], [])
    for k, (even, pair) in enumerate(((even_x, 0), (even_x, 1), (even_y, 0), (even_y, 1))):
        start = 0 if k < 2 else 2
        from_even = even if pair == 0 else jnp.logical_not(even)

        def received(parts, rows):
            return jnp.where(from_even, parts[start][rows, spot], parts[start + 1][rows, spot])

        rows = slice(4 * k, 4 * k + 4)
        held = z_ref[rows, :]
        if first:
            scaled, target = (None, held)
        else:
            scaled = ym_old_ref[rows, :] - held
            target = held - scaled
        flows = received(now, slice(4, 8))
        for j in range(4):
            flows = flows + received(fixed_parts, slice(8 + 4 * j, 12 + 4 * j)) * spread8(target[j : j + 1], 4)
        penalty = received(fixed_parts, slice(24, 25))
        y = flows if first else flows + scaled
        if first:
            ym_ref[rows, :] = y
        high, low = halves(spread8(penalty, 4) * y)
        part = jnp.concatenate([high, low], axis=0)
        tile = spread8(places[k] >> 7)
        left = [jnp.where(tile == h, part, 0.0) for h in range(len(tables))]
        if first:
            left.append(jnp.where(spread8(places[k] >> 7, 16) == row16, spread8(penalty, 16), 0.0))
        lefts.append(jnp.concatenate(left, axis=0))
        rights.append(one_hot(places[k], sublane))
    out = contract(jnp.concatenate(lefts[:2], axis=1), jnp.concatenate(rights[:2], axis=1))
    out = out + contract(jnp.concatenate(lefts[2:], axis=1), jnp.concatenate(rights[2:], axis=1))

    fresh = []
    for h in range(len(tables)):
        cols = slice(h * LANES, (h + 1) * LANES)
        whole = pl.ds(pl.multiple_of(base + h * LANES, LANES), LANES)
        total = acc_ref[:, cols] + sums[h] + out[8 * h : 8 * h + 8]
        total = total + pltpu.roll(total, 4, 0)
        total = total + jnp.where(power, spread8(sum_ref[0:1, whole]), 0.0)
        prior = doubled(prior_ref[:, cols])
        total = total + prior * doubled(target_ref[:, cols])
        if first:
            count = 8 * len(tables)
            weight = weight_in_ref[0:1, cols] + weights[h] + out[count + h : count + h + 1]
            weight = spread8(weight) + jnp.where(power, spread8(hv_weight_ref[0:1, whole]), 0.0) + prior
            inverse = 1.0 / weight
            inv_ref[:, cols] = inverse
        else:
            inverse = inv_ref[:, cols]
        state = total * inverse
        new_ref[:, whole] = state
        if not first:
            state_ref[:, cols] = state[:4]
        fresh.append(state)

    _, picks = list_picks(fresh, list_ref, step, base, upper)
    write_ghosts(outs, picks, step)
    if first:
        zn_ref[0:8, :] = picks[0]
        zn_ref[8:16, :] = picks[1]
        parts = []
        for t in range(cross // LANES):
            cols = slice(t * LANES, (t + 1) * LANES)
            near = from_ref[0:1, cols] - (base + t * PAIR)
            ends = pick(fresh[4 * t : 4 * t + 4], spread8(near), range(4))
            target = 2.0 * ends - outputs[t]
            part = product(kkt_ref, cols, jnp.where(upper, target, 0.0))
            parts.append(jnp.where(act_ref[:, cols] == 1, lim_ref[:, cols], part)[4:])
        for ref, here in slots(outs, step, per_list_steps):

            @pl.when(here)
            def _():
                for t, part in enumerate(parts):
                    ref[4:8, cross_spot(step, per_list_steps, t, cross)] = part

    @pl.when(step == pl.num_programs(0) - 1)
    def _():
        reached = hv_states(new_ref, bus_ref, work_ref)
        left_over = hold_ref[...] - reached
        penalty = hv_penalties(level_ref, pen_ref)
        if first:
            hv_scaled_ref[...] = left_over
            hv_own_ref[...] = reached - left_over
            write_hv(hv_ref, reached - left_over, penalty)
        else:
            row = as_row(penalty * left_over, LANES, 0)
            hv_dual_ref[...] = row[:, : hv_dual_ref.shape[1]]


def inner_dual_kernel(s_ref, index_ref, y_ref, lev_ref, dual_ref):
    step = pl.program_id(0)
    upper = lax.broadcasted_iota(jnp.int32, (8, LANES), 0) < 4
    width = s_ref.shape[1]
    per_pair = index_ref.shape[1] // (width // PAIR)
    for p in range(width // PAIR):
        tables = tiles_of(s_ref[:, p * PAIR : (p + 1) * PAIR])
        base = step * width + p * PAIR
        for t in range(per_pair // LANES):
            cols = slice(p * per_pair + t * LANES, p * per_pair + (t + 1) * LANES)
            ends, _, _, _ = inner_ends_of(tables, index_ref, base, cols, t, upper)
            penalty = 0.25 * lev_ref[0:1, cols].astype(F32)
            dual_ref[:, cols] = spread8(penalty) * (y_ref[:, cols] - ends)


def outer_dual_kernel(dual_in_ref, xe, xo, ye, yo, s_ref, from_ref, y_ref, lev_ref, dual_ref):
    step = pl.program_id(0)
    width = s_ref.shape[1]
    upper = lax.broadcasted_iota(jnp.int32, (8, LANES), 0) < 4
    even_x, even_y = even_sides()
    tables = tiles_of(s_ref[...])
    cross = from_ref.shape[1]
    per_list_steps = xe.shape[1] // cross
    block = step // per_list_steps
    use_even = jnp.where(even_x, block == 1, block == 0) | (jnp.where(even_y, block == 3, block == 2))
    along_x = block < 2
    for t in range(cross // LANES):
        cols = slice(t * LANES, (t + 1) * LANES)
        spot = cross_spot(step, per_list_steps, t, cross)
        ghost = jnp.where(
            along_x,
            jnp.where(use_even, xe[0:4, spot], xo[0:4, spot]),
            jnp.where(use_even, ye[0:4, spot], yo[0:4, spot]),
        )
        near = from_ref[0:1, cols] - (step * width + t * PAIR)
        ends = pick(tables[4 * t : 4 * t + 4], spread8(near), range(4))
        ends = jnp.where(upper, ends, doubled(ghost))
        penalty = 0.25 * lev_ref[0:1, cols].astype(F32)
        dual_ref[:, cols] = spread8(penalty) * (y_ref[:, cols] - ends)


def split(rows, width, first=0):
    return pl.BlockSpec((rows, width), lambda g: (0, first + g))


def whole(shape):
    return pl.BlockSpec(shape, lambda g: (0,) * len(shape))


def scalars():
    return pl.BlockSpec(memory_space=pltpu.SMEM)


def shape_of(*dims):
    return jax.ShapeDtypeStruct(dims, F32)


def params():
    return pltpu.CompilerParams(
        dimension_semantics=("arbitrary",), vmem_limit_bytes=32 * 1024 * 1024
    )


def cost(flops, moved):
    return pl.CostEstimate(flops=flops, bytes_accessed=moved, transcendentals=0)


def on_device(
    bus_start, bus_target, bus_weight, inner_ends, cross_from, boundary_lists, kkt_map, active_set, limits,
    penalty_level, hv_bus, hv_partner, hv_level,
):
    _, bus_count = bus_start.shape
    list_len = boundary_lists.shape[1] // 4
    inner_count = inner_ends.shape[1]
    cross_count = cross_from.shape[0]
    branch_count = kkt_map.shape[2]
    terms = hv_bus.shape[0]
    devices = lax.axis_size("gx") * lax.axis_size("gy")
    steps = bus_count // (GROUP * BLK)
    buses, inner, cross = (bus_count // steps, inner_count // steps, cross_count // steps)
    start = inner_count // cross
    hv_width = max(LANES, 2 * terms)
    kkt = kkt_map.reshape(64, branch_count)
    from_row = cross_from.reshape(1, cross_count)
    level_row = penalty_level.reshape(1, branch_count)
    inner_args = (inner_ends, kkt, active_set, limits, level_row)
    inner_specs = [split(2, inner), split(64, inner), split(8, inner), split(8, inner), split(1, inner)]
    cross_args = (from_row, kkt, active_set, limits, level_row)
    cross_specs = [
        split(1, cross), split(64, cross, start), split(8, cross, start), split(8, cross, start), split(1, cross, start),
    ]
    hv_block = (terms, LANES)
    common = dict(grid=(steps,), compiler_params=params())

    *sent, held, hv_rows, hv_own = pl.pallas_call(
        start_kernel,
        name="first_messages",
        in_specs=[scalars(), scalars(), whole(bus_start.shape), whole(boundary_lists.shape)] + cross_specs,
        out_shape=[shape_of(STATIC_ROWS, list_len)] * 4
        + [shape_of(16, list_len), shape_of(devices, hv_width), shape_of(*hv_block)],
        out_specs=[whole((STATIC_ROWS, list_len))] * 4
        + [split(16, LANES), whole((devices, hv_width)), whole(hv_block)],
        scratch_shapes=[pltpu.VMEM(hv_block, F32), pltpu.VMEM((64 * (cross // LANES), LANES), F32)],
        cost_estimate=cost(10**6, 4 * 10**6),
        **common,
    )(hv_bus, hv_level, bus_start, boundary_lists, *cross_args)

    def exchange(messages):
        xe, xo, ye, yo = messages
        xo = swapped(xo, "gx", 1)
        yo = swapped(yo, "gy", 1)
        xe = swapped(xe, "gx", 0)
        ye = swapped(ye, "gy", 0)
        return (xe, xo, ye, yo)

    first_got = exchange(sent)
    hv_all = to_all(hv_rows)
    y_inner, sums, weights = pl.pallas_call(
        functools.partial(inner_kernel, True),
        name="inner_first",
        in_specs=[split(4, buses)] + inner_specs,
        out_shape=[shape_of(8, inner_count), shape_of(8, bus_count), shape_of(1, bus_count)],
        out_specs=[split(8, inner), split(8, buses), split(1, buses)],
        cost_estimate=cost(10**8, 10**7),
        **common,
    )(bus_start, *inner_args)
    message_shape = (8, list_len)
    state, inverse, *rest = pl.pallas_call(
        functools.partial(outer_kernel, True),
        name="outer_first",
        in_specs=[scalars()] * 3
        + [whole((devices, hv_width)), whole(hv_block)]
        + [whole((STATIC_ROWS, list_len))] * 4
        + [split(8, buses), split(1, buses), split(4, buses), whole(boundary_lists.shape)]
        + cross_specs
        + [split(16, LANES), split(4, buses), split(4, buses)],
        out_shape=[shape_of(8, bus_count), shape_of(8, bus_count)]
        + [shape_of(*message_shape)] * 4
        + [shape_of(8, cross_count), shape_of(16, list_len), shape_of(16, list_len)]
        + [shape_of(devices, hv_width), shape_of(*hv_block), shape_of(*hv_block)],
        out_specs=[whole((8, bus_count)), split(8, buses)]
        + [whole(message_shape)] * 4
        + [split(8, cross), split(16, LANES), split(16, LANES)]
        + [whole((devices, hv_width)), whole(hv_block), whole(hv_block)],
        scratch_shapes=[pltpu.VMEM((1, bus_count), F32)] * 2 + [pltpu.VMEM(hv_block, F32)] * 3,
        cost_estimate=cost(10**7, 5 * 10**6),
        **common,
    )(
        hv_bus, hv_partner, hv_level, hv_all, hv_own, *first_got, sums, weights, bus_start, boundary_lists,
        *cross_args, held, bus_target, bus_weight,
    )
    sent, (y_cross, y_mirror, held, hv_rows, hv_scaled, hv_own) = (rest[:4], rest[4:])

    second_got = exchange(sent)
    hv_all = to_all(hv_rows)
    y_inner, sums = pl.pallas_call(
        functools.partial(inner_kernel, False),
        name="inner_second",
        in_specs=[split(8, buses)] + inner_specs + [split(8, inner)],
        out_shape=[shape_of(8, inner_count), shape_of(8, bus_count)],
        out_specs=[split(8, inner), split(8, buses)],
        cost_estimate=cost(10**8, 10**7),
        **common,
    )(state, *inner_args, y_inner)
    last_shape = (4, list_len)
    state, bus_state, *rest = pl.pallas_call(
        functools.partial(outer_kernel, False),
        name="outer_second",
        in_specs=[scalars()] * 3
        + [whole((devices, hv_width)), whole(hv_block), whole(hv_block)]
        + [whole((STATIC_ROWS, list_len))] * 4
        + [whole(message_shape)] * 4
        + [split(8, buses), split(8, buses), split(8, buses), whole(boundary_lists.shape)]
        + cross_specs
        + [split(16, LANES), split(8, cross), split(16, LANES), split(4, buses), split(4, buses)],
        out_shape=[shape_of(8, bus_count), shape_of(4, bus_count)]
        + [shape_of(*last_shape)] * 4
        + [shape_of(8, cross_count), shape_of(1, terms)],
        out_specs=[whole((8, bus_count)), split(4, buses)]
        + [whole(last_shape)] * 4
        + [split(8, cross), whole((1, terms))],
        scratch_shapes=[pltpu.VMEM((1, bus_count), F32)] + [pltpu.VMEM(hv_block, F32)] * 3,
        cost_estimate=cost(10**7, 5 * 10**6),
        **common,
    )(
        hv_bus, hv_partner, hv_level, hv_all, hv_own, hv_scaled, *first_got, *second_got, sums, inverse, state,
        boundary_lists, *cross_args, held, y_cross, y_mirror, bus_target, bus_weight,
    )
    sent, (y_cross, hv_dual) = (rest[:4], rest[4:])

    last_got = exchange(sent)
    duals = pl.pallas_call(
        inner_dual_kernel,
        name="inner_duals",
        in_specs=[split(8, buses), split(2, inner), split(8, inner), split(1, inner)],
        out_shape=shape_of(8, branch_count),
        out_specs=split(8, inner),
        cost_estimate=cost(10**7, 3 * 10**6),
        **common,
    )(state, inner_ends, y_inner, level_row)
    duals = pl.pallas_call(
        outer_dual_kernel,
        name="outer_duals",
        in_specs=[pl.BlockSpec(memory_space=pl.ANY)]
        + [whole(last_shape)] * 4
        + [split(8, buses), split(1, cross), split(8, cross), split(1, cross, start)],
        out_shape=shape_of(8, branch_count),
        out_specs=split(8, cross, start),
        input_output_aliases={0: 0},
        cost_estimate=cost(10**6, 10**6),
        **common,
    )(duals, *last_got, state, from_row, y_cross, level_row)
    return (bus_state, duals, hv_dual.reshape(terms))


def solution(mesh):
    return jax.shard_map(
        on_device,
        mesh=mesh,
        in_specs=(
            P(None, ("gx", "gy")),
            P(None, ("gx", "gy")),
            P(None, ("gx", "gy")),
            P(None, ("gx", "gy")),
            P(("gx", "gy")),
            P(("gx", "gy"), None),
            P(None, None, ("gx", "gy")),
            P(None, ("gx", "gy")),
            P(None, ("gx", "gy")),
            P(("gx", "gy")),
            P(("gx", "gy")),
            P(("gx", "gy")),
            P(("gx", "gy")),
        ),
        out_specs=(P(None, ("gx", "gy")), P(None, ("gx", "gy")), P(("gx", "gy"))),
        check_vma=False,
    )
```

```python
import functools

import jax
import jax.numpy as jnp
from jax import lax
from jax.experimental import pallas as pl
from jax.experimental.pallas import tpu as pltpu
from jax.sharding import PartitionSpec as P

F32 = jnp.float32
BF16 = jnp.bfloat16
BLK = 256
LANES = 128
GROUP = 8
PAIR = 2 * BLK
STATIC_ROWS = 25


def swapped(value, axis, first):
    count = lax.axis_size(axis)
    moves = []
    for low in range(first, count - 1, 2):
        moves += [(low, low + 1), (low + 1, low)]
    return lax.ppermute(value, axis, moves)


def to_all(rows):
    return lax.all_to_all(rows, ("gx", "gy"), split_axis=0, concat_axis=0, tiled=True)


def take_lanes(table, lane):
    return jnp.take_along_axis(table, lane, axis=1, mode="promise_in_bounds")


def pick(tables, index, tiles):
    lane, tile = (index & (LANES - 1), index >> 7)
    found = None
    for h in tiles:
        got = take_lanes(tables[h], lane)
        found = got if found is None else jnp.where(tile == h, got, found)
    return found


def spread8(row, rows=8):
    return jnp.broadcast_to(row, (rows, row.shape[-1]))


def one_hot(index, sublane):
    low = spread8(index & (LANES - 1), 16).astype(F32).astype(BF16)
    column = jnp.concatenate([low] * (LANES // 16), axis=0)
    return jnp.where(column == sublane, jnp.ones((), BF16), jnp.zeros((), BF16))


def contract(left, right):
    return lax.dot_general(
        left.astype(BF16), right, (((1,), (1,)), ((), ())), preferred_element_type=F32
    )


def halves(values):
    high = values.astype(BF16).astype(F32)
    return high, values - high


def sublanes():
    return lax.broadcasted_iota(jnp.int32, (LANES, LANES), 0).astype(F32).astype(BF16)


def folded(first, second, distance, mask):
    return jnp.where(
        mask,
        first + pltpu.roll(first, 8 - distance, 0),
        second + pltpu.roll(second, distance, 0),
    )


def product(kkt_ref, cols, target):
    row = lax.broadcasted_iota(jnp.int32, (8, LANES), 0)
    terms = [kkt_ref[8 * i : 8 * i + 8, cols] * target for i in range(8)]
    upper = row < 4
    quads = [
        jnp.where(upper, terms[i], terms[i + 4]) + pltpu.roll(jnp.where(upper, terms[i + 4], terms[i]), 4, 0)
        for i in range(4)
    ]
    even_two = (row & 2) == 0
    twos = [folded(quads[i], quads[i + 2], 2, even_two) for i in range(2)]
    return folded(twos[0], twos[1], 1, (row & 1) == 0)


def doubled(block):
    return block if block.shape[0] == 8 else jnp.concatenate([block, block], axis=0)


def tiles_of(states):
    return [states[:, h * LANES : (h + 1) * LANES] for h in range(states.shape[1] // LANES)]


def inner_ends_of(tables, index_ref, base, cols, t, upper):
    near = index_ref[0:1, cols] - base
    far = index_ref[1:2, cols] - base
    tiles = (0, 1) if t < 2 else (2, 3) if t > 2 else (0, 1, 2, 3)
    both = jnp.where(upper, spread8(near), spread8(far))
    return pick(tables, both, tiles), near, far, tiles


def inner_kernel(first, *refs):
    if first:
        s_ref, index_ref, kkt_ref, act_ref, lim_ref, lev_ref, y_ref, acc_ref, w_ref = refs
    else:
        s_ref, index_ref, kkt_ref, act_ref, lim_ref, lev_ref, old_ref, y_ref, acc_ref = refs
    step = pl.program_id(0)
    states = doubled(s_ref[...])
    upper = lax.broadcasted_iota(jnp.int32, (8, LANES), 0) < 4
    row16 = lax.broadcasted_iota(jnp.int32, (16, LANES), 0)
    sublane = sublanes()
    width = states.shape[1]
    per_pair = kkt_ref.shape[1] // (width // PAIR)
    for p in range(width // PAIR):
        tables = tiles_of(states[:, p * PAIR : (p + 1) * PAIR])
        base = step * width + p * PAIR
        sums = [jnp.zeros((8, LANES), F32)] * 4
        weights = jnp.zeros((16, LANES), F32)
        for t in range(per_pair // LANES):
            cols = slice(p * per_pair + t * LANES, p * per_pair + (t + 1) * LANES)
            ends, near, far, tiles = inner_ends_of(tables, index_ref, base, cols, t, upper)
            penalty = 0.25 * lev_ref[0:1, cols].astype(F32)
            if first:
                scaled, target = (None, ends)
            else:
                scaled = old_ref[:, cols] - ends
                target = ends - scaled
            flows = product(kkt_ref, cols, target)
            flows = jnp.where(act_ref[:, cols] == 1, lim_ref[:, cols], flows)
            y = flows if first else flows + scaled
            y_ref[:, cols] = y
            high, low = halves(spread8(penalty) * y)
            from_part = jnp.where(upper, high, pltpu.roll(low, 4, 0))
            to_part = jnp.where(upper, pltpu.roll(high, 4, 0), low)
            near_tile, far_tile = (spread8(near >> 7), spread8(far >> 7))
            left = [
                jnp.concatenate(
                    [
                        jnp.where(near_tile == h, from_part, 0.0),
                        jnp.where(far_tile == h, to_part, 0.0),
                    ],
                    axis=1,
                )
                for h in tiles
            ]
            if first:
                level = spread8(penalty, 16)
                left.append(
                    jnp.concatenate(
                        [
                            jnp.where(spread8(near >> 7, 16) == row16, level, 0.0),
                            jnp.where(spread8(far >> 7, 16) == row16, level, 0.0),
                        ],
                        axis=1,
                    )
                )
            right = jnp.concatenate([one_hot(near, sublane), one_hot(far, sublane)], axis=1)
            out = contract(jnp.concatenate(left, axis=0), right)
            for place, h in enumerate(tiles):
                sums[h] = sums[h] + out[8 * place : 8 * place + 8]
            if first:
                weights = weights + out[8 * len(tiles) :]
        for h in range(4):
            spot = slice(p * PAIR + h * LANES, p * PAIR + (h + 1) * LANES)
            acc_ref[:, spot] = sums[h]
            if first:
                w_ref[0:1, spot] = weights[h : h + 1]


def list_picks(tables, list_ref, step, base, upper):
    count = list_ref.shape[1] // 4
    places = [
        list_ref[0:1, pl.ds(pl.multiple_of(k * count + step * LANES, LANES), LANES)] - base
        for k in range(4)
    ]
    picks = []
    for k in (0, 2):
        both = jnp.where(upper, spread8(places[k]), spread8(places[k + 1]))
        picks.append(pick(tables, both, range(len(tables))))
    return places, picks


def even_sides():
    return lax.axis_index("gx") % 2 == 0, lax.axis_index("gy") % 2 == 0


def slots(outs, step, per_list_steps):
    even_x, even_y = even_sides()
    block = step // per_list_steps
    wanted = (
        jnp.where(even_x, 1, 0),
        jnp.where(even_x, 0, 1),
        jnp.where(even_y, 3, 2),
        jnp.where(even_y, 2, 3),
    )
    return [(ref, block == want) for ref, want in zip(outs, wanted)]


def write_ghosts(outs, picks, step):
    even_x, even_y = even_sides()
    spot = pl.ds(pl.multiple_of(step * LANES, LANES), LANES)
    for out_even, out_odd, even, both in (
        (outs[0], outs[1], even_x, picks[0]),
        (outs[2], outs[3], even_y, picks[1]),
    ):
        out_even[0:4, spot] = jnp.where(even, both[:4], both[4:])
        out_odd[0:4, spot] = jnp.where(even, both[4:], both[:4])


def cross_spot(step, per_list_steps, t, width):
    start = (step % per_list_steps) * width + t * LANES
    return pl.ds(pl.multiple_of(start, LANES), LANES)


def hv_states(s_ref, hv_bus_ref, work_ref):
    lane = lax.broadcasted_iota(jnp.int32, (1, LANES), 1)

    def body(t, carry):
        bus = hv_bus_ref[t]
        start = pl.multiple_of((bus >> 7) * LANES, LANES)
        row = s_ref[2:3, pl.ds(start, LANES)]
        work_ref[pl.ds(t, 1), :] = jnp.where(lane == (bus & (LANES - 1)), row, 0.0)
        return carry

    lax.fori_loop(0, work_ref.shape[0], body, 0, unroll=8)
    return jnp.broadcast_to(jnp.sum(work_ref[...], axis=1, keepdims=True), work_ref.shape)


def hv_penalties(level_ref, work_ref):
    def body(t, carry):
        work_ref[pl.ds(t, 1), :] = jnp.full((1, LANES), level_ref[t], jnp.int32).astype(F32) * 0.25
        return carry

    lax.fori_loop(0, work_ref.shape[0], body, 0, unroll=8)
    return work_ref[...]


def as_row(values, width, offset):
    count = values.shape[0]
    wide = jnp.broadcast_to(values[:, :1], (count, width))
    lane = lax.broadcasted_iota(jnp.int32, (count, width), 1)
    own = lax.broadcasted_iota(jnp.int32, (count, width), 0)
    return jnp.sum(jnp.where(lane == own + offset, wide, 0.0), axis=0, keepdims=True)


def write_hv(out_ref, values, penalties):
    width = out_ref.shape[-1]
    row = as_row(values, width, 0) + as_row(penalties, width, values.shape[0])
    out_ref[...] = jnp.broadcast_to(row, out_ref.shape)


def start_kernel(
    bus_ref, level_ref, s_ref, list_ref, from_ref, kkt_ref, act_ref, lim_ref, lev_ref,
    xe_ref, xo_ref, ye_ref, yo_ref, z_ref, hv_ref, hv_own_ref, work_ref, turn_ref,
):
    step = pl.program_id(0)
    width = s_ref.shape[1] // pl.num_programs(0)
    outs = (xe_ref, xo_ref, ye_ref, yo_ref)
    upper = lax.broadcasted_iota(jnp.int32, (8, LANES), 0) < 4

    @pl.when(step == 0)
    def _():
        values = hv_states(s_ref, bus_ref, work_ref)
        hv_own_ref[...] = values
        penalties = hv_penalties(level_ref, work_ref)
        write_hv(hv_ref, values, penalties)

    base = step * width
    states = doubled(s_ref[:, pl.ds(pl.multiple_of(base, width), width)])
    tables = tiles_of(states)
    _, picks = list_picks(tables, list_ref, step, base, upper)
    z_ref[0:8, :] = picks[0]
    z_ref[8:16, :] = picks[1]
    write_ghosts(outs, picks, step)
    cross = from_ref.shape[1]
    per_list_steps = xe_ref.shape[1] // cross
    found = []
    for t in range(cross // LANES):
        cols = slice(t * LANES, (t + 1) * LANES)
        index = spread8(from_ref[0:1, cols] - (base + t * PAIR))
        ends = pick(tables[4 * t : 4 * t + 4], index, range(4))
        fixed = act_ref[:, cols] == 1
        part = jnp.where(fixed, lim_ref[:, cols], product(kkt_ref, cols, jnp.where(upper, ends, 0.0)))
        for i in range(8):
            turn_ref[64 * t + 8 * i : 64 * t + 8 * i + 8, :] = kkt_ref[8 * i : 8 * i + 8, cols]
        block = [
            jnp.where(fixed, 0.0, turn_ref[pl.ds(64 * t + 4 + j, 8, stride=8), :])[4:] for j in range(4)
        ]
        found.append((part[4:], block, 0.25 * lev_ref[0:1, cols].astype(F32)))
    for ref, here in slots(outs, step, per_list_steps):

        @pl.when(here)
        def _():
            for t, (part, block, penalty) in enumerate(found):
                spot = cross_spot(step, per_list_steps, t, cross)
                ref[4:8, spot] = part
                for j in range(4):
                    ref[8 + 4 * j : 12 + 4 * j, spot] = block[j]
                ref[24:25, spot] = penalty


def far_hv(first, bus_ref, partner_ref, level_ref, all_ref, own, scaled, sum_ref, weight_ref, work_ref, pen_ref):
    count = work_ref.shape[0]
    width = all_ref.shape[-1]
    lane = lax.broadcasted_iota(jnp.int32, (1, LANES), 1)
    wide = lax.broadcasted_iota(jnp.int32, (1, width), 1)

    def fetch(t, carry):
        partner = partner_ref[t]
        device, place = (partner // count, partner % count)
        row = all_ref[pl.ds(device, 1), :]
        value = jnp.sum(jnp.where(wide == place, row, 0.0), axis=1, keepdims=True)
        weight = jnp.sum(jnp.where(wide == place + count, row, 0.0), axis=1, keepdims=True)
        work_ref[pl.ds(t, 1), :] = jnp.broadcast_to(value, (1, LANES))
        pen_ref[pl.ds(t, 1), :] = jnp.broadcast_to(weight, (1, LANES))
        return carry

    lax.fori_loop(0, count, fetch, 0, unroll=8)
    far_value = work_ref[...]
    far_penalty = pen_ref[...]
    penalty = hv_penalties(level_ref, pen_ref)
    flow = (penalty * own - far_penalty * far_value) / (penalty + far_penalty)
    y = flow if first else flow + scaled
    work_ref[...] = penalty * y
    sum_ref[...] = jnp.zeros_like(sum_ref)
    if first:
        weight_ref[...] = jnp.zeros_like(weight_ref)

    def place_terms(t, carry):
        bus = bus_ref[t]
        spot = pl.ds(pl.multiple_of((bus >> 7) * LANES, LANES), LANES)
        here = lane == (bus & (LANES - 1))
        sum_ref[0:1, spot] += jnp.where(here, work_ref[pl.ds(t, 1), :], 0.0)
        if first:
            weight_ref[0:1, spot] += jnp.where(here, pen_ref[pl.ds(t, 1), :], 0.0)
        return carry

    lax.fori_loop(0, count, place_terms, 0, unroll=8)
    return penalty, y


def outer_kernel(first, *refs):
    if first:
        (
            bus_ref, partner_ref, level_ref, all_ref, own_ref, xe, xo, ye, yo, acc_ref, weight_in_ref,
            s_ref, list_ref, from_ref, kkt_ref, act_ref, lim_ref, lev_ref, z_ref, target_ref, prior_ref,
            new_ref, inv_ref, oxe, oxo, oye, oyo, yc_ref, ym_ref, zn_ref, hv_ref, hv_scaled_ref, hv_own_ref,
            sum_ref, hv_weight_ref, work_ref, pen_ref, hold_ref,
        ) = refs
        now = (xe, xo, ye, yo)
        scaled_ref = None
    else:
        (
            bus_ref, partner_ref, level_ref, all_ref, own_ref, scaled_ref, xe, xo, ye, yo, nxe, nxo, nye, nyo,
            acc_ref, inv_ref, s_ref, list_ref, from_ref, kkt_ref, act_ref, lim_ref, lev_ref, z_ref, yc_old_ref,
            ym_old_ref, target_ref, prior_ref,
            new_ref, state_ref, oxe, oxo, oye, oyo, yc_ref, hv_dual_ref,
            sum_ref, work_ref, pen_ref, hold_ref,
        ) = refs
        now = (nxe, nxo, nye, nyo)
        hv_weight_ref = None
    fixed_parts = (xe, xo, ye, yo)
    outs = (oxe, oxo, oye, oyo)
    step = pl.program_id(0)
    width = s_ref.shape[1]
    upper = lax.broadcasted_iota(jnp.int32, (8, LANES), 0) < 4
    row8 = lax.broadcasted_iota(jnp.int32, (8, LANES), 0)
    row16 = lax.broadcasted_iota(jnp.int32, (16, LANES), 0)
    power = (row8 == 2) | (row8 == 6)
    sublane = sublanes()
    even_x, even_y = even_sides()

    @pl.when(step == 0)
    def _():
        scaled = None if first else scaled_ref[...]
        _, y = far_hv(
            first, bus_ref, partner_ref, level_ref, all_ref, own_ref[...], scaled, sum_ref, hv_weight_ref,
            work_ref, pen_ref,
        )
        hold_ref[...] = y

    base = step * width
    tables = tiles_of(doubled(s_ref[...]))
    cross = from_ref.shape[1]
    per_list_steps = xe.shape[1] // cross
    block = step // per_list_steps
    places, _ = (
        [
            list_ref[0:1, pl.ds(pl.multiple_of(k * (list_ref.shape[1] // 4) + step * LANES, LANES), LANES)] - base
            for k in range(4)
        ],
        None,
    )
    sums = [None] * len(tables)
    weights = [None] * len(tables)

    use_even = jnp.where(even_x, block == 1, block == 0) | (jnp.where(even_y, block == 3, block == 2))
    along_x = block < 2
    outputs = []
    for t in range(cross // LANES):
        cols = slice(t * LANES, (t + 1) * LANES)
        spot = cross_spot(step, per_list_steps, t, cross)
        ghost = jnp.where(
            along_x,
            jnp.where(use_even, now[0][0:4, spot], now[1][0:4, spot]),
            jnp.where(use_even, now[2][0:4, spot], now[3][0:4, spot]),
        )
        near = from_ref[0:1, cols] - (base + t * PAIR)
        ends = pick(tables[4 * t : 4 * t + 4], spread8(near), range(4))
        ends = jnp.where(upper, ends, doubled(ghost))
        penalty = 0.25 * lev_ref[0:1, cols].astype(F32)
        if first:
            scaled, target = (None, ends)
        else:
            scaled = yc_old_ref[:, cols] - ends
            target = ends - scaled
        flows = product(kkt_ref, cols, target)
        flows = jnp.where(act_ref[:, cols] == 1, lim_ref[:, cols], flows)
        y = flows if first else flows + scaled
        yc_ref[:, cols] = y
        outputs.append(y)
        high, low = halves(spread8(penalty) * y)
        part = jnp.where(upper, high, pltpu.roll(low, 4, 0))
        tile = spread8(near >> 7)
        left = [jnp.where(tile == h, part, 0.0) for h in range(4)]
        if first:
            left.append(jnp.where(spread8(near >> 7, 16) == row16, spread8(penalty, 16), 0.0))
        out = contract(jnp.concatenate(left, axis=0), one_hot(near, sublane))
        for h in range(4):
            sums[4 * t + h] = out[8 * h : 8 * h + 8]
            if first:
                weights[4 * t + h] = out[32 + h : 33 + h]

    spot = pl.ds(pl.multiple_of(step * LANES, LANES), LANES)
    lefts, rights = ([], [])
    for k, (even, pair) in enumerate(((even_x, 0), (even_x, 1), (even_y, 0), (even_y, 1))):
        start = 0 if k < 2 else 2
        from_even = even if pair == 0 else jnp.logical_not(even)

        def received(parts, rows):
            return jnp.where(from_even, parts[start][rows, spot], parts[start + 1][rows, spot])

        rows = slice(4 * k, 4 * k + 4)
        held = z_ref[rows, :]
        if first:
            scaled, target = (None, held)
        else:
            scaled = ym_old_ref[rows, :] - held
            target = held - scaled
        flows = received(now, slice(4, 8))
        for j in range(4):
            flows = flows + received(fixed_parts, slice(8 + 4 * j, 12 + 4 * j)) * spread8(target[j : j + 1], 4)
        penalty = received(fixed_parts, slice(24, 25))
        y = flows if first else flows + scaled
        if first:
            ym_ref[rows, :] = y
        high, low = halves(spread8(penalty, 4) * y)
        part = jnp.concatenate([high, low], axis=0)
        tile = spread8(places[k] >> 7)
        left = [jnp.where(tile == h, part, 0.0) for h in range(len(tables))]
        if first:
            left.append(jnp.where(spread8(places[k] >> 7, 16) == row16, spread8(penalty, 16), 0.0))
        lefts.append(jnp.concatenate(left, axis=0))
        rights.append(one_hot(places[k], sublane))
    out = contract(jnp.concatenate(lefts[:2], axis=1), jnp.concatenate(rights[:2], axis=1))
    out = out + contract(jnp.concatenate(lefts[2:], axis=1), jnp.concatenate(rights[2:], axis=1))

    fresh = []
    for h in range(len(tables)):
        cols = slice(h * LANES, (h + 1) * LANES)
        whole = pl.ds(pl.multiple_of(base + h * LANES, LANES), LANES)
        total = acc_ref[:, cols] + sums[h] + out[8 * h : 8 * h + 8]
        total = total + pltpu.roll(total, 4, 0)
        total = total + jnp.where(power, spread8(sum_ref[0:1, whole]), 0.0)
        prior = doubled(prior_ref[:, cols])
        total = total + prior * doubled(target_ref[:, cols])
        if first:
            count = 8 * len(tables)
            weight = weight_in_ref[0:1, cols] + weights[h] + out[count + h : count + h + 1]
            weight = spread8(weight) + jnp.where(power, spread8(hv_weight_ref[0:1, whole]), 0.0) + prior
            inverse = 1.0 / weight
            inv_ref[:, cols] = inverse
        else:
            inverse = inv_ref[:, cols]
        state = total * inverse
        new_ref[:, whole] = state
        if not first:
            state_ref[:, cols] = state[:4]
        fresh.append(state)

    _, picks = list_picks(fresh, list_ref, step, base, upper)
    write_ghosts(outs, picks, step)
    if first:
        zn_ref[0:8, :] = picks[0]
        zn_ref[8:16, :] = picks[1]
        parts = []
        for t in range(cross // LANES):
            cols = slice(t * LANES, (t + 1) * LANES)
            near = from_ref[0:1, cols] - (base + t * PAIR)
            ends = pick(fresh[4 * t : 4 * t + 4], spread8(near), range(4))
            target = 2.0 * ends - outputs[t]
            part = product(kkt_ref, cols, jnp.where(upper, target, 0.0))
            parts.append(jnp.where(act_ref[:, cols] == 1, lim_ref[:, cols], part)[4:])
        for ref, here in slots(outs, step, per_list_steps):

            @pl.when(here)
            def _():
                for t, part in enumerate(parts):
                    ref[4:8, cross_spot(step, per_list_steps, t, cross)] = part

    @pl.when(step == pl.num_programs(0) - 1)
    def _():
        reached = hv_states(new_ref, bus_ref, work_ref)
        left_over = hold_ref[...] - reached
        penalty = hv_penalties(level_ref, pen_ref)
        if first:
            hv_scaled_ref[...] = left_over
            hv_own_ref[...] = reached - left_over
            write_hv(hv_ref, reached - left_over, penalty)
        else:
            row = as_row(penalty * left_over, LANES, 0)
            hv_dual_ref[...] = row[:, : hv_dual_ref.shape[1]]


def inner_dual_kernel(s_ref, index_ref, y_ref, lev_ref, dual_ref):
    step = pl.program_id(0)
    upper = lax.broadcasted_iota(jnp.int32, (8, LANES), 0) < 4
    width = s_ref.shape[1]
    per_pair = index_ref.shape[1] // (width // PAIR)
    for p in range(width // PAIR):
        tables = tiles_of(s_ref[:, p * PAIR : (p + 1) * PAIR])
        base = step * width + p * PAIR
        for t in range(per_pair // LANES):
            cols = slice(p * per_pair + t * LANES, p * per_pair + (t + 1) * LANES)
            ends, _, _, _ = inner_ends_of(tables, index_ref, base, cols, t, upper)
            penalty = 0.25 * lev_ref[0:1, cols].astype(F32)
            dual_ref[:, cols] = spread8(penalty) * (y_ref[:, cols] - ends)


def outer_dual_kernel(dual_in_ref, xe, xo, ye, yo, s_ref, from_ref, y_ref, lev_ref, dual_ref):
    step = pl.program_id(0)
    width = s_ref.shape[1]
    upper = lax.broadcasted_iota(jnp.int32, (8, LANES), 0) < 4
    even_x, even_y = even_sides()
    tables = tiles_of(s_ref[...])
    cross = from_ref.shape[1]
    per_list_steps = xe.shape[1] // cross
    block = step // per_list_steps
    use_even = jnp.where(even_x, block == 1, block == 0) | (jnp.where(even_y, block == 3, block == 2))
    along_x = block < 2
    for t in range(cross // LANES):
        cols = slice(t * LANES, (t + 1) * LANES)
        spot = cross_spot(step, per_list_steps, t, cross)
        ghost = jnp.where(
            along_x,
            jnp.where(use_even, xe[0:4, spot], xo[0:4, spot]),
            jnp.where(use_even, ye[0:4, spot], yo[0:4, spot]),
        )
        near = from_ref[0:1, cols] - (step * width + t * PAIR)
        ends = pick(tables[4 * t : 4 * t + 4], spread8(near), range(4))
        ends = jnp.where(upper, ends, doubled(ghost))
        penalty = 0.25 * lev_ref[0:1, cols].astype(F32)
        dual_ref[:, cols] = spread8(penalty) * (y_ref[:, cols] - ends)


def split(rows, width, first=0):
    return pl.BlockSpec((rows, width), lambda g: (0, first + g))


def whole(shape):
    return pl.BlockSpec(shape, lambda g: (0,) * len(shape))


def scalars():
    return pl.BlockSpec(memory_space=pltpu.SMEM)


def shape_of(*dims):
    return jax.ShapeDtypeStruct(dims, F32)


def params():
    return pltpu.CompilerParams(
        dimension_semantics=("arbitrary",), vmem_limit_bytes=64 * 1024 * 1024
    )


def cost(flops, moved):
    return pl.CostEstimate(flops=flops, bytes_accessed=moved, transcendentals=0)


def on_device(
    bus_start, bus_target, bus_weight, inner_ends, cross_from, boundary_lists, kkt_map, active_set, limits,
    penalty_level, hv_bus, hv_partner, hv_level,
):
    _, bus_count = bus_start.shape
    list_len = boundary_lists.shape[1] // 4
    inner_count = inner_ends.shape[1]
    cross_count = cross_from.shape[0]
    branch_count = kkt_map.shape[2]
    terms = hv_bus.shape[0]
    devices = lax.axis_size("gx") * lax.axis_size("gy")
    steps = bus_count // (GROUP * BLK)
    buses, inner, cross = (bus_count // steps, inner_count // steps, cross_count // steps)
    start = inner_count // cross
    hv_width = max(LANES, 2 * terms)
    kkt = kkt_map.reshape(64, branch_count)
    from_row = cross_from.reshape(1, cross_count)
    level_row = penalty_level.reshape(1, branch_count)
    inner_args = (inner_ends, kkt, active_set, limits, level_row)
    inner_specs = [split(2, inner), split(64, inner), split(8, inner), split(8, inner), split(1, inner)]
    cross_args = (from_row, kkt, active_set, limits, level_row)
    cross_specs = [
        split(1, cross), split(64, cross, start), split(8, cross, start), split(8, cross, start), split(1, cross, start),
    ]
    hv_block = (terms, LANES)
    common = dict(grid=(steps,), compiler_params=params())

    *sent, held, hv_rows, hv_own = pl.pallas_call(
        start_kernel,
        name="first_messages",
        in_specs=[scalars(), scalars(), whole(bus_start.shape), whole(boundary_lists.shape)] + cross_specs,
        out_shape=[shape_of(STATIC_ROWS, list_len)] * 4
        + [shape_of(16, list_len), shape_of(devices, hv_width), shape_of(*hv_block)],
        out_specs=[whole((STATIC_ROWS, list_len))] * 4
        + [split(16, LANES), whole((devices, hv_width)), whole(hv_block)],
        scratch_shapes=[pltpu.VMEM(hv_block, F32), pltpu.VMEM((64 * (cross // LANES), LANES), F32)],
        cost_estimate=cost(10**6, 4 * 10**6),
        **common,
    )(hv_bus, hv_level, bus_start, boundary_lists, *cross_args)

    def exchange(messages):
        xe, xo, ye, yo = messages
        xo = swapped(xo, "gx", 1)
        yo = swapped(yo, "gy", 1)
        xe = swapped(xe, "gx", 0)
        ye = swapped(ye, "gy", 0)
        return (xe, xo, ye, yo)

    first_got = exchange(sent)
    hv_all = to_all(hv_rows)
    y_inner, sums, weights = pl.pallas_call(
        functools.partial(inner_kernel, True),
        name="inner_first",
        in_specs=[split(4, buses)] + inner_specs,
        out_shape=[shape_of(8, inner_count), shape_of(8, bus_count), shape_of(1, bus_count)],
        out_specs=[split(8, inner), split(8, buses), split(1, buses)],
        cost_estimate=cost(10**8, 10**7),
        **common,
    )(bus_start, *inner_args)
    message_shape = (8, list_len)
    state, inverse, *rest = pl.pallas_call(
        functools.partial(outer_kernel, True),
        name="outer_first",
        in_specs=[scalars()] * 3
        + [whole((devices, hv_width)), whole(hv_block)]
        + [whole((STATIC_ROWS, list_len))] * 4
        + [split(8, buses), split(1, buses), split(4, buses), whole(boundary_lists.shape)]
        + cross_specs
        + [split(16, LANES), split(4, buses), split(4, buses)],
        out_shape=[shape_of(8, bus_count), shape_of(8, bus_count)]
        + [shape_of(*message_shape)] * 4
        + [shape_of(8, cross_count), shape_of(16, list_len), shape_of(16, list_len)]
        + [shape_of(devices, hv_width), shape_of(*hv_block), shape_of(*hv_block)],
        out_specs=[whole((8, bus_count)), split(8, buses)]
        + [whole(message_shape)] * 4
        + [split(8, cross), split(16, LANES), split(16, LANES)]
        + [whole((devices, hv_width)), whole(hv_block), whole(hv_block)],
        scratch_shapes=[pltpu.VMEM((1, bus_count), F32)] * 2 + [pltpu.VMEM(hv_block, F32)] * 3,
        cost_estimate=cost(10**7, 5 * 10**6),
        **common,
    )(
        hv_bus, hv_partner, hv_level, hv_all, hv_own, *first_got, sums, weights, bus_start, boundary_lists,
        *cross_args, held, bus_target, bus_weight,
    )
    sent, (y_cross, y_mirror, held, hv_rows, hv_scaled, hv_own) = (rest[:4], rest[4:])

    second_got = exchange(sent)
    hv_all = to_all(hv_rows)
    y_inner, sums = pl.pallas_call(
        functools.partial(inner_kernel, False),
        name="inner_second",
        in_specs=[split(8, buses)] + inner_specs + [split(8, inner)],
        out_shape=[shape_of(8, inner_count), shape_of(8, bus_count)],
        out_specs=[split(8, inner), split(8, buses)],
        cost_estimate=cost(10**8, 10**7),
        **common,
    )(state, *inner_args, y_inner)
    last_shape = (4, list_len)
    state, bus_state, *rest = pl.pallas_call(
        functools.partial(outer_kernel, False),
        name="outer_second",
        in_specs=[scalars()] * 3
        + [whole((devices, hv_width)), whole(hv_block), whole(hv_block)]
        + [whole((STATIC_ROWS, list_len))] * 4
        + [whole(message_shape)] * 4
        + [split(8, buses), split(8, buses), split(8, buses), whole(boundary_lists.shape)]
        + cross_specs
        + [split(16, LANES), split(8, cross), split(16, LANES), split(4, buses), split(4, buses)],
        out_shape=[shape_of(8, bus_count), shape_of(4, bus_count)]
        + [shape_of(*last_shape)] * 4
        + [shape_of(8, cross_count), shape_of(1, terms)],
        out_specs=[whole((8, bus_count)), split(4, buses)]
        + [whole(last_shape)] * 4
        + [split(8, cross), whole((1, terms))],
        scratch_shapes=[pltpu.VMEM((1, bus_count), F32)] + [pltpu.VMEM(hv_block, F32)] * 3,
        cost_estimate=cost(10**7, 5 * 10**6),
        **common,
    )(
        hv_bus, hv_partner, hv_level, hv_all, hv_own, hv_scaled, *first_got, *second_got, sums, inverse, state,
        boundary_lists, *cross_args, held, y_cross, y_mirror, bus_target, bus_weight,
    )
    sent, (y_cross, hv_dual) = (rest[:4], rest[4:])

    last_got = exchange(sent)
    duals = pl.pallas_call(
        inner_dual_kernel,
        name="inner_duals",
        in_specs=[split(8, buses), split(2, inner), split(8, inner), split(1, inner)],
        out_shape=shape_of(8, branch_count),
        out_specs=split(8, inner),
        cost_estimate=cost(10**7, 3 * 10**6),
        **common,
    )(state, inner_ends, y_inner, level_row)
    duals = pl.pallas_call(
        outer_dual_kernel,
        name="outer_duals",
        in_specs=[pl.BlockSpec(memory_space=pl.ANY)]
        + [whole(last_shape)] * 4
        + [split(8, buses), split(1, cross), split(8, cross), split(1, cross, start)],
        out_shape=shape_of(8, branch_count),
        out_specs=split(8, cross, start),
        input_output_aliases={0: 0},
        cost_estimate=cost(10**6, 10**6),
        **common,
    )(duals, *last_got, state, from_row, y_cross, level_row)
    return (bus_state, duals, hv_dual.reshape(terms))


def solution(mesh):
    return jax.shard_map(
        on_device,
        mesh=mesh,
        in_specs=(
            P(None, ("gx", "gy")),
            P(None, ("gx", "gy")),
            P(None, ("gx", "gy")),
            P(None, ("gx", "gy")),
            P(("gx", "gy")),
            P(("gx", "gy"), None),
            P(None, None, ("gx", "gy")),
            P(None, ("gx", "gy")),
            P(None, ("gx", "gy")),
            P(("gx", "gy")),
            P(("gx", "gy")),
            P(("gx", "gy")),
            P(("gx", "gy")),
        ),
        out_specs=(P(None, ("gx", "gy")), P(None, ("gx", "gy")), P(("gx", "gy"))),
        check_vma=False,
    )
```

```python
import functools

import jax
import jax.numpy as jnp
from jax import lax
from jax.experimental import pallas as pl
from jax.experimental.pallas import tpu as pltpu
from jax.sharding import PartitionSpec as P

F32 = jnp.float32
BF16 = jnp.bfloat16
BLK = 256
LANES = 128
GROUP = 8
PAIR = 2 * BLK
STATIC_ROWS = 25
CHUNKS = 4


def swapped(value, axis, first):
    count = lax.axis_size(axis)
    moves = []
    for low in range(first, count - 1, 2):
        moves += [(low, low + 1), (low + 1, low)]
    return lax.ppermute(value, axis, moves)


def to_all(rows):
    return lax.all_to_all(rows, ("gx", "gy"), split_axis=0, concat_axis=0, tiled=True)


def take_lanes(table, lane):
    return jnp.take_along_axis(table, lane, axis=1, mode="promise_in_bounds")


def pick(tables, index, tiles):
    lane, tile = (index & (LANES - 1), index >> 7)
    found = None
    for h in tiles:
        got = take_lanes(tables[h], lane)
        found = got if found is None else jnp.where(tile == h, got, found)
    return found


def spread8(row, rows=8):
    return jnp.broadcast_to(row, (rows, row.shape[-1]))


def one_hot(index, sublane):
    low = spread8(index & (LANES - 1), 16).astype(F32).astype(BF16)
    column = jnp.concatenate([low] * (LANES // 16), axis=0)
    return jnp.where(column == sublane, jnp.ones((), BF16), jnp.zeros((), BF16))


def contract(left, right):
    return lax.dot_general(
        left.astype(BF16), right, (((1,), (1,)), ((), ())), preferred_element_type=F32
    )


def halves(values):
    high = values.astype(BF16).astype(F32)
    return high, values - high


def sublanes():
    return lax.broadcasted_iota(jnp.int32, (LANES, LANES), 0).astype(F32).astype(BF16)


def folded(first, second, distance, mask):
    return jnp.where(
        mask,
        first + pltpu.roll(first, 8 - distance, 0),
        second + pltpu.roll(second, distance, 0),
    )


def product(kkt_ref, cols, target):
    row = lax.broadcasted_iota(jnp.int32, (8, LANES), 0)
    terms = [kkt_ref[8 * i : 8 * i + 8, cols] * target for i in range(8)]
    upper = row < 4
    quads = [
        jnp.where(upper, terms[i], terms[i + 4]) + pltpu.roll(jnp.where(upper, terms[i + 4], terms[i]), 4, 0)
        for i in range(4)
    ]
    even_two = (row & 2) == 0
    twos = [folded(quads[i], quads[i + 2], 2, even_two) for i in range(2)]
    return folded(twos[0], twos[1], 1, (row & 1) == 0)


def doubled(block):
    return block if block.shape[0] == 8 else jnp.concatenate([block, block], axis=0)


def tiles_of(states):
    return [states[:, h * LANES : (h + 1) * LANES] for h in range(states.shape[1] // LANES)]


def lanes(start):
    return pl.ds(pl.multiple_of(start, LANES), LANES)


def upper_half():
    return lax.broadcasted_iota(jnp.int32, (8, LANES), 0) < 4


def inner_ends_of(tables, index_ref, base, cols, t, upper):
    near = index_ref[0:1, cols] - base
    far = index_ref[1:2, cols] - base
    tiles = (0, 1) if t < 2 else (2, 3) if t > 2 else (0, 1, 2, 3)
    both = jnp.where(upper, spread8(near), spread8(far))
    return pick(tables, both, tiles), near, far, tiles


def chunk_copies(sources, buffers, sems, chunk, width):
    spot = pl.ds(chunk * width, width)
    return [
        pltpu.make_async_copy(source.at[:, spot], buffer.at[:, spot], sems.at[k, chunk])
        for k, (source, buffer) in enumerate(zip(sources, buffers))
    ]


def inner_kernel(first, *refs):
    if first:
        s_ref, index_ref, lev_ref, kkt_hbm, act_hbm, lim_hbm, y_hbm, acc_ref, w_ref, *rest = refs
        kkt_ref, act_ref, lim_ref, y_ref, sems, out_sems = rest
        sources, buffers = ((kkt_hbm, act_hbm, lim_hbm), (kkt_ref, act_ref, lim_ref))
        old_ref = None
    else:
        s_ref, index_ref, lev_ref, kkt_hbm, act_hbm, lim_hbm, old_hbm, y_hbm, acc_ref, *rest = refs
        kkt_ref, act_ref, lim_ref, old_ref, y_ref, sems, out_sems = rest
        sources, buffers = ((kkt_hbm, act_hbm, lim_hbm, old_hbm), (kkt_ref, act_ref, lim_ref, old_ref))
        w_ref = None
    upper = upper_half()
    row16 = lax.broadcasted_iota(jnp.int32, (16, LANES), 0)
    sublane = sublanes()
    bus_count = s_ref.shape[1]
    inner = index_ref.shape[1]
    groups = bus_count // (GROUP * BLK)
    chunk = inner // CHUNKS
    for c in range(CHUNKS):
        for copy in chunk_copies(sources, buffers, sems, c, chunk):
            copy.start()
    buses, branches = (bus_count // groups, inner // groups)
    per_pair = branches // (GROUP // 2)
    per_chunk = groups // CHUNKS

    def group(g):
        for p in range(GROUP // 2):
            base = g * buses + p * PAIR
            tables = [doubled(s_ref[:, lanes(base + h * LANES)]) for h in range(4)]
            sums = [jnp.zeros((8, LANES), F32)] * 4
            weights = jnp.zeros((16, LANES), F32)
            for t in range(per_pair // LANES):
                cols = lanes(g * branches + p * per_pair + t * LANES)
                ends, near, far, tiles = inner_ends_of(tables, index_ref, base, cols, t, upper)
                penalty = 0.25 * lev_ref[0:1, cols].astype(F32)
                if first:
                    scaled, target = (None, ends)
                else:
                    scaled = old_ref[:, cols] - ends
                    target = ends - scaled
                flows = product(kkt_ref, cols, target)
                flows = jnp.where(act_ref[:, cols] == 1, lim_ref[:, cols], flows)
                y = flows if first else flows + scaled
                y_ref[:, cols] = y
                high, low = halves(spread8(penalty) * y)
                from_part = jnp.where(upper, high, pltpu.roll(low, 4, 0))
                to_part = jnp.where(upper, pltpu.roll(high, 4, 0), low)
                near_tile, far_tile = (spread8(near >> 7), spread8(far >> 7))
                left = [
                    jnp.concatenate(
                        [
                            jnp.where(near_tile == h, from_part, 0.0),
                            jnp.where(far_tile == h, to_part, 0.0),
                        ],
                        axis=1,
                    )
                    for h in tiles
                ]
                if first:
                    level = spread8(penalty, 16)
                    left.append(
                        jnp.concatenate(
                            [
                                jnp.where(spread8(near >> 7, 16) == row16, level, 0.0),
                                jnp.where(spread8(far >> 7, 16) == row16, level, 0.0),
                            ],
                            axis=1,
                        )
                    )
                right = jnp.concatenate([one_hot(near, sublane), one_hot(far, sublane)], axis=1)
                out = contract(jnp.concatenate(left, axis=0), right)
                for place, h in enumerate(tiles):
                    sums[h] = sums[h] + out[8 * place : 8 * place + 8]
                if first:
                    weights = weights + out[8 * len(tiles) :]
            for h in range(4):
                spot = lanes(base + h * LANES)
                acc_ref[:, spot] = sums[h]
                if first:
                    w_ref[0:1, spot] = weights[h : h + 1]

    for c in range(CHUNKS):
        for copy in chunk_copies(sources, buffers, sems, c, chunk):
            copy.wait()

        @pl.loop(c * per_chunk, (c + 1) * per_chunk)
        def _(g):
            group(g)

        spot = pl.ds(c * chunk, chunk)
        pltpu.make_async_copy(y_ref.at[:, spot], y_hbm.at[:, spot], out_sems.at[c]).start()
    for c in range(CHUNKS):
        spot = pl.ds(c * chunk, chunk)
        pltpu.make_async_copy(y_ref.at[:, spot], y_hbm.at[:, spot], out_sems.at[c]).wait()


def list_places(list_ref, g, base):
    count = list_ref.shape[1] // 4
    return [list_ref[0:1, lanes(k * count + g * LANES)] - base for k in range(4)]


def list_picks(tables, places, upper):
    picks = []
    for k in (0, 2):
        both = jnp.where(upper, spread8(places[k]), spread8(places[k + 1]))
        picks.append(pick(tables, both, range(len(tables))))
    return picks


def even_sides():
    return lax.axis_index("gx") % 2 == 0, lax.axis_index("gy") % 2 == 0


def slots(outs, block):
    even_x, even_y = even_sides()
    wanted = (
        jnp.where(even_x, 1, 0),
        jnp.where(even_x, 0, 1),
        jnp.where(even_y, 3, 2),
        jnp.where(even_y, 2, 3),
    )
    return [(ref, block == want) for ref, want in zip(outs, wanted)]


def write_ghosts(outs, picks, g):
    even_x, even_y = even_sides()
    spot = lanes(g * LANES)
    for out_even, out_odd, even, both in (
        (outs[0], outs[1], even_x, picks[0]),
        (outs[2], outs[3], even_y, picks[1]),
    ):
        out_even[0:4, spot] = jnp.where(even, both[:4], both[4:])
        out_odd[0:4, spot] = jnp.where(even, both[4:], both[:4])


def read_ghost(got, block, spot):
    even_x, even_y = even_sides()
    by_even = jnp.where(even_x, block == 1, block == 0) | jnp.where(even_y, block == 3, block == 2)
    return jnp.where(
        block < 2,
        jnp.where(by_even, got[0][0:4, spot], got[1][0:4, spot]),
        jnp.where(by_even, got[2][0:4, spot], got[3][0:4, spot]),
    )


def hv_states(s_ref, hv_bus_ref, work_ref):
    lane = lax.broadcasted_iota(jnp.int32, (1, LANES), 1)

    def body(t, carry):
        bus = hv_bus_ref[t]
        row = s_ref[2:3, lanes((bus >> 7) * LANES)]
        work_ref[pl.ds(t, 1), :] = jnp.where(lane == (bus & (LANES - 1)), row, 0.0)
        return carry

    lax.fori_loop(0, work_ref.shape[0], body, 0, unroll=8)
    return jnp.broadcast_to(jnp.sum(work_ref[...], axis=1, keepdims=True), work_ref.shape)


def as_row(values, width, offset):
    count = values.shape[0]
    wide = jnp.broadcast_to(values[:, :1], (count, width))
    lane = lax.broadcasted_iota(jnp.int32, (count, width), 1)
    own = lax.broadcasted_iota(jnp.int32, (count, width), 0)
    return jnp.sum(jnp.where(lane == own + offset, wide, 0.0), axis=0, keepdims=True)


def write_hv(out_ref, values, penalties):
    width = out_ref.shape[-1]
    row = as_row(values, width, 0) + as_row(penalties, width, values.shape[0])
    out_ref[...] = jnp.broadcast_to(row, out_ref.shape)


def start_kernel(
    bus_ref, level_ref, s_ref, list_ref, from_ref, kkt_ref, act_ref, lim_ref, lev_ref,
    xe_ref, xo_ref, ye_ref, yo_ref, z_ref, hv_ref, hv_own_ref, hv_pen_ref, work_ref, turn_ref,
):
    outs = (xe_ref, xo_ref, ye_ref, yo_ref)
    upper = upper_half()
    values = hv_states(s_ref, bus_ref, work_ref)
    hv_own_ref[...] = values

    def body(t, carry):
        hv_pen_ref[pl.ds(t, 1), :] = jnp.full((1, LANES), level_ref[t], jnp.int32).astype(F32) * 0.25
        return carry

    lax.fori_loop(0, hv_pen_ref.shape[0], body, 0, unroll=8)
    write_hv(hv_ref, values, hv_pen_ref[...])
    groups = s_ref.shape[1] // (GROUP * BLK)
    buses, cross = (GROUP * BLK, from_ref.shape[1] // groups)
    per_list = xe_ref.shape[1] // cross

    @pl.loop(0, groups)
    def _(g):
        base = g * buses
        tables = [doubled(s_ref[:, lanes(base + h * LANES)]) for h in range(buses // LANES)]
        picks = list_picks(tables, list_places(list_ref, g, base), upper)
        z_ref[0:8, lanes(g * LANES)] = picks[0]
        z_ref[8:16, lanes(g * LANES)] = picks[1]
        write_ghosts(outs, picks, g)
        found = []
        for t in range(cross // LANES):
            cols = lanes(g * cross + t * LANES)
            index = spread8(from_ref[0:1, cols] - (base + t * PAIR))
            ends = pick(tables[4 * t : 4 * t + 4], index, range(4))
            fixed = act_ref[:, cols] == 1
            part = jnp.where(fixed, lim_ref[:, cols], product(kkt_ref, cols, jnp.where(upper, ends, 0.0)))
            for i in range(8):
                turn_ref[64 * t + 8 * i : 64 * t + 8 * i + 8, :] = kkt_ref[8 * i : 8 * i + 8, cols]
            block = [
                jnp.where(fixed, 0.0, turn_ref[pl.ds(64 * t + 4 + j, 8, stride=8), :])[4:] for j in range(4)
            ]
            found.append((part[4:], block, 0.25 * lev_ref[0:1, cols].astype(F32)))
        for ref, here in slots(outs, g // per_list):

            @pl.when(here)
            def _():
                for t, (part, block, penalty) in enumerate(found):
                    spot = lanes((g % per_list) * cross + t * LANES)
                    ref[4:8, spot] = part
                    for j in range(4):
                        ref[8 + 4 * j : 12 + 4 * j, spot] = block[j]
                    ref[24:25, spot] = penalty


def far_hv(first, bus_ref, partner_ref, all_ref, own, penalty, scaled, sum_ref, weight_ref, work_ref, other_ref):
    count = work_ref.shape[0]
    width = all_ref.shape[-1]
    lane = lax.broadcasted_iota(jnp.int32, (1, LANES), 1)
    wide = lax.broadcasted_iota(jnp.int32, (1, width), 1)

    def narrow(row):
        return functools.reduce(jnp.add, [row[:, k : k + LANES] for k in range(0, width, LANES)])

    def fetch(t, carry):
        partner = partner_ref[t]
        device, place = (partner // count, partner % count)
        row = all_ref[pl.ds(device, 1), :]
        work_ref[pl.ds(t, 1), :] = narrow(jnp.where(wide == place, row, 0.0))
        other_ref[pl.ds(t, 1), :] = narrow(jnp.where(wide == place + count, row, 0.0))
        return carry

    lax.fori_loop(0, count, fetch, 0, unroll=8)
    far_value = jnp.sum(work_ref[...], axis=1, keepdims=True)
    far_penalty = jnp.sum(other_ref[...], axis=1, keepdims=True)
    flow = (penalty * own - far_penalty * far_value) / (penalty + far_penalty)
    y = flow if first else flow + scaled
    work_ref[...] = penalty * y
    other_ref[...] = penalty
    sum_ref[...] = jnp.zeros_like(sum_ref)
    if first:
        weight_ref[...] = jnp.zeros_like(weight_ref)

    def place_terms(t, carry):
        bus = bus_ref[t]
        spot = lanes((bus >> 7) * LANES)
        here = lane == (bus & (LANES - 1))
        sum_ref[0:1, spot] += jnp.where(here, work_ref[pl.ds(t, 1), :], 0.0)
        if first:
            weight_ref[0:1, spot] += jnp.where(here, other_ref[pl.ds(t, 1), :], 0.0)
        return carry

    lax.fori_loop(0, count, place_terms, 0, unroll=8)
    return y


def outer_kernel(first, *refs):
    if first:
        (
            bus_ref, partner_ref, all_ref, own_ref, hv_pen_ref, xe, xo, ye, yo, acc_ref, weight_in_ref,
            s_ref, list_ref, from_ref, kkt_ref, act_ref, lim_ref, lev_ref, z_ref, target_ref, prior_ref,
            new_ref, inv_ref, oxe, oxo, oye, oyo, yc_ref, ym_ref, zn_ref, hv_ref, hv_scaled_ref, hv_own_ref,
            sum_ref, hv_weight_ref, work_ref, other_ref,
        ) = refs
        now = (xe, xo, ye, yo)
        scaled = None
    else:
        (
            bus_ref, partner_ref, all_ref, own_ref, hv_pen_ref, scaled_ref, xe, xo, ye, yo, nxe, nxo, nye, nyo,
            acc_ref, inv_ref, s_ref, list_ref, from_ref, kkt_ref, act_ref, lim_ref, lev_ref, z_ref, yc_old_ref,
            ym_old_ref, target_ref, prior_ref,
            new_ref, state_ref, oxe, oxo, oye, oyo, yc_ref, hv_dual_ref,
            sum_ref, work_ref, other_ref,
        ) = refs
        now = (nxe, nxo, nye, nyo)
        hv_weight_ref = None
        scaled = scaled_ref[...]
    fixed_parts = (xe, xo, ye, yo)
    outs = (oxe, oxo, oye, oyo)
    upper = upper_half()
    row8 = lax.broadcasted_iota(jnp.int32, (8, LANES), 0)
    row16 = lax.broadcasted_iota(jnp.int32, (16, LANES), 0)
    power = (row8 == 2) | (row8 == 6)
    sublane = sublanes()
    even_x, even_y = even_sides()
    groups = s_ref.shape[1] // (GROUP * BLK)
    buses, cross = (GROUP * BLK, from_ref.shape[1] // groups)
    per_list = xe.shape[1] // cross
    count = buses // LANES
    hv_y = far_hv(
        first, bus_ref, partner_ref, all_ref, own_ref[...], hv_pen_ref[...], scaled, sum_ref, hv_weight_ref,
        work_ref, other_ref,
    )

    @pl.loop(0, groups)
    def _(g):
        base = g * buses
        tables = [doubled(s_ref[:, lanes(base + h * LANES)]) for h in range(count)]
        places = list_places(list_ref, g, base)
        sums = [None] * count
        weights = [None] * count
        outputs = []
        for t in range(cross // LANES):
            cols = lanes(g * cross + t * LANES)
            ghost = read_ghost(now, g // per_list, lanes((g % per_list) * cross + t * LANES))
            near = from_ref[0:1, cols] - (base + t * PAIR)
            ends = pick(tables[4 * t : 4 * t + 4], spread8(near), range(4))
            ends = jnp.where(upper, ends, doubled(ghost))
            penalty = 0.25 * lev_ref[0:1, cols].astype(F32)
            if first:
                scaled, target = (None, ends)
            else:
                scaled = yc_old_ref[:, cols] - ends
                target = ends - scaled
            flows = product(kkt_ref, cols, target)
            flows = jnp.where(act_ref[:, cols] == 1, lim_ref[:, cols], flows)
            y = flows if first else flows + scaled
            yc_ref[:, cols] = y
            outputs.append(y)
            high, low = halves(spread8(penalty) * y)
            part = jnp.where(upper, high, pltpu.roll(low, 4, 0))
            tile = spread8(near >> 7)
            left = [jnp.where(tile == h, part, 0.0) for h in range(4)]
            if first:
                left.append(jnp.where(spread8(near >> 7, 16) == row16, spread8(penalty, 16), 0.0))
            out = contract(jnp.concatenate(left, axis=0), one_hot(near, sublane))
            for h in range(4):
                sums[4 * t + h] = out[8 * h : 8 * h + 8]
                if first:
                    weights[4 * t + h] = out[32 + h : 33 + h]

        spot = lanes(g * LANES)
        lefts, rights = ([], [])
        for k, (even, pair) in enumerate(((even_x, 0), (even_x, 1), (even_y, 0), (even_y, 1))):
            start = 0 if k < 2 else 2
            from_even = even if pair == 0 else jnp.logical_not(even)

            def received(parts, rows):
                return jnp.where(from_even, parts[start][rows, spot], parts[start + 1][rows, spot])

            rows = slice(4 * k, 4 * k + 4)
            held = z_ref[rows, spot]
            if first:
                scaled, target = (None, held)
            else:
                scaled = ym_old_ref[rows, spot] - held
                target = held - scaled
            flows = received(now, slice(4, 8))
            for j in range(4):
                flows = flows + received(fixed_parts, slice(8 + 4 * j, 12 + 4 * j)) * spread8(target[j : j + 1], 4)
            penalty = received(fixed_parts, slice(24, 25))
            y = flows if first else flows + scaled
            if first:
                ym_ref[rows, spot] = y
            high, low = halves(spread8(penalty, 4) * y)
            part = jnp.concatenate([high, low], axis=0)
            tile = spread8(places[k] >> 7)
            left = [jnp.where(tile == h, part, 0.0) for h in range(count)]
            if first:
                left.append(jnp.where(spread8(places[k] >> 7, 16) == row16, spread8(penalty, 16), 0.0))
            lefts.append(jnp.concatenate(left, axis=0))
            rights.append(one_hot(places[k], sublane))
        out = contract(jnp.concatenate(lefts[:2], axis=1), jnp.concatenate(rights[:2], axis=1))
        out = out + contract(jnp.concatenate(lefts[2:], axis=1), jnp.concatenate(rights[2:], axis=1))

        fresh = []
        for h in range(count):
            cols = lanes(base + h * LANES)
            total = acc_ref[:, cols] + sums[h] + out[8 * h : 8 * h + 8]
            total = total + pltpu.roll(total, 4, 0)
            total = total + jnp.where(power, spread8(sum_ref[0:1, cols]), 0.0)
            prior = doubled(prior_ref[:, cols])
            total = total + prior * doubled(target_ref[:, cols])
            if first:
                weight = weight_in_ref[0:1, cols] + weights[h] + out[8 * count + h : 8 * count + h + 1]
                weight = spread8(weight) + jnp.where(power, spread8(hv_weight_ref[0:1, cols]), 0.0) + prior
                inverse = 1.0 / weight
                inv_ref[:, cols] = inverse
            else:
                inverse = inv_ref[:, cols]
            state = total * inverse
            new_ref[:, cols] = state
            if not first:
                state_ref[:, cols] = state[:4]
            fresh.append(state)

        picks = list_picks(fresh, places, upper)
        write_ghosts(outs, picks, g)
        if first:
            zn_ref[0:8, spot] = picks[0]
            zn_ref[8:16, spot] = picks[1]
            parts = []
            for t in range(cross // LANES):
                cols = lanes(g * cross + t * LANES)
                near = from_ref[0:1, cols] - (base + t * PAIR)
                ends = pick(fresh[4 * t : 4 * t + 4], spread8(near), range(4))
                target = 2.0 * ends - outputs[t]
                part = product(kkt_ref, cols, jnp.where(upper, target, 0.0))
                parts.append(jnp.where(act_ref[:, cols] == 1, lim_ref[:, cols], part)[4:])
            for ref, here in slots(outs, g // per_list):

                @pl.when(here)
                def _():
                    for t, part in enumerate(parts):
                        ref[4:8, lanes((g % per_list) * cross + t * LANES)] = part

    reached = hv_states(new_ref, bus_ref, work_ref)
    left_over = hv_y - reached
    penalty = hv_pen_ref[...]
    if first:
        hv_scaled_ref[...] = left_over
        hv_own_ref[...] = reached - left_over
        write_hv(hv_ref, reached - left_over, penalty)
    else:
        row = as_row(penalty * left_over, LANES, 0)
        hv_dual_ref[...] = row[:, : hv_dual_ref.shape[1]]


def inner_dual_kernel(s_ref, index_ref, y_ref, lev_ref, dual_ref):
    upper = upper_half()
    groups = s_ref.shape[1] // (GROUP * BLK)
    branches = index_ref.shape[1] // groups
    per_pair = branches // (GROUP // 2)

    @pl.loop(0, groups)
    def _(g):
        for p in range(GROUP // 2):
            base = g * GROUP * BLK + p * PAIR
            tables = [s_ref[:, lanes(base + h * LANES)] for h in range(4)]
            for t in range(per_pair // LANES):
                cols = lanes(g * branches + p * per_pair + t * LANES)
                ends, _, _, _ = inner_ends_of(tables, index_ref, base, cols, t, upper)
                penalty = 0.25 * lev_ref[0:1, cols].astype(F32)
                dual_ref[:, cols] = spread8(penalty) * (y_ref[:, cols] - ends)


def outer_dual_kernel(dual_in_ref, xe, xo, ye, yo, s_ref, from_ref, y_ref, lev_ref, dual_ref):
    upper = upper_half()
    groups = s_ref.shape[1] // (GROUP * BLK)
    cross = from_ref.shape[1] // groups
    per_list = xe.shape[1] // cross

    @pl.loop(0, groups)
    def _(g):
        for t in range(cross // LANES):
            base = g * GROUP * BLK + t * PAIR
            cols = lanes(g * cross + t * LANES)
            ghost = read_ghost((xe, xo, ye, yo), g // per_list, lanes((g % per_list) * cross + t * LANES))
            near = from_ref[0:1, cols] - base
            tables = [s_ref[:, lanes(base + h * LANES)] for h in range(4)]
            ends = pick(tables, spread8(near), range(4))
            ends = jnp.where(upper, ends, doubled(ghost))
            penalty = 0.25 * lev_ref[0:1, cols].astype(F32)
            dual_ref[:, cols] = spread8(penalty) * (y_ref[:, cols] - ends)


def part(rows, width, index=0):
    return pl.BlockSpec((rows, width), lambda g: (0, index))


def scalars():
    return pl.BlockSpec(memory_space=pltpu.SMEM)


def in_place():
    return pl.BlockSpec(memory_space=pl.ANY)


def shape_of(*dims):
    return jax.ShapeDtypeStruct(dims, F32)


def params():
    return pltpu.CompilerParams(
        dimension_semantics=("arbitrary",), vmem_limit_bytes=24 * 1024 * 1024
    )


def cost(flops, moved):
    return pl.CostEstimate(flops=flops, bytes_accessed=moved, transcendentals=0)


def on_device(
    bus_start, bus_target, bus_weight, inner_ends, cross_from, boundary_lists, kkt_map, active_set, limits,
    penalty_level, hv_bus, hv_partner, hv_level,
):
    def hbm(x):
        return pltpu.with_memory_space_constraint(x, pltpu.HBM)

    bus_start, bus_target, bus_weight, inner_ends, boundary_lists, active_set, limits = map(
        hbm, (bus_start, bus_target, bus_weight, inner_ends, boundary_lists, active_set, limits)
    )
    hv_bus, hv_partner, hv_level = map(hbm, (hv_bus, hv_partner, hv_level))
    _, bus_count = bus_start.shape
    list_len = boundary_lists.shape[1] // 4
    inner = inner_ends.shape[1]
    cross = cross_from.shape[0]
    branches = kkt_map.shape[2]
    terms = hv_bus.shape[0]
    devices = lax.axis_size("gx") * lax.axis_size("gy")
    behind = inner // cross
    hv_width = max(LANES, 2 * terms)
    kkt = hbm(kkt_map.reshape(64, branches))
    from_row = hbm(cross_from.reshape(1, cross))
    level_row = hbm(penalty_level.reshape(1, branches))
    lists = part(1, 4 * list_len)
    level_in = part(1, inner)
    cross_args = (from_row, kkt, active_set, limits, level_row)
    cross_specs = [part(1, cross), part(64, cross, behind), part(8, cross, behind), part(8, cross, behind), part(1, cross, behind)]
    hv_block = (terms, LANES)
    hv_all_spec = part(devices, hv_width)
    hv_spec = part(*hv_block)
    state_spec, state4_spec, row_spec = (part(8, bus_count), part(4, bus_count), part(1, bus_count))
    held_spec = part(16, list_len)
    common = dict(grid=(1,), compiler_params=params())

    *sent, held, hv_rows, hv_own, hv_pen = pl.pallas_call(
        start_kernel,
        name="first_messages",
        in_specs=[scalars(), scalars(), state4_spec, lists] + cross_specs,
        out_shape=[shape_of(STATIC_ROWS, list_len)] * 4
        + [shape_of(16, list_len), shape_of(devices, hv_width), shape_of(*hv_block), shape_of(*hv_block)],
        out_specs=[part(STATIC_ROWS, list_len)] * 4 + [held_spec, hv_all_spec, hv_spec, hv_spec],
        scratch_shapes=[
            pltpu.VMEM(hv_block, F32),
            pltpu.VMEM((64 * (GROUP // 2), LANES), F32),
        ],
        cost_estimate=cost(10**6, 4 * 10**6),
        **common,
    )(hv_bus, hv_level, bus_start, boundary_lists, *cross_args)

    def exchange(messages):
        xe, xo, ye, yo = messages
        xo = swapped(xo, "gx", 1)
        yo = swapped(yo, "gy", 1)
        xe = swapped(xe, "gx", 0)
        ye = swapped(ye, "gy", 0)
        return (xe, xo, ye, yo)

    def buffers(count):
        kinds = [F32, jnp.int32, F32, F32][:count]
        return (
            [pltpu.VMEM((64 if k == 0 else 8, inner), kind) for k, kind in enumerate(kinds)]
            + [pltpu.VMEM((8, inner), F32)]
            + [pltpu.SemaphoreType.DMA((count, CHUNKS)), pltpu.SemaphoreType.DMA((CHUNKS,))]
        )

    first_got = exchange(sent)
    hv_all = to_all(hv_rows)
    y_inner, sums, weights = pl.pallas_call(
        functools.partial(inner_kernel, True),
        name="inner_first",
        in_specs=[state4_spec, part(2, inner), level_in] + [in_place()] * 3,
        out_shape=[shape_of(8, inner), shape_of(8, bus_count), shape_of(1, bus_count)],
        out_specs=[in_place(), state_spec, row_spec],
        scratch_shapes=buffers(3),
        cost_estimate=cost(10**8, 10**7),
        **common,
    )(bus_start, inner_ends, level_row, kkt, active_set, limits)
    message = part(8, list_len)
    state, inverse, *rest = pl.pallas_call(
        functools.partial(outer_kernel, True),
        name="outer_first",
        in_specs=[scalars()] * 2
        + [hv_all_spec, hv_spec, hv_spec]
        + [part(STATIC_ROWS, list_len)] * 4
        + [state_spec, row_spec, state4_spec, lists]
        + cross_specs
        + [held_spec, state4_spec, state4_spec],
        out_shape=[shape_of(8, bus_count), shape_of(8, bus_count)]
        + [shape_of(8, list_len)] * 4
        + [shape_of(8, cross), pltpu.HBM((16, list_len), F32), pltpu.HBM((16, list_len), F32)]
        + [shape_of(devices, hv_width), pltpu.HBM(hv_block, F32), pltpu.HBM(hv_block, F32)],
        out_specs=[state_spec, state_spec]
        + [message] * 4
        + [part(8, cross), held_spec, held_spec]
        + [hv_all_spec, hv_spec, hv_spec],
        scratch_shapes=[pltpu.VMEM((1, bus_count), F32)] * 2 + [pltpu.VMEM(hv_block, F32)] * 2,
        cost_estimate=cost(10**7, 5 * 10**6),
        **common,
    )(
        hv_bus, hv_partner, hv_all, hv_own, hv_pen, *first_got, sums, weights, bus_start, boundary_lists,
        *cross_args, held, bus_target, bus_weight,
    )
    sent, (y_cross, y_mirror, held, hv_rows, hv_scaled, hv_own) = (rest[:4], rest[4:])
    y_mirror, held, hv_scaled, hv_own = map(hbm, (y_mirror, held, hv_scaled, hv_own))

    second_got = exchange(sent)
    hv_all = to_all(hv_rows)
    y_inner, sums = pl.pallas_call(
        functools.partial(inner_kernel, False),
        name="inner_second",
        in_specs=[state_spec, part(2, inner), level_in] + [in_place()] * 4,
        out_shape=[shape_of(8, inner), shape_of(8, bus_count)],
        out_specs=[in_place(), state_spec],
        scratch_shapes=buffers(4),
        cost_estimate=cost(10**8, 10**7),
        **common,
    )(state, inner_ends, level_row, kkt, active_set, limits, y_inner)
    last = part(4, list_len)
    state, bus_state, *rest = pl.pallas_call(
        functools.partial(outer_kernel, False),
        name="outer_second",
        in_specs=[scalars()] * 2
        + [hv_all_spec, hv_spec, hv_spec, hv_spec]
        + [part(STATIC_ROWS, list_len)] * 4
        + [message] * 4
        + [state_spec, state_spec, state_spec, lists]
        + cross_specs
        + [held_spec, part(8, cross), held_spec, state4_spec, state4_spec],
        out_shape=[shape_of(8, bus_count), shape_of(4, bus_count)]
        + [shape_of(4, list_len)] * 4
        + [shape_of(8, cross), shape_of(1, terms)],
        out_specs=[state_spec, state4_spec] + [last] * 4 + [part(8, cross), part(1, terms)],
        scratch_shapes=[pltpu.VMEM((1, bus_count), F32)] + [pltpu.VMEM(hv_block, F32)] * 2,
        cost_estimate=cost(10**7, 5 * 10**6),
        **common,
    )(
        hv_bus, hv_partner, hv_all, hv_own, hv_pen, hv_scaled, *first_got, *second_got, sums, inverse, state,
        boundary_lists, *cross_args, held, y_cross, y_mirror, bus_target, bus_weight,
    )
    sent, (y_cross, hv_dual) = (rest[:4], rest[4:])

    last_got = exchange(sent)
    duals = pl.pallas_call(
        inner_dual_kernel,
        name="inner_duals",
        in_specs=[state_spec, part(2, inner), part(8, inner), level_in],
        out_shape=shape_of(8, branches),
        out_specs=part(8, inner),
        cost_estimate=cost(10**7, 3 * 10**6),
        **common,
    )(state, inner_ends, y_inner, level_row)
    duals = pl.pallas_call(
        outer_dual_kernel,
        name="outer_duals",
        in_specs=[in_place()] + [last] * 4 + [state_spec, part(1, cross), part(8, cross), part(1, cross, behind)],
        out_shape=shape_of(8, branches),
        out_specs=part(8, cross, behind),
        input_output_aliases={0: 0},
        cost_estimate=cost(10**6, 10**6),
        **common,
    )(duals, *last_got, state, from_row, y_cross, level_row)
    return (bus_state, duals, hv_dual.reshape(terms))


def solution(mesh):
    return jax.shard_map(
        on_device,
        mesh=mesh,
        in_specs=(
            P(None, ("gx", "gy")),
            P(None, ("gx", "gy")),
            P(None, ("gx", "gy")),
            P(None, ("gx", "gy")),
            P(("gx", "gy")),
            P(("gx", "gy"), None),
            P(None, None, ("gx", "gy")),
            P(None, ("gx", "gy")),
            P(None, ("gx", "gy")),
            P(("gx", "gy")),
            P(("gx", "gy")),
            P(("gx", "gy")),
            P(("gx", "gy")),
        ),
        out_specs=(P(None, ("gx", "gy")), P(None, ("gx", "gy")), P(("gx", "gy"))),
        check_vma=False,
    )
```

```python
import functools

import jax
import jax.numpy as jnp
from jax import lax
from jax.experimental import pallas as pl
from jax.experimental.pallas import tpu as pltpu
from jax.sharding import PartitionSpec as P

F32 = jnp.float32
BF16 = jnp.bfloat16
BLK = 256
LANES = 128
GROUP = 8
PAIR = 2 * BLK
SPAN = 64
STATIC_ROWS = 25


def swapped(value, axis, first):
    count = lax.axis_size(axis)
    moves = []
    for low in range(first, count - 1, 2):
        moves += [(low, low + 1), (low + 1, low)]
    return lax.ppermute(value, axis, moves)


def to_all(rows):
    return lax.all_to_all(rows, ("gx", "gy"), split_axis=0, concat_axis=0, tiled=True)


def take_lanes(table, lane):
    return lax.gather(
        table,
        lane[..., None],
        lax.GatherDimensionNumbers(
            offset_dims=(),
            collapsed_slice_dims=(1,),
            start_index_map=(1,),
            operand_batching_dims=(0,),
            start_indices_batching_dims=(0,),
        ),
        (1, 1),
        mode=lax.GatherScatterMode.PROMISE_IN_BOUNDS,
    )


def pick(tables, index, tiles):
    lane, tile = (index & (LANES - 1), index >> 7)
    found = None
    for h in tiles:
        got = take_lanes(tables[h], lane)
        found = got if found is None else jnp.where(tile == h, got, found)
    return found


def spread8(row, rows=8):
    return jnp.broadcast_to(row, (rows, row.shape[-1]))


def one_hot(index, sublane):
    length = sublane.shape[0]
    low = spread8(index & (length - 1), 16).astype(F32).astype(BF16)
    column = jnp.concatenate([low] * (length // 16), axis=0)
    return jnp.where(column == sublane, jnp.ones((), BF16), jnp.zeros((), BF16))


def contract(left, right):
    return lax.dot_general(
        left.astype(BF16), right, (((1,), (1,)), ((), ())), preferred_element_type=F32
    )


def halves(values):
    high = values.astype(BF16).astype(F32)
    return high, values - high


def sublanes(length):
    return lax.broadcasted_iota(jnp.int32, (length, LANES), 0).astype(F32).astype(BF16)


def folded(first, second, distance, mask):
    return jnp.where(
        mask,
        first + pltpu.roll(first, 8 - distance, 0),
        second + pltpu.roll(second, distance, 0),
    )


def product(kkt_ref, cols, target):
    row = lax.broadcasted_iota(jnp.int32, (8, LANES), 0)
    terms = [kkt_ref[8 * i : 8 * i + 8, cols] * target for i in range(8)]
    upper = row < 4
    quads = [
        jnp.where(upper, terms[i], terms[i + 4]) + pltpu.roll(jnp.where(upper, terms[i + 4], terms[i]), 4, 0)
        for i in range(4)
    ]
    even_two = (row & 2) == 0
    twos = [folded(quads[i], quads[i + 2], 2, even_two) for i in range(2)]
    return folded(twos[0], twos[1], 1, (row & 1) == 0)


def doubled(block):
    return block if block.shape[0] == 8 else jnp.concatenate([block, block], axis=0)


def tiles_of(states):
    return [states[:, h * LANES : (h + 1) * LANES] for h in range(states.shape[1] // LANES)]


def lanes(start):
    return pl.ds(pl.multiple_of(start, LANES), LANES)


def upper_half():
    return lax.broadcasted_iota(jnp.int32, (8, LANES), 0) < 4


def inner_ends_of(tables, index_ref, base, cols, t, upper):
    near = index_ref[0:1, cols] - base
    far = index_ref[1:2, cols] - base
    tiles = (0, 1) if t < 2 else (2, 3) if t > 2 else (0, 1, 2, 3)
    both = jnp.where(upper, spread8(near), spread8(far))
    return pick(tables, both, tiles), near, far, tiles


def fetching(kernel, spots):
    def wrapped(*refs):
        *refs, sems = refs
        buffers = refs[len(refs) - len(spots) :]
        refs = list(refs[: len(refs) - len(spots)])
        copies = []
        for k, ((place, first), buffer) in enumerate(zip(spots.items(), buffers)):
            source = refs[place].at[:, pl.ds(first, buffer.shape[1])]
            copies.append(pltpu.make_async_copy(source, buffer, sems.at[k]))
            copies[-1].start()
            refs[place] = buffer

        def ready():
            for copy in copies:
                copy.wait()

        kernel(ready, *refs)

    return wrapped


def fetched(*shapes):
    return [pltpu.VMEM(shape, kind) for shape, kind in shapes] + [pltpu.SemaphoreType.DMA((len(shapes),))]


def chunk_copies(sources, buffers, sems, chunk, width):
    spot = pl.ds(pl.multiple_of(chunk * width, LANES), width)
    return [
        pltpu.make_async_copy(source.at[:, spot], buffer.at[:, spot], sems.at[k, chunk])
        for k, (source, buffer) in enumerate(zip(sources, buffers))
    ]


def inner_kernel(first, ready, *refs):
    if first:
        s_ref, index_ref, lev_ref, kkt_hbm, act_hbm, lim_hbm, y_hbm, acc_ref, w_ref, *rest = refs
        kkt_ref, act_ref, lim_ref, y_ref, sems, out_sems = rest
        sources, buffers = ((kkt_hbm, act_hbm, lim_hbm), (kkt_ref, act_ref, lim_ref))
        old_ref = None
    else:
        s_ref, index_ref, lev_ref, kkt_hbm, act_hbm, lim_hbm, old_hbm, y_hbm, acc_ref, *rest = refs
        kkt_ref, act_ref, lim_ref, old_ref, y_ref, sems, out_sems = rest
        sources, buffers = ((kkt_hbm, act_hbm, lim_hbm, old_hbm), (kkt_ref, act_ref, lim_ref, old_ref))
        w_ref = None
    upper = upper_half()
    row16 = lax.broadcasted_iota(jnp.int32, (16, LANES), 0)
    sublane = sublanes(SPAN)
    bus_count = s_ref.shape[1]
    inner = index_ref.shape[1]
    groups = bus_count // (GROUP * BLK)
    buses, branches = (bus_count // groups, inner // groups)
    per_pair = branches // (GROUP // 2)

    @pl.loop(0, groups)
    def _(g):
        for copy in chunk_copies(sources, buffers, sems, g, branches):
            copy.start()

    ready()

    def group(g):
        for p in range(GROUP // 2):
            base = g * buses + p * PAIR
            tables = [doubled(s_ref[:, lanes(base + h * LANES)]) for h in range(4)]
            sums = [jnp.zeros((8, SPAN), F32)] * (PAIR // SPAN)
            weights = jnp.zeros((16, SPAN), F32)
            jobs = []
            for t in range(per_pair // LANES):
                cols = lanes(g * branches + p * per_pair + t * LANES)
                ends, near, far, tiles = inner_ends_of(tables, index_ref, base, cols, t, upper)
                penalty = 0.25 * lev_ref[0:1, cols].astype(F32)
                if first:
                    scaled, target = (None, ends)
                else:
                    scaled = old_ref[:, cols] - ends
                    target = ends - scaled
                flows = product(kkt_ref, cols, target)
                flows = jnp.where(act_ref[:, cols] == 1, lim_ref[:, cols], flows)
                y = flows if first else flows + scaled
                y_ref[:, cols] = y
                high, low = halves(spread8(penalty) * y)
                from_part = jnp.where(upper, high, pltpu.roll(low, 4, 0))
                to_part = jnp.where(upper, pltpu.roll(high, 4, 0), low)
                near_span, far_span = (near >> 6, far >> 6)
                near_tile, far_tile = (spread8(near_span), spread8(far_span))
                spans = [2 * h + half for h in tiles for half in range(2)]
                left = [
                    jnp.concatenate(
                        [
                            jnp.where(near_tile == h, from_part, 0.0),
                            jnp.where(far_tile == h, to_part, 0.0),
                        ],
                        axis=1,
                    )
                    for h in spans
                ]
                if first:
                    level = spread8(penalty, 16)
                    left.append(
                        jnp.concatenate(
                            [
                                jnp.where(spread8(near_span, 16) == row16, level, 0.0),
                                jnp.where(spread8(far_span, 16) == row16, level, 0.0),
                            ],
                            axis=1,
                        )
                    )
                right = jnp.concatenate([one_hot(near, sublane), one_hot(far, sublane)], axis=1)
                jobs.append((jnp.concatenate(left, axis=0).astype(BF16), right, spans))
            for left, right, spans in jobs:
                out = contract(left, right)
                for place, h in enumerate(spans):
                    sums[h] = sums[h] + out[8 * place : 8 * place + 8]
                if first:
                    weights = weights + out[8 * len(spans) :]
            for h in range(4):
                spot = lanes(base + h * LANES)
                acc_ref[:, spot] = jnp.concatenate([sums[2 * h], sums[2 * h + 1]], axis=1)
                if first:
                    w_ref[0:1, spot] = jnp.concatenate(
                        [weights[2 * h : 2 * h + 1], weights[2 * h + 1 : 2 * h + 2]], axis=1
                    )

    def out_copy(g):
        spot = pl.ds(pl.multiple_of(g * branches, LANES), branches)
        return pltpu.make_async_copy(y_ref.at[:, spot], y_hbm.at[:, spot], out_sems.at[g])

    @pl.loop(0, groups, step=2)
    def _(start):
        for g in range(2):
            for copy in chunk_copies(sources, buffers, sems, start + g, branches):
                copy.wait()
        for g in range(2):
            group(start + g)
        for g in range(2):
            out_copy(start + g).start()

    @pl.loop(0, groups)
    def _(g):
        out_copy(g).wait()


def list_places(list_ref, g, base):
    count = list_ref.shape[1] // 4
    return [list_ref[0:1, lanes(k * count + g * LANES)] - base for k in range(4)]


def list_picks(tables, places, upper):
    picks = []
    for k in (0, 2):
        both = jnp.where(upper, spread8(places[k]), spread8(places[k + 1]))
        picks.append(pick(tables, both, range(len(tables))))
    return picks


def even_sides():
    return lax.axis_index("gx") % 2 == 0, lax.axis_index("gy") % 2 == 0


def slots(outs, block):
    even_x, even_y = even_sides()
    wanted = (
        jnp.where(even_x, 1, 0),
        jnp.where(even_x, 0, 1),
        jnp.where(even_y, 3, 2),
        jnp.where(even_y, 2, 3),
    )
    return [(ref, block == want) for ref, want in zip(outs, wanted)]


def write_ghosts(outs, picks, g):
    even_x, even_y = even_sides()
    spot = lanes(g * LANES)
    for out_even, out_odd, even, both in (
        (outs[0], outs[1], even_x, picks[0]),
        (outs[2], outs[3], even_y, picks[1]),
    ):
        out_even[0:4, spot] = jnp.where(even, both[:4], both[4:])
        out_odd[0:4, spot] = jnp.where(even, both[4:], both[:4])


def read_ghost(got, block, spot):
    even_x, even_y = even_sides()
    by_even = jnp.where(even_x, block == 1, block == 0) | jnp.where(even_y, block == 3, block == 2)
    return jnp.where(
        block < 2,
        jnp.where(by_even, got[0][0:4, spot], got[1][0:4, spot]),
        jnp.where(by_even, got[2][0:4, spot], got[3][0:4, spot]),
    )


def hv_states(s_ref, hv_bus_ref, work_ref):
    lane = lax.broadcasted_iota(jnp.int32, (1, LANES), 1)

    def body(t, carry):
        bus = hv_bus_ref[t]
        row = s_ref[2:3, lanes((bus >> 7) * LANES)]
        work_ref[pl.ds(t, 1), :] = jnp.where(lane == (bus & (LANES - 1)), row, 0.0)
        return carry

    lax.fori_loop(0, work_ref.shape[0], body, 0, unroll=8)
    return jnp.broadcast_to(jnp.sum(work_ref[...], axis=1, keepdims=True), work_ref.shape)


def as_row(values, width, offset):
    count = values.shape[0]
    wide = jnp.broadcast_to(values[:, :1], (count, width))
    lane = lax.broadcasted_iota(jnp.int32, (count, width), 1)
    own = lax.broadcasted_iota(jnp.int32, (count, width), 0)
    return jnp.sum(jnp.where(lane == own + offset, wide, 0.0), axis=0, keepdims=True)


def write_hv(out_ref, values, penalties):
    width = out_ref.shape[-1]
    row = as_row(values, width, 0) + as_row(penalties, width, values.shape[0])
    out_ref[...] = jnp.broadcast_to(row, out_ref.shape)


def start_kernel(
    bus_ref, level_ref, s_ref, list_ref, from_ref, kkt_ref, act_ref, lim_ref, lev_ref,
    xe_ref, xo_ref, ye_ref, yo_ref, z_ref, hv_ref, hv_own_ref, hv_pen_ref, work_ref, turn_ref,
):
    outs = (xe_ref, xo_ref, ye_ref, yo_ref)
    upper = upper_half()
    values = hv_states(s_ref, bus_ref, work_ref)
    hv_own_ref[...] = values

    def body(t, carry):
        hv_pen_ref[pl.ds(t, 1), :] = jnp.full((1, LANES), level_ref[t], jnp.int32).astype(F32) * 0.25
        return carry

    lax.fori_loop(0, hv_pen_ref.shape[0], body, 0, unroll=8)
    write_hv(hv_ref, values, hv_pen_ref[...])
    groups = s_ref.shape[1] // (GROUP * BLK)
    buses, cross = (GROUP * BLK, from_ref.shape[1] // groups)
    per_list = xe_ref.shape[1] // cross

    @pl.loop(0, groups, unroll=2)
    def _(g):
        base = g * buses
        tables = [doubled(s_ref[:, lanes(base + h * LANES)]) for h in range(buses // LANES)]
        picks = list_picks(tables, list_places(list_ref, g, base), upper)
        z_ref[0:8, lanes(g * LANES)] = picks[0]
        z_ref[8:16, lanes(g * LANES)] = picks[1]
        write_ghosts(outs, picks, g)
        found = []
        for t in range(cross // LANES):
            cols = lanes(g * cross + t * LANES)
            index = spread8(from_ref[0:1, cols] - (base + t * PAIR))
            ends = pick(tables[4 * t : 4 * t + 4], index, range(4))
            fixed = act_ref[:, cols] == 1
            part = jnp.where(fixed, lim_ref[:, cols], product(kkt_ref, cols, jnp.where(upper, ends, 0.0)))
            for i in range(8):
                turn_ref[64 * t + 8 * i : 64 * t + 8 * i + 8, :] = kkt_ref[8 * i : 8 * i + 8, cols]
            block = [
                jnp.where(fixed, 0.0, turn_ref[pl.ds(64 * t + 4 + j, 8, stride=8), :])[4:] for j in range(4)
            ]
            found.append((part[4:], block, 0.25 * lev_ref[0:1, cols].astype(F32)))
        for ref, here in slots(outs, g // per_list):

            @pl.when(here)
            def _():
                for t, (part, block, penalty) in enumerate(found):
                    spot = lanes((g % per_list) * cross + t * LANES)
                    ref[4:8, spot] = part
                    for j in range(4):
                        ref[8 + 4 * j : 12 + 4 * j, spot] = block[j]
                    ref[24:25, spot] = penalty


def far_hv(first, bus_ref, partner_ref, all_ref, own, penalty, scaled, sum_ref, weight_ref, work_ref, other_ref):
    count = work_ref.shape[0]
    width = all_ref.shape[-1]
    lane = lax.broadcasted_iota(jnp.int32, (1, LANES), 1)
    wide = lax.broadcasted_iota(jnp.int32, (1, width), 1)

    def narrow(row):
        return functools.reduce(jnp.add, [row[:, k : k + LANES] for k in range(0, width, LANES)])

    def fetch(t, carry):
        partner = partner_ref[t]
        device, place = (partner // count, partner % count)
        row = all_ref[pl.ds(device, 1), :]
        work_ref[pl.ds(t, 1), :] = narrow(jnp.where(wide == place, row, 0.0))
        other_ref[pl.ds(t, 1), :] = narrow(jnp.where(wide == place + count, row, 0.0))
        return carry

    lax.fori_loop(0, count, fetch, 0, unroll=8)
    far_value = jnp.sum(work_ref[...], axis=1, keepdims=True)
    far_penalty = jnp.sum(other_ref[...], axis=1, keepdims=True)
    flow = (penalty * own - far_penalty * far_value) / (penalty + far_penalty)
    y = flow if first else flow + scaled
    work_ref[...] = penalty * y
    other_ref[...] = penalty
    sum_ref[...] = jnp.zeros_like(sum_ref)
    if first:
        weight_ref[...] = jnp.zeros_like(weight_ref)

    def place_terms(t, carry):
        bus = bus_ref[t]
        spot = lanes((bus >> 7) * LANES)
        here = lane == (bus & (LANES - 1))
        sum_ref[0:1, spot] += jnp.where(here, work_ref[pl.ds(t, 1), :], 0.0)
        if first:
            weight_ref[0:1, spot] += jnp.where(here, other_ref[pl.ds(t, 1), :], 0.0)
        return carry

    lax.fori_loop(0, count, place_terms, 0, unroll=8)
    return y


def outer_kernel(first, *refs):
    if first:
        (
            bus_ref, partner_ref, all_ref, own_ref, hv_pen_ref, xe, xo, ye, yo, acc_ref, weight_in_ref,
            s_ref, list_ref, from_ref, kkt_ref, act_ref, lim_ref, lev_ref, z_ref, target_ref, prior_ref,
            new_ref, inv_ref, oxe, oxo, oye, oyo, yc_ref, ym_ref, zn_ref, hv_ref, hv_scaled_ref, hv_own_ref,
            sum_ref, hv_weight_ref, work_ref, other_ref,
        ) = refs
        now = (xe, xo, ye, yo)
        scaled = None
    else:
        (
            bus_ref, partner_ref, all_ref, own_ref, hv_pen_ref, scaled_ref, xe, xo, ye, yo, nxe, nxo, nye, nyo,
            acc_ref, inv_ref, s_ref, list_ref, from_ref, kkt_ref, act_ref, lim_ref, lev_ref, z_ref, yc_old_ref,
            ym_old_ref, target_ref, prior_ref,
            new_ref, state_ref, oxe, oxo, oye, oyo, yc_ref, hv_dual_ref,
            sum_ref, work_ref, other_ref,
        ) = refs
        now = (nxe, nxo, nye, nyo)
        hv_weight_ref = None
        scaled = scaled_ref[...]
    fixed_parts = (xe, xo, ye, yo)
    outs = (oxe, oxo, oye, oyo)
    upper = upper_half()
    row8 = lax.broadcasted_iota(jnp.int32, (8, LANES), 0)
    row16 = lax.broadcasted_iota(jnp.int32, (16, LANES), 0)
    power = (row8 == 2) | (row8 == 6)
    sublane = sublanes(LANES)
    even_x, even_y = even_sides()
    groups = s_ref.shape[1] // (GROUP * BLK)
    buses, cross = (GROUP * BLK, from_ref.shape[1] // groups)
    per_list = xe.shape[1] // cross
    count = buses // LANES
    hv_y = far_hv(
        first, bus_ref, partner_ref, all_ref, own_ref[...], hv_pen_ref[...], scaled, sum_ref, hv_weight_ref,
        work_ref, other_ref,
    )

    @pl.loop(0, groups, unroll=2)
    def _(g):
        base = g * buses
        tables = [doubled(s_ref[:, lanes(base + h * LANES)]) for h in range(count)]
        places = list_places(list_ref, g, base)
        sums = [None] * count
        weights = [None] * count
        outputs = []
        for t in range(cross // LANES):
            cols = lanes(g * cross + t * LANES)
            ghost = read_ghost(now, g // per_list, lanes((g % per_list) * cross + t * LANES))
            near = from_ref[0:1, cols] - (base + t * PAIR)
            ends = pick(tables[4 * t : 4 * t + 4], spread8(near), range(4))
            ends = jnp.where(upper, ends, doubled(ghost))
            penalty = 0.25 * lev_ref[0:1, cols].astype(F32)
            if first:
                scaled, target = (None, ends)
            else:
                scaled = yc_old_ref[:, cols] - ends
                target = ends - scaled
            flows = product(kkt_ref, cols, target)
            flows = jnp.where(act_ref[:, cols] == 1, lim_ref[:, cols], flows)
            y = flows if first else flows + scaled
            yc_ref[:, cols] = y
            outputs.append(y)
            high, low = halves(spread8(penalty) * y)
            part = jnp.where(upper, high, pltpu.roll(low, 4, 0))
            tile = spread8(near >> 7)
            left = [jnp.where(tile == h, part, 0.0) for h in range(4)]
            if first:
                left.append(jnp.where(spread8(near >> 7, 16) == row16, spread8(penalty, 16), 0.0))
            out = contract(jnp.concatenate(left, axis=0), one_hot(near, sublane))
            for h in range(4):
                sums[4 * t + h] = out[8 * h : 8 * h + 8]
                if first:
                    weights[4 * t + h] = out[32 + h : 33 + h]

        spot = lanes(g * LANES)
        lefts, rights = ([], [])
        for k, (even, pair) in enumerate(((even_x, 0), (even_x, 1), (even_y, 0), (even_y, 1))):
            start = 0 if k < 2 else 2
            from_even = even if pair == 0 else jnp.logical_not(even)

            def received(parts, rows):
                return jnp.where(from_even, parts[start][rows, spot], parts[start + 1][rows, spot])

            rows = slice(4 * k, 4 * k + 4)
            held = z_ref[rows, spot]
            if first:
                scaled, target = (None, held)
            else:
                scaled = ym_old_ref[rows, spot] - held
                target = held - scaled
            flows = received(now, slice(4, 8))
            for j in range(4):
                flows = flows + received(fixed_parts, slice(8 + 4 * j, 12 + 4 * j)) * spread8(target[j : j + 1], 4)
            penalty = received(fixed_parts, slice(24, 25))
            y = flows if first else flows + scaled
            if first:
                ym_ref[rows, spot] = y
            high, low = halves(spread8(penalty, 4) * y)
            part = jnp.concatenate([high, low], axis=0)
            tile = spread8(places[k] >> 7)
            left = [jnp.where(tile == h, part, 0.0) for h in range(count)]
            if first:
                left.append(jnp.where(spread8(places[k] >> 7, 16) == row16, spread8(penalty, 16), 0.0))
            lefts.append(jnp.concatenate(left, axis=0))
            rights.append(one_hot(places[k], sublane))
        out = contract(jnp.concatenate(lefts[:2], axis=1), jnp.concatenate(rights[:2], axis=1))
        out = out + contract(jnp.concatenate(lefts[2:], axis=1), jnp.concatenate(rights[2:], axis=1))

        fresh = []
        for h in range(count):
            cols = lanes(base + h * LANES)
            total = acc_ref[:, cols] + sums[h] + out[8 * h : 8 * h + 8]
            total = total + pltpu.roll(total, 4, 0)
            total = total + jnp.where(power, spread8(sum_ref[0:1, cols]), 0.0)
            prior = doubled(prior_ref[:, cols])
            total = total + prior * doubled(target_ref[:, cols])
            if first:
                weight = weight_in_ref[0:1, cols] + weights[h] + out[8 * count + h : 8 * count + h + 1]
                weight = spread8(weight) + jnp.where(power, spread8(hv_weight_ref[0:1, cols]), 0.0) + prior
                inverse = 1.0 / weight
                inv_ref[:, cols] = inverse
            else:
                inverse = inv_ref[:, cols]
            state = total * inverse
            new_ref[:, cols] = state
            if not first:
                state_ref[:, cols] = state[:4]
            fresh.append(state)

        picks = list_picks(fresh, places, upper)
        write_ghosts(outs, picks, g)
        if first:
            zn_ref[0:8, spot] = picks[0]
            zn_ref[8:16, spot] = picks[1]
            parts = []
            for t in range(cross // LANES):
                cols = lanes(g * cross + t * LANES)
                near = from_ref[0:1, cols] - (base + t * PAIR)
                ends = pick(fresh[4 * t : 4 * t + 4], spread8(near), range(4))
                target = 2.0 * ends - outputs[t]
                part = product(kkt_ref, cols, jnp.where(upper, target, 0.0))
                parts.append(jnp.where(act_ref[:, cols] == 1, lim_ref[:, cols], part)[4:])
            for ref, here in slots(outs, g // per_list):

                @pl.when(here)
                def _():
                    for t, part in enumerate(parts):
                        ref[4:8, lanes((g % per_list) * cross + t * LANES)] = part

    reached = hv_states(new_ref, bus_ref, work_ref)
    left_over = hv_y - reached
    penalty = hv_pen_ref[...]
    if first:
        hv_scaled_ref[...] = left_over
        hv_own_ref[...] = reached - left_over
        write_hv(hv_ref, reached - left_over, penalty)
    else:
        row = as_row(penalty * left_over, LANES, 0)
        hv_dual_ref[...] = row[:, : hv_dual_ref.shape[1]]


def inner_dual_kernel(s_ref, index_ref, y_ref, lev_ref, dual_ref):
    upper = upper_half()
    groups = s_ref.shape[1] // (GROUP * BLK)
    branches = index_ref.shape[1] // groups
    per_pair = branches // (GROUP // 2)

    @pl.loop(0, groups, unroll=2)
    def _(g):
        for p in range(GROUP // 2):
            base = g * GROUP * BLK + p * PAIR
            tables = [s_ref[:, lanes(base + h * LANES)] for h in range(4)]
            for t in range(per_pair // LANES):
                cols = lanes(g * branches + p * per_pair + t * LANES)
                ends, _, _, _ = inner_ends_of(tables, index_ref, base, cols, t, upper)
                penalty = 0.25 * lev_ref[0:1, cols].astype(F32)
                dual_ref[:, cols] = spread8(penalty) * (y_ref[:, cols] - ends)


def outer_dual_kernel(dual_in_ref, xe, xo, ye, yo, s_ref, from_ref, y_ref, lev_ref, dual_ref):
    upper = upper_half()
    groups = s_ref.shape[1] // (GROUP * BLK)
    cross = from_ref.shape[1] // groups
    per_list = xe.shape[1] // cross

    @pl.loop(0, groups, unroll=2)
    def _(g):
        for t in range(cross // LANES):
            base = g * GROUP * BLK + t * PAIR
            cols = lanes(g * cross + t * LANES)
            ghost = read_ghost((xe, xo, ye, yo), g // per_list, lanes((g % per_list) * cross + t * LANES))
            near = from_ref[0:1, cols] - base
            tables = [s_ref[:, lanes(base + h * LANES)] for h in range(4)]
            ends = pick(tables, spread8(near), range(4))
            ends = jnp.where(upper, ends, doubled(ghost))
            penalty = 0.25 * lev_ref[0:1, cols].astype(F32)
            dual_ref[:, cols] = spread8(penalty) * (y_ref[:, cols] - ends)


def part(rows, width, index=0):
    return pl.BlockSpec((rows, width), lambda g: (0, index))


def scalars():
    return pl.BlockSpec(memory_space=pltpu.SMEM)


def in_place():
    return pl.BlockSpec(memory_space=pl.ANY)


def shape_of(*dims):
    return jax.ShapeDtypeStruct(dims, F32)


def params():
    return pltpu.CompilerParams(
        dimension_semantics=("arbitrary",), vmem_limit_bytes=24 * 1024 * 1024
    )


def cost(flops, moved):
    return pl.CostEstimate(flops=flops, bytes_accessed=moved, transcendentals=0)


def on_device(
    bus_start, bus_target, bus_weight, inner_ends, cross_from, boundary_lists, kkt_map, active_set, limits,
    penalty_level, hv_bus, hv_partner, hv_level,
):
    def hbm(x):
        return pltpu.with_memory_space_constraint(x, pltpu.HBM)

    bus_start, bus_target, bus_weight, inner_ends, boundary_lists, active_set, limits = map(
        hbm, (bus_start, bus_target, bus_weight, inner_ends, boundary_lists, active_set, limits)
    )
    hv_bus, hv_partner, hv_level = map(hbm, (hv_bus, hv_partner, hv_level))
    _, bus_count = bus_start.shape
    list_len = boundary_lists.shape[1] // 4
    inner = inner_ends.shape[1]
    cross = cross_from.shape[0]
    branches = kkt_map.shape[2]
    terms = hv_bus.shape[0]
    devices = lax.axis_size("gx") * lax.axis_size("gy")
    behind = inner // cross
    groups = bus_count // (GROUP * BLK)
    hv_width = max(LANES, 2 * terms)
    kkt = hbm(kkt_map.reshape(64, branches))
    from_row = hbm(cross_from.reshape(1, cross))
    level_row = hbm(penalty_level.reshape(1, branches))
    lists = part(1, 4 * list_len)
    level_in = part(1, inner)
    cross_args = (from_row, kkt, active_set, limits, level_row)
    cross_specs = [part(1, cross), part(64, cross, behind), part(8, cross, behind), part(8, cross, behind), part(1, cross, behind)]
    hv_block = (terms, LANES)
    hv_all_spec = part(devices, hv_width)
    hv_spec = part(*hv_block)
    state_spec, state4_spec, row_spec = (part(8, bus_count), part(4, bus_count), part(1, bus_count))
    held_spec = part(16, list_len)
    common = dict(grid=(1,), compiler_params=params())

    *sent, held, hv_rows, hv_own, hv_pen = pl.pallas_call(
        start_kernel,
        name="first_messages",
        in_specs=[scalars(), scalars(), state4_spec, lists] + cross_specs,
        out_shape=[shape_of(STATIC_ROWS, list_len)] * 4
        + [shape_of(16, list_len), shape_of(devices, hv_width), shape_of(*hv_block), shape_of(*hv_block)],
        out_specs=[part(STATIC_ROWS, list_len)] * 4 + [held_spec, hv_all_spec, hv_spec, hv_spec],
        scratch_shapes=[
            pltpu.VMEM(hv_block, F32),
            pltpu.VMEM((64 * (GROUP // 2), LANES), F32),
        ],
        cost_estimate=cost(10**6, 4 * 10**6),
        **common,
    )(hv_bus, hv_level, bus_start, boundary_lists, *cross_args)

    def exchange(messages):
        xe, xo, ye, yo = messages
        xo = swapped(xo, "gx", 1)
        yo = swapped(yo, "gy", 1)
        xe = swapped(xe, "gx", 0)
        ye = swapped(ye, "gy", 0)
        return (xe, xo, ye, yo)

    def buffers(count):
        kinds = [F32, jnp.int32, F32, F32][:count]
        return (
            [pltpu.VMEM((64 if k == 0 else 8, inner), kind) for k, kind in enumerate(kinds)]
            + [pltpu.VMEM((8, inner), F32)]
            + [pltpu.SemaphoreType.DMA((count, groups)), pltpu.SemaphoreType.DMA((groups,))]
        )

    inner_small = (((2, inner), jnp.int32), ((1, inner), jnp.int32))
    first_got = exchange(sent)
    hv_all = to_all(hv_rows)
    y_inner, sums, weights = pl.pallas_call(
        fetching(functools.partial(inner_kernel, True), {0: 0, 1: 0, 2: 0}),
        name="inner_first",
        in_specs=[in_place()] * 6,
        out_shape=[shape_of(8, inner), shape_of(8, bus_count), shape_of(1, bus_count)],
        out_specs=[in_place(), state_spec, row_spec],
        scratch_shapes=buffers(3) + fetched(((4, bus_count), F32), *inner_small),
        cost_estimate=cost(10**8, 10**7),
        **common,
    )(bus_start, inner_ends, level_row, kkt, active_set, limits)
    message = part(8, list_len)
    state, inverse, *rest = pl.pallas_call(
        functools.partial(outer_kernel, True),
        name="outer_first",
        in_specs=[scalars()] * 2
        + [hv_all_spec, hv_spec, hv_spec]
        + [part(STATIC_ROWS, list_len)] * 4
        + [state_spec, row_spec, state4_spec, lists]
        + cross_specs
        + [held_spec, state4_spec, state4_spec],
        out_shape=[shape_of(8, bus_count), shape_of(8, bus_count)]
        + [shape_of(8, list_len)] * 4
        + [shape_of(8, cross), pltpu.HBM((16, list_len), F32), pltpu.HBM((16, list_len), F32)]
        + [shape_of(devices, hv_width), pltpu.HBM(hv_block, F32), pltpu.HBM(hv_block, F32)],
        out_specs=[state_spec, state_spec]
        + [message] * 4
        + [part(8, cross), held_spec, held_spec]
        + [hv_all_spec, hv_spec, hv_spec],
        scratch_shapes=[pltpu.VMEM((1, bus_count), F32)] * 2 + [pltpu.VMEM(hv_block, F32)] * 2,
        cost_estimate=cost(10**7, 5 * 10**6),
        **common,
    )(
        hv_bus, hv_partner, hv_all, hv_own, hv_pen, *first_got, sums, weights, bus_start, boundary_lists,
        *cross_args, held, bus_target, bus_weight,
    )
    sent, (y_cross, y_mirror, held, hv_rows, hv_scaled, hv_own) = (rest[:4], rest[4:])
    y_mirror, held, hv_scaled, hv_own = map(hbm, (y_mirror, held, hv_scaled, hv_own))

    second_got = exchange(sent)
    hv_all = to_all(hv_rows)
    y_inner, sums = pl.pallas_call(
        fetching(functools.partial(inner_kernel, False), {0: 0, 1: 0, 2: 0}),
        name="inner_second",
        in_specs=[in_place()] * 7,
        out_shape=[shape_of(8, inner), shape_of(8, bus_count)],
        out_specs=[in_place(), state_spec],
        scratch_shapes=buffers(4) + fetched(((8, bus_count), F32), *inner_small),
        cost_estimate=cost(10**8, 10**7),
        **common,
    )(state, inner_ends, level_row, kkt, active_set, limits, y_inner)
    last = part(4, list_len)
    state, bus_state, *rest = pl.pallas_call(
        functools.partial(outer_kernel, False),
        name="outer_second",
        in_specs=[scalars()] * 2
        + [hv_all_spec, hv_spec, hv_spec, hv_spec]
        + [part(STATIC_ROWS, list_len)] * 4
        + [message] * 4
        + [state_spec, state_spec, state_spec, lists]
        + cross_specs
        + [held_spec, part(8, cross), held_spec, state4_spec, state4_spec],
        out_shape=[shape_of(8, bus_count), shape_of(4, bus_count)]
        + [shape_of(4, list_len)] * 4
        + [shape_of(8, cross), shape_of(1, terms)],
        out_specs=[state_spec, state4_spec] + [last] * 4 + [part(8, cross), part(1, terms)],
        scratch_shapes=[pltpu.VMEM((1, bus_count), F32)] + [pltpu.VMEM(hv_block, F32)] * 2,
        cost_estimate=cost(10**7, 5 * 10**6),
        **common,
    )(
        hv_bus, hv_partner, hv_all, hv_own, hv_pen, hv_scaled, *first_got, *second_got, sums, inverse, state,
        boundary_lists, *cross_args, held, y_cross, y_mirror, bus_target, bus_weight,
    )
    sent, (y_cross, hv_dual) = (rest[:4], rest[4:])

    last_got = exchange(sent)
    duals = pl.pallas_call(
        inner_dual_kernel,
        name="inner_duals",
        in_specs=[state_spec, part(2, inner), part(8, inner), level_in],
        out_shape=shape_of(8, branches),
        out_specs=part(8, inner),
        cost_estimate=cost(10**7, 3 * 10**6),
        **common,
    )(state, inner_ends, y_inner, level_row)
    duals = pl.pallas_call(
        outer_dual_kernel,
        name="outer_duals",
        in_specs=[in_place()] + [last] * 4 + [state_spec, part(1, cross), part(8, cross), part(1, cross, behind)],
        out_shape=shape_of(8, branches),
        out_specs=part(8, cross, behind),
        input_output_aliases={0: 0},
        cost_estimate=cost(10**6, 10**6),
        **common,
    )(duals, *last_got, state, from_row, y_cross, level_row)
    return (bus_state, duals, hv_dual.reshape(terms))


def solution(mesh):
    return jax.shard_map(
        on_device,
        mesh=mesh,
        in_specs=(
            P(None, ("gx", "gy")),
            P(None, ("gx", "gy")),
            P(None, ("gx", "gy")),
            P(None, ("gx", "gy")),
            P(("gx", "gy")),
            P(("gx", "gy"), None),
            P(None, None, ("gx", "gy")),
            P(None, ("gx", "gy")),
            P(None, ("gx", "gy")),
            P(("gx", "gy")),
            P(("gx", "gy")),
            P(("gx", "gy")),
            P(("gx", "gy")),
        ),
        out_specs=(P(None, ("gx", "gy")), P(None, ("gx", "gy")), P(("gx", "gy"))),
        check_vma=False,
    )
```

```python
import functools

import jax
import jax.numpy as jnp
from jax import lax
from jax.experimental import pallas as pl
from jax.experimental.pallas import tpu as pltpu
from jax.sharding import PartitionSpec as P

F32 = jnp.float32
BF16 = jnp.bfloat16
BLK = 256
LANES = 128
GROUP = 8
PAIR = 2 * BLK
SPAN = 64
STATIC_ROWS = 25


def swapped(value, axis, first):
    count = lax.axis_size(axis)
    moves = []
    for low in range(first, count - 1, 2):
        moves += [(low, low + 1), (low + 1, low)]
    return lax.ppermute(value, axis, moves)


def to_all(rows):
    return lax.all_to_all(rows, ("gx", "gy"), split_axis=0, concat_axis=0, tiled=True)


def take_lanes(table, lane):
    return lax.gather(
        table,
        lane[..., None],
        lax.GatherDimensionNumbers(
            offset_dims=(),
            collapsed_slice_dims=(1,),
            start_index_map=(1,),
            operand_batching_dims=(0,),
            start_indices_batching_dims=(0,),
        ),
        (1, 1),
        mode=lax.GatherScatterMode.PROMISE_IN_BOUNDS,
    )


def pick(tables, index, tiles):
    lane, tile = (index & (LANES - 1), index >> 7)
    found = None
    for h in tiles:
        got = take_lanes(tables[h], lane)
        found = got if found is None else jnp.where(tile == h, got, found)
    return found


def spread8(row, rows=8):
    return jnp.broadcast_to(row, (rows, row.shape[-1]))


def one_hot(index, sublane):
    length = sublane.shape[0]
    low = spread8(index & (length - 1), 16).astype(F32).astype(BF16)
    column = jnp.concatenate([low] * (length // 16), axis=0)
    return jnp.where(column == sublane, jnp.ones((), BF16), jnp.zeros((), BF16))


def contract(left, right):
    return lax.dot_general(
        left.astype(BF16), right, (((1,), (1,)), ((), ())), preferred_element_type=F32
    )


def halves(values):
    high = values.astype(BF16).astype(F32)
    return high, values - high


def sublanes(length):
    return lax.broadcasted_iota(jnp.int32, (length, LANES), 0).astype(F32).astype(BF16)


def folded(first, second, distance, mask):
    return jnp.where(
        mask,
        first + pltpu.roll(first, 8 - distance, 0),
        second + pltpu.roll(second, distance, 0),
    )


def product(kkt_ref, cols, target):
    row = lax.broadcasted_iota(jnp.int32, (8, LANES), 0)
    terms = [kkt_ref[8 * i : 8 * i + 8, cols] * target for i in range(8)]
    upper = row < 4
    quads = [
        jnp.where(upper, terms[i], terms[i + 4]) + pltpu.roll(jnp.where(upper, terms[i + 4], terms[i]), 4, 0)
        for i in range(4)
    ]
    even_two = (row & 2) == 0
    twos = [folded(quads[i], quads[i + 2], 2, even_two) for i in range(2)]
    return folded(twos[0], twos[1], 1, (row & 1) == 0)


def doubled(block):
    return block if block.shape[0] == 8 else jnp.concatenate([block, block], axis=0)


def tiles_of(states):
    return [states[:, h * LANES : (h + 1) * LANES] for h in range(states.shape[1] // LANES)]


def lanes(start):
    return pl.ds(pl.multiple_of(start, LANES), LANES)


def upper_half():
    return lax.broadcasted_iota(jnp.int32, (8, LANES), 0) < 4


def inner_ends_of(tables, index_ref, base, cols, t, upper):
    near = index_ref[0:1, cols] - base
    far = index_ref[1:2, cols] - base
    tiles = (0, 1) if t < 2 else (2, 3) if t > 2 else (0, 1, 2, 3)
    both = jnp.where(upper, spread8(near), spread8(far))
    return pick(tables, both, tiles), near, far, tiles


def fetching(kernel, spots):
    def wrapped(*refs):
        *refs, sems = refs
        buffers = refs[len(refs) - len(spots) :]
        refs = list(refs[: len(refs) - len(spots)])
        copies = []
        for k, ((place, first), buffer) in enumerate(zip(spots.items(), buffers)):
            source = refs[place].at[:, pl.ds(first, buffer.shape[1])]
            copies.append(pltpu.make_async_copy(source, buffer, sems.at[k]))
            copies[-1].start()
            refs[place] = buffer

        def ready():
            for copy in copies:
                copy.wait()

        kernel(ready, *refs)

    return wrapped


def fetched(*shapes):
    return [pltpu.VMEM(shape, kind) for shape, kind in shapes] + [pltpu.SemaphoreType.DMA((len(shapes),))]


def chunk_copies(sources, buffers, sems, chunk, width):
    spot = pl.ds(pl.multiple_of(chunk * width, LANES), width)
    return [
        pltpu.make_async_copy(source.at[:, spot], buffer.at[:, spot], sems.at[k, chunk])
        for k, (source, buffer) in enumerate(zip(sources, buffers))
    ]


def inner_kernel(first, ready, *refs):
    if first:
        s_ref, index_ref, lev_ref, kkt_hbm, act_hbm, lim_hbm, y_hbm, acc_ref, w_ref, *rest = refs
        kkt_ref, act_ref, lim_ref, y_ref, sems, out_sems = rest
        sources, buffers = ((kkt_hbm, act_hbm, lim_hbm), (kkt_ref, act_ref, lim_ref))
        old_ref = None
    else:
        s_ref, index_ref, lev_ref, kkt_hbm, act_hbm, lim_hbm, old_hbm, y_hbm, acc_ref, *rest = refs
        kkt_ref, act_ref, lim_ref, old_ref, y_ref, sems, out_sems = rest
        sources, buffers = ((kkt_hbm, act_hbm, lim_hbm, old_hbm), (kkt_ref, act_ref, lim_ref, old_ref))
        w_ref = None
    upper = upper_half()
    row16 = lax.broadcasted_iota(jnp.int32, (16, LANES), 0)
    sublane = sublanes(SPAN)
    bus_count = s_ref.shape[1]
    inner = index_ref.shape[1]
    groups = bus_count // (GROUP * BLK)
    buses, branches = (bus_count // groups, inner // groups)
    per_pair = branches // (GROUP // 2)

    @pl.loop(0, groups)
    def _(g):
        for copy in chunk_copies(sources, buffers, sems, g, branches):
            copy.start()

    ready()

    def group(g):
        for p in range(GROUP // 2):
            base = g * buses + p * PAIR
            tables = [doubled(s_ref[:, lanes(base + h * LANES)]) for h in range(4)]
            sums = [jnp.zeros((8, SPAN), F32)] * (PAIR // SPAN)
            weights = jnp.zeros((16, SPAN), F32)
            jobs = []
            for t in range(per_pair // LANES):
                cols = lanes(g * branches + p * per_pair + t * LANES)
                ends, near, far, tiles = inner_ends_of(tables, index_ref, base, cols, t, upper)
                penalty = 0.25 * lev_ref[0:1, cols].astype(F32)
                if first:
                    scaled, target = (None, ends)
                else:
                    scaled = old_ref[:, cols] - ends
                    target = ends - scaled
                flows = product(kkt_ref, cols, target)
                flows = jnp.where(act_ref[:, cols] == 1, lim_ref[:, cols], flows)
                y = flows if first else flows + scaled
                y_ref[:, cols] = y
                high, low = halves(spread8(penalty) * y)
                from_part = jnp.where(upper, high, pltpu.roll(low, 4, 0))
                to_part = jnp.where(upper, pltpu.roll(high, 4, 0), low)
                near_span, far_span = (near >> 6, far >> 6)
                near_tile, far_tile = (spread8(near_span), spread8(far_span))
                spans = [2 * h + half for h in tiles for half in range(2)]
                left = [
                    jnp.concatenate(
                        [
                            jnp.where(near_tile == h, from_part, 0.0),
                            jnp.where(far_tile == h, to_part, 0.0),
                        ],
                        axis=1,
                    )
                    for h in spans
                ]
                if first:
                    level = spread8(penalty, 16)
                    left.append(
                        jnp.concatenate(
                            [
                                jnp.where(spread8(near_span, 16) == row16, level, 0.0),
                                jnp.where(spread8(far_span, 16) == row16, level, 0.0),
                            ],
                            axis=1,
                        )
                    )
                right = jnp.concatenate([one_hot(near, sublane), one_hot(far, sublane)], axis=1)
                jobs.append((jnp.concatenate(left, axis=0).astype(BF16), right, spans))
            for left, right, spans in jobs:
                out = contract(left, right)
                for place, h in enumerate(spans):
                    sums[h] = sums[h] + out[8 * place : 8 * place + 8]
                if first:
                    weights = weights + out[8 * len(spans) :]
            for h in range(4):
                spot = lanes(base + h * LANES)
                acc_ref[:, spot] = jnp.concatenate([sums[2 * h], sums[2 * h + 1]], axis=1)
                if first:
                    w_ref[0:1, spot] = jnp.concatenate(
                        [weights[2 * h : 2 * h + 1], weights[2 * h + 1 : 2 * h + 2]], axis=1
                    )

    def out_copy(g):
        spot = pl.ds(pl.multiple_of(g * branches, LANES), branches)
        return pltpu.make_async_copy(y_ref.at[:, spot], y_hbm.at[:, spot], out_sems.at[g])

    @pl.loop(0, groups, step=2)
    def _(start):
        for g in range(2):
            for copy in chunk_copies(sources, buffers, sems, start + g, branches):
                copy.wait()
        for g in range(2):
            group(start + g)
        for g in range(2):
            out_copy(start + g).start()

    @pl.loop(0, groups)
    def _(g):
        out_copy(g).wait()


def list_places(list_ref, g, base):
    count = list_ref.shape[1] // 4
    return [list_ref[0:1, lanes(k * count + g * LANES)] - base for k in range(4)]


def list_picks(tables, places, upper):
    picks = []
    for k in (0, 2):
        both = jnp.where(upper, spread8(places[k]), spread8(places[k + 1]))
        picks.append(pick(tables, both, range(len(tables))))
    return picks


def even_sides():
    return lax.axis_index("gx") % 2 == 0, lax.axis_index("gy") % 2 == 0


def write_blocks(outs, kept, rows):
    even_x, even_y = even_sides()
    count = outs[0].shape[1]

    def block(k):
        return kept[rows, k * count : (k + 1) * count]

    for out, even, at_even, at_odd in (
        (outs[0], even_x, 1, 0),
        (outs[1], even_x, 0, 1),
        (outs[2], even_y, 3, 2),
        (outs[3], even_y, 2, 3),
    ):
        out[rows, :] = jnp.where(even, block(at_even), block(at_odd))


def write_ghosts(outs, picks, g):
    even_x, even_y = even_sides()
    spot = lanes(g * LANES)
    for out_even, out_odd, even, both in (
        (outs[0], outs[1], even_x, picks[0]),
        (outs[2], outs[3], even_y, picks[1]),
    ):
        out_even[0:4, spot] = jnp.where(even, both[:4], both[4:])
        out_odd[0:4, spot] = jnp.where(even, both[4:], both[:4])


def read_ghost(got, block, spot):
    even_x, even_y = even_sides()
    by_even = jnp.where(even_x, block == 1, block == 0) | jnp.where(even_y, block == 3, block == 2)
    return jnp.where(
        block < 2,
        jnp.where(by_even, got[0][0:4, spot], got[1][0:4, spot]),
        jnp.where(by_even, got[2][0:4, spot], got[3][0:4, spot]),
    )


def hv_states(s_ref, hv_bus_ref, work_ref):
    lane = lax.broadcasted_iota(jnp.int32, (1, LANES), 1)

    def body(t, carry):
        bus = hv_bus_ref[t]
        row = s_ref[2:3, lanes((bus >> 7) * LANES)]
        work_ref[pl.ds(t, 1), :] = jnp.where(lane == (bus & (LANES - 1)), row, 0.0)
        return carry

    lax.fori_loop(0, work_ref.shape[0], body, 0, unroll=8)
    return jnp.broadcast_to(jnp.sum(work_ref[...], axis=1, keepdims=True), work_ref.shape)


def as_row(values, width, offset):
    count = values.shape[0]
    wide = jnp.broadcast_to(values[:, :1], (count, width))
    lane = lax.broadcasted_iota(jnp.int32, (count, width), 1)
    own = lax.broadcasted_iota(jnp.int32, (count, width), 0)
    return jnp.sum(jnp.where(lane == own + offset, wide, 0.0), axis=0, keepdims=True)


def write_hv(out_ref, values, penalties):
    width = out_ref.shape[-1]
    row = as_row(values, width, 0) + as_row(penalties, width, values.shape[0])
    out_ref[...] = jnp.broadcast_to(row, out_ref.shape)


def start_kernel(
    bus_ref, level_ref, s_ref, list_ref, from_ref, kkt_ref, act_ref, lim_ref, lev_ref,
    xe_ref, xo_ref, ye_ref, yo_ref, z_ref, hv_ref, hv_own_ref, hv_pen_ref, work_ref, turn_ref, kept_ref,
):
    outs = (xe_ref, xo_ref, ye_ref, yo_ref)
    upper = upper_half()
    values = hv_states(s_ref, bus_ref, work_ref)
    hv_own_ref[...] = values

    def body(t, carry):
        hv_pen_ref[pl.ds(t, 1), :] = jnp.full((1, LANES), level_ref[t], jnp.int32).astype(F32) * 0.25
        return carry

    lax.fori_loop(0, hv_pen_ref.shape[0], body, 0, unroll=8)
    write_hv(hv_ref, values, hv_pen_ref[...])
    groups = s_ref.shape[1] // (GROUP * BLK)
    buses, cross = (GROUP * BLK, from_ref.shape[1] // groups)

    @pl.loop(0, groups, unroll=2)
    def _(g):
        base = g * buses
        tables = [doubled(s_ref[:, lanes(base + h * LANES)]) for h in range(buses // LANES)]
        picks = list_picks(tables, list_places(list_ref, g, base), upper)
        z_ref[0:8, lanes(g * LANES)] = picks[0]
        z_ref[8:16, lanes(g * LANES)] = picks[1]
        write_ghosts(outs, picks, g)
        for t in range(cross // LANES):
            cols = lanes(g * cross + t * LANES)
            index = spread8(from_ref[0:1, cols] - (base + t * PAIR))
            ends = pick(tables[4 * t : 4 * t + 4], index, range(4))
            fixed = act_ref[:, cols] == 1
            part = jnp.where(fixed, lim_ref[:, cols], product(kkt_ref, cols, jnp.where(upper, ends, 0.0)))
            for i in range(8):
                turn_ref[64 * t + 8 * i : 64 * t + 8 * i + 8, :] = kkt_ref[8 * i : 8 * i + 8, cols]
            block = [
                jnp.where(fixed, 0.0, turn_ref[pl.ds(64 * t + 4 + j, 8, stride=8), :])[4:] for j in range(4)
            ]
            kept_ref[0:8, cols] = part
            for j in range(4):
                kept_ref[8 + 4 * j : 12 + 4 * j, cols] = block[j]
            kept_ref[24:25, cols] = 0.25 * lev_ref[0:1, cols].astype(F32)

    for rows in (slice(4, 8), slice(8, 24), slice(24, 25)):
        write_blocks(outs, kept_ref, rows)


def far_hv(first, bus_ref, partner_ref, all_ref, own, penalty, scaled, sum_ref, weight_ref, work_ref, other_ref):
    count = work_ref.shape[0]
    width = all_ref.shape[-1]
    lane = lax.broadcasted_iota(jnp.int32, (1, LANES), 1)
    wide = lax.broadcasted_iota(jnp.int32, (1, width), 1)

    def narrow(row):
        return functools.reduce(jnp.add, [row[:, k : k + LANES] for k in range(0, width, LANES)])

    def fetch(t, carry):
        partner = partner_ref[t]
        device, place = (partner // count, partner % count)
        row = all_ref[pl.ds(device, 1), :]
        work_ref[pl.ds(t, 1), :] = narrow(jnp.where(wide == place, row, 0.0))
        other_ref[pl.ds(t, 1), :] = narrow(jnp.where(wide == place + count, row, 0.0))
        return carry

    lax.fori_loop(0, count, fetch, 0, unroll=8)
    far_value = jnp.sum(work_ref[...], axis=1, keepdims=True)
    far_penalty = jnp.sum(other_ref[...], axis=1, keepdims=True)
    flow = (penalty * own - far_penalty * far_value) / (penalty + far_penalty)
    y = flow if first else flow + scaled
    work_ref[...] = penalty * y
    other_ref[...] = penalty
    sum_ref[...] = jnp.zeros_like(sum_ref)
    if first:
        weight_ref[...] = jnp.zeros_like(weight_ref)

    def place_terms(t, carry):
        bus = bus_ref[t]
        spot = lanes((bus >> 7) * LANES)
        here = lane == (bus & (LANES - 1))
        sum_ref[0:1, spot] += jnp.where(here, work_ref[pl.ds(t, 1), :], 0.0)
        if first:
            weight_ref[0:1, spot] += jnp.where(here, other_ref[pl.ds(t, 1), :], 0.0)
        return carry

    lax.fori_loop(0, count, place_terms, 0, unroll=8)
    return y


def outer_kernel(first, *refs):
    if first:
        (
            bus_ref, partner_ref, all_ref, own_ref, hv_pen_ref, xe, xo, ye, yo, acc_ref, weight_in_ref,
            s_ref, list_ref, from_ref, kkt_ref, act_ref, lim_ref, lev_ref, z_ref, target_ref, prior_ref,
            new_ref, inv_ref, oxe, oxo, oye, oyo, yc_ref, ym_ref, zn_ref, hv_ref, hv_scaled_ref, hv_own_ref,
            sum_ref, hv_weight_ref, work_ref, other_ref, kept_ref,
        ) = refs
        now = (xe, xo, ye, yo)
        scaled = None
    else:
        (
            bus_ref, partner_ref, all_ref, own_ref, hv_pen_ref, scaled_ref, xe, xo, ye, yo, nxe, nxo, nye, nyo,
            acc_ref, inv_ref, s_ref, list_ref, from_ref, kkt_ref, act_ref, lim_ref, lev_ref, z_ref, yc_old_ref,
            ym_old_ref, target_ref, prior_ref,
            new_ref, state_ref, oxe, oxo, oye, oyo, yc_ref, hv_dual_ref,
            sum_ref, work_ref, other_ref,
        ) = refs
        now = (nxe, nxo, nye, nyo)
        hv_weight_ref = None
        scaled = scaled_ref[...]
    fixed_parts = (xe, xo, ye, yo)
    outs = (oxe, oxo, oye, oyo)
    upper = upper_half()
    row8 = lax.broadcasted_iota(jnp.int32, (8, LANES), 0)
    row16 = lax.broadcasted_iota(jnp.int32, (16, LANES), 0)
    power = (row8 == 2) | (row8 == 6)
    sublane = sublanes(LANES)
    even_x, even_y = even_sides()
    groups = s_ref.shape[1] // (GROUP * BLK)
    buses, cross = (GROUP * BLK, from_ref.shape[1] // groups)
    per_list = xe.shape[1] // cross
    count = buses // LANES
    hv_y = far_hv(
        first, bus_ref, partner_ref, all_ref, own_ref[...], hv_pen_ref[...], scaled, sum_ref, hv_weight_ref,
        work_ref, other_ref,
    )

    @pl.loop(0, groups, unroll=4)
    def _(g):
        base = g * buses
        tables = [doubled(s_ref[:, lanes(base + h * LANES)]) for h in range(count)]
        places = list_places(list_ref, g, base)
        sums = [None] * count
        weights = [None] * count
        outputs = []
        for t in range(cross // LANES):
            cols = lanes(g * cross + t * LANES)
            ghost = read_ghost(now, g // per_list, lanes((g % per_list) * cross + t * LANES))
            near = from_ref[0:1, cols] - (base + t * PAIR)
            ends = pick(tables[4 * t : 4 * t + 4], spread8(near), range(4))
            ends = jnp.where(upper, ends, doubled(ghost))
            penalty = 0.25 * lev_ref[0:1, cols].astype(F32)
            if first:
                scaled, target = (None, ends)
            else:
                scaled = yc_old_ref[:, cols] - ends
                target = ends - scaled
            flows = product(kkt_ref, cols, target)
            flows = jnp.where(act_ref[:, cols] == 1, lim_ref[:, cols], flows)
            y = flows if first else flows + scaled
            yc_ref[:, cols] = y
            outputs.append(y)
            high, low = halves(spread8(penalty) * y)
            part = jnp.where(upper, high, pltpu.roll(low, 4, 0))
            tile = spread8(near >> 7)
            left = [jnp.where(tile == h, part, 0.0) for h in range(4)]
            if first:
                left.append(jnp.where(spread8(near >> 7, 16) == row16, spread8(penalty, 16), 0.0))
            out = contract(jnp.concatenate(left, axis=0), one_hot(near, sublane))
            for h in range(4):
                sums[4 * t + h] = out[8 * h : 8 * h + 8]
                if first:
                    weights[4 * t + h] = out[32 + h : 33 + h]

        spot = lanes(g * LANES)
        lefts, rights = ([], [])
        for k, (even, pair) in enumerate(((even_x, 0), (even_x, 1), (even_y, 0), (even_y, 1))):
            start = 0 if k < 2 else 2
            from_even = even if pair == 0 else jnp.logical_not(even)

            def received(parts, rows):
                return jnp.where(from_even, parts[start][rows, spot], parts[start + 1][rows, spot])

            rows = slice(4 * k, 4 * k + 4)
            held = z_ref[rows, spot]
            if first:
                scaled, target = (None, held)
            else:
                scaled = ym_old_ref[rows, spot] - held
                target = held - scaled
            flows = received(now, slice(4, 8))
            for j in range(4):
                flows = flows + received(fixed_parts, slice(8 + 4 * j, 12 + 4 * j)) * spread8(target[j : j + 1], 4)
            penalty = received(fixed_parts, slice(24, 25))
            y = flows if first else flows + scaled
            if first:
                ym_ref[rows, spot] = y
            high, low = halves(spread8(penalty, 4) * y)
            part = jnp.concatenate([high, low], axis=0)
            tile = spread8(places[k] >> 7)
            left = [jnp.where(tile == h, part, 0.0) for h in range(count)]
            if first:
                left.append(jnp.where(spread8(places[k] >> 7, 16) == row16, spread8(penalty, 16), 0.0))
            lefts.append(jnp.concatenate(left, axis=0))
            rights.append(one_hot(places[k], sublane))
        out = contract(jnp.concatenate(lefts[:2], axis=1), jnp.concatenate(rights[:2], axis=1))
        out = out + contract(jnp.concatenate(lefts[2:], axis=1), jnp.concatenate(rights[2:], axis=1))

        fresh = []
        for h in range(count):
            cols = lanes(base + h * LANES)
            total = acc_ref[:, cols] + sums[h] + out[8 * h : 8 * h + 8]
            total = total + pltpu.roll(total, 4, 0)
            total = total + jnp.where(power, spread8(sum_ref[0:1, cols]), 0.0)
            prior = doubled(prior_ref[:, cols])
            total = total + prior * doubled(target_ref[:, cols])
            if first:
                weight = weight_in_ref[0:1, cols] + weights[h] + out[8 * count + h : 8 * count + h + 1]
                weight = spread8(weight) + jnp.where(power, spread8(hv_weight_ref[0:1, cols]), 0.0) + prior
                inverse = 1.0 / weight
                inv_ref[:, cols] = inverse
            else:
                inverse = inv_ref[:, cols]
            state = total * inverse
            new_ref[:, cols] = state
            if not first:
                state_ref[:, cols] = state[:4]
            fresh.append(state)

        picks = list_picks(fresh, places, upper)
        write_ghosts(outs, picks, g)
        if first:
            zn_ref[0:8, spot] = picks[0]
            zn_ref[8:16, spot] = picks[1]
            for t in range(cross // LANES):
                cols = lanes(g * cross + t * LANES)
                near = from_ref[0:1, cols] - (base + t * PAIR)
                ends = pick(fresh[4 * t : 4 * t + 4], spread8(near), range(4))
                target = 2.0 * ends - outputs[t]
                part = product(kkt_ref, cols, jnp.where(upper, target, 0.0))
                kept_ref[:, cols] = jnp.where(act_ref[:, cols] == 1, lim_ref[:, cols], part)

    if first:
        write_blocks(outs, kept_ref, slice(4, 8))
    reached = hv_states(new_ref, bus_ref, work_ref)
    left_over = hv_y - reached
    penalty = hv_pen_ref[...]
    if first:
        hv_scaled_ref[...] = left_over
        hv_own_ref[...] = reached - left_over
        write_hv(hv_ref, reached - left_over, penalty)
    else:
        row = as_row(penalty * left_over, LANES, 0)
        hv_dual_ref[...] = row[:, : hv_dual_ref.shape[1]]


def inner_dual_kernel(s_ref, index_ref, y_ref, lev_ref, dual_ref):
    upper = upper_half()
    groups = s_ref.shape[1] // (GROUP * BLK)
    branches = index_ref.shape[1] // groups
    per_pair = branches // (GROUP // 2)

    @pl.loop(0, groups, unroll=4)
    def _(g):
        for p in range(GROUP // 2):
            base = g * GROUP * BLK + p * PAIR
            tables = [s_ref[:, lanes(base + h * LANES)] for h in range(4)]
            for t in range(per_pair // LANES):
                cols = lanes(g * branches + p * per_pair + t * LANES)
                ends, _, _, _ = inner_ends_of(tables, index_ref, base, cols, t, upper)
                penalty = 0.25 * lev_ref[0:1, cols].astype(F32)
                dual_ref[:, cols] = spread8(penalty) * (y_ref[:, cols] - ends)


def outer_dual_kernel(dual_in_ref, xe, xo, ye, yo, s_ref, from_ref, y_ref, lev_ref, dual_ref):
    upper = upper_half()
    groups = s_ref.shape[1] // (GROUP * BLK)
    cross = from_ref.shape[1] // groups
    per_list = xe.shape[1] // cross

    @pl.loop(0, groups, unroll=8)
    def _(g):
        for t in range(cross // LANES):
            base = g * GROUP * BLK + t * PAIR
            cols = lanes(g * cross + t * LANES)
            ghost = read_ghost((xe, xo, ye, yo), g // per_list, lanes((g % per_list) * cross + t * LANES))
            near = from_ref[0:1, cols] - base
            tables = [s_ref[:, lanes(base + h * LANES)] for h in range(4)]
            ends = pick(tables, spread8(near), range(4))
            ends = jnp.where(upper, ends, doubled(ghost))
            penalty = 0.25 * lev_ref[0:1, cols].astype(F32)
            dual_ref[:, cols] = spread8(penalty) * (y_ref[:, cols] - ends)


def part(rows, width, index=0):
    return pl.BlockSpec((rows, width), lambda g: (0, index))


def scalars():
    return pl.BlockSpec(memory_space=pltpu.SMEM)


def in_place():
    return pl.BlockSpec(memory_space=pl.ANY)


def shape_of(*dims):
    return jax.ShapeDtypeStruct(dims, F32)


def params():
    return pltpu.CompilerParams(
        dimension_semantics=("arbitrary",), vmem_limit_bytes=24 * 1024 * 1024
    )


def cost(flops, moved):
    return pl.CostEstimate(flops=flops, bytes_accessed=moved, transcendentals=0)


def on_device(
    bus_start, bus_target, bus_weight, inner_ends, cross_from, boundary_lists, kkt_map, active_set, limits,
    penalty_level, hv_bus, hv_partner, hv_level,
):
    def hbm(x):
        return pltpu.with_memory_space_constraint(x, pltpu.HBM)

    bus_start, bus_target, bus_weight, inner_ends, boundary_lists, active_set, limits = map(
        hbm, (bus_start, bus_target, bus_weight, inner_ends, boundary_lists, active_set, limits)
    )
    hv_bus, hv_partner, hv_level = map(hbm, (hv_bus, hv_partner, hv_level))
    _, bus_count = bus_start.shape
    list_len = boundary_lists.shape[1] // 4
    inner = inner_ends.shape[1]
    cross = cross_from.shape[0]
    branches = kkt_map.shape[2]
    terms = hv_bus.shape[0]
    devices = lax.axis_size("gx") * lax.axis_size("gy")
    behind = inner // cross
    groups = bus_count // (GROUP * BLK)
    hv_width = max(LANES, 2 * terms)
    kkt = hbm(kkt_map.reshape(64, branches))
    from_row = hbm(cross_from.reshape(1, cross))
    level_row = hbm(penalty_level.reshape(1, branches))
    lists = part(1, 4 * list_len)
    level_in = part(1, inner)
    cross_args = (from_row, kkt, active_set, limits, level_row)
    cross_specs = [part(1, cross), part(64, cross, behind), part(8, cross, behind), part(8, cross, behind), part(1, cross, behind)]
    hv_block = (terms, LANES)
    hv_all_spec = part(devices, hv_width)
    hv_spec = part(*hv_block)
    state_spec, state4_spec, row_spec = (part(8, bus_count), part(4, bus_count), part(1, bus_count))
    held_spec = part(16, list_len)
    common = dict(grid=(1,), compiler_params=params())

    *sent, held, hv_rows, hv_own, hv_pen = pl.pallas_call(
        start_kernel,
        name="first_messages",
        in_specs=[scalars(), scalars(), state4_spec, lists] + cross_specs,
        out_shape=[shape_of(STATIC_ROWS, list_len)] * 4
        + [shape_of(16, list_len), shape_of(devices, hv_width), shape_of(*hv_block), shape_of(*hv_block)],
        out_specs=[part(STATIC_ROWS, list_len)] * 4 + [held_spec, hv_all_spec, hv_spec, hv_spec],
        scratch_shapes=[
            pltpu.VMEM(hv_block, F32),
            pltpu.VMEM((64 * (GROUP // 2), LANES), F32),
            pltpu.VMEM((STATIC_ROWS, cross), F32),
        ],
        cost_estimate=cost(10**6, 4 * 10**6),
        **common,
    )(hv_bus, hv_level, bus_start, boundary_lists, *cross_args)

    def exchange(messages):
        xe, xo, ye, yo = messages
        xo = swapped(xo, "gx", 1)
        yo = swapped(yo, "gy", 1)
        xe = swapped(xe, "gx", 0)
        ye = swapped(ye, "gy", 0)
        return (xe, xo, ye, yo)

    def buffers(count):
        kinds = [F32, jnp.int32, F32, F32][:count]
        return (
            [pltpu.VMEM((64 if k == 0 else 8, inner), kind) for k, kind in enumerate(kinds)]
            + [pltpu.VMEM((8, inner), F32)]
            + [pltpu.SemaphoreType.DMA((count, groups)), pltpu.SemaphoreType.DMA((groups,))]
        )

    inner_small = (((2, inner), jnp.int32), ((1, inner), jnp.int32))
    first_got = exchange(sent)
    hv_all = to_all(hv_rows)
    y_inner, sums, weights = pl.pallas_call(
        fetching(functools.partial(inner_kernel, True), {0: 0, 1: 0, 2: 0}),
        name="inner_first",
        in_specs=[in_place()] * 6,
        out_shape=[shape_of(8, inner), shape_of(8, bus_count), shape_of(1, bus_count)],
        out_specs=[in_place(), state_spec, row_spec],
        scratch_shapes=buffers(3) + fetched(((4, bus_count), F32), *inner_small),
        cost_estimate=cost(10**8, 10**7),
        **common,
    )(bus_start, inner_ends, level_row, kkt, active_set, limits)
    message = part(8, list_len)
    state, inverse, *rest = pl.pallas_call(
        functools.partial(outer_kernel, True),
        name="outer_first",
        in_specs=[scalars()] * 2
        + [hv_all_spec, hv_spec, hv_spec]
        + [part(STATIC_ROWS, list_len)] * 4
        + [state_spec, row_spec, state4_spec, lists]
        + cross_specs
        + [held_spec, state4_spec, state4_spec],
        out_shape=[shape_of(8, bus_count), shape_of(8, bus_count)]
        + [shape_of(8, list_len)] * 4
        + [shape_of(8, cross), pltpu.HBM((16, list_len), F32), pltpu.HBM((16, list_len), F32)]
        + [shape_of(devices, hv_width), pltpu.HBM(hv_block, F32), pltpu.HBM(hv_block, F32)],
        out_specs=[state_spec, state_spec]
        + [message] * 4
        + [part(8, cross), held_spec, held_spec]
        + [hv_all_spec, hv_spec, hv_spec],
        scratch_shapes=[pltpu.VMEM((1, bus_count), F32)] * 2 + [pltpu.VMEM(hv_block, F32)] * 2 + [pltpu.VMEM((8, cross), F32)],
        cost_estimate=cost(10**7, 5 * 10**6),
        **common,
    )(
        hv_bus, hv_partner, hv_all, hv_own, hv_pen, *first_got, sums, weights, bus_start, boundary_lists,
        *cross_args, held, bus_target, bus_weight,
    )
    sent, (y_cross, y_mirror, held, hv_rows, hv_scaled, hv_own) = (rest[:4], rest[4:])
    y_mirror, held, hv_scaled, hv_own = map(hbm, (y_mirror, held, hv_scaled, hv_own))

    second_got = exchange(sent)
    hv_all = to_all(hv_rows)
    y_inner, sums = pl.pallas_call(
        fetching(functools.partial(inner_kernel, False), {0: 0, 1: 0, 2: 0}),
        name="inner_second",
        in_specs=[in_place()] * 7,
        out_shape=[shape_of(8, inner), shape_of(8, bus_count)],
        out_specs=[in_place(), state_spec],
        scratch_shapes=buffers(4) + fetched(((8, bus_count), F32), *inner_small),
        cost_estimate=cost(10**8, 10**7),
        **common,
    )(state, inner_ends, level_row, kkt, active_set, limits, y_inner)
    last = part(4, list_len)
    state, bus_state, *rest = pl.pallas_call(
        functools.partial(outer_kernel, False),
        name="outer_second",
        in_specs=[scalars()] * 2
        + [hv_all_spec, hv_spec, hv_spec, hv_spec]
        + [part(STATIC_ROWS, list_len)] * 4
        + [message] * 4
        + [state_spec, state_spec, state_spec, lists]
        + cross_specs
        + [held_spec, part(8, cross), held_spec, state4_spec, state4_spec],
        out_shape=[shape_of(8, bus_count), shape_of(4, bus_count)]
        + [shape_of(4, list_len)] * 4
        + [shape_of(8, cross), shape_of(1, terms)],
        out_specs=[state_spec, state4_spec] + [last] * 4 + [part(8, cross), part(1, terms)],
        scratch_shapes=[pltpu.VMEM((1, bus_count), F32)] + [pltpu.VMEM(hv_block, F32)] * 2,
        cost_estimate=cost(10**7, 5 * 10**6),
        **common,
    )(
        hv_bus, hv_partner, hv_all, hv_own, hv_pen, hv_scaled, *first_got, *second_got, sums, inverse, state,
        boundary_lists, *cross_args, held, y_cross, y_mirror, bus_target, bus_weight,
    )
    sent, (y_cross, hv_dual) = (rest[:4], rest[4:])

    last_got = exchange(sent)
    duals = pl.pallas_call(
        inner_dual_kernel,
        name="inner_duals",
        in_specs=[state_spec, part(2, inner), part(8, inner), level_in],
        out_shape=shape_of(8, branches),
        out_specs=part(8, inner),
        cost_estimate=cost(10**7, 3 * 10**6),
        **common,
    )(state, inner_ends, y_inner, level_row)
    duals = pl.pallas_call(
        outer_dual_kernel,
        name="outer_duals",
        in_specs=[in_place()] + [last] * 4 + [state_spec, part(1, cross), part(8, cross), part(1, cross, behind)],
        out_shape=shape_of(8, branches),
        out_specs=part(8, cross, behind),
        input_output_aliases={0: 0},
        cost_estimate=cost(10**6, 10**6),
        **common,
    )(duals, *last_got, state, from_row, y_cross, level_row)
    return (bus_state, duals, hv_dual.reshape(terms))


def solution(mesh):
    return jax.shard_map(
        on_device,
        mesh=mesh,
        in_specs=(
            P(None, ("gx", "gy")),
            P(None, ("gx", "gy")),
            P(None, ("gx", "gy")),
            P(None, ("gx", "gy")),
            P(("gx", "gy")),
            P(("gx", "gy"), None),
            P(None, None, ("gx", "gy")),
            P(None, ("gx", "gy")),
            P(None, ("gx", "gy")),
            P(("gx", "gy")),
            P(("gx", "gy")),
            P(("gx", "gy")),
            P(("gx", "gy")),
        ),
        out_specs=(P(None, ("gx", "gy")), P(None, ("gx", "gy")), P(("gx", "gy"))),
        check_vma=False,
    )
```

```python
import functools

import jax
import jax.numpy as jnp
from jax import lax
from jax.experimental import pallas as pl
from jax.experimental.pallas import tpu as pltpu
from jax.sharding import PartitionSpec as P

F32 = jnp.float32
BF16 = jnp.bfloat16
BLK = 256
LANES = 128
GROUP = 8
PAIR = 2 * BLK
SPAN = 64
STATIC_ROWS = 25


def swapped(value, axis, first):
    count = lax.axis_size(axis)
    moves = []
    for low in range(first, count - 1, 2):
        moves += [(low, low + 1), (low + 1, low)]
    return lax.ppermute(value, axis, moves)


def to_all(rows):
    return lax.all_to_all(rows, ("gx", "gy"), split_axis=0, concat_axis=0, tiled=True)


def take_lanes(table, lane):
    return lax.gather(
        table,
        lane[..., None],
        lax.GatherDimensionNumbers(
            offset_dims=(),
            collapsed_slice_dims=(1,),
            start_index_map=(1,),
            operand_batching_dims=(0,),
            start_indices_batching_dims=(0,),
        ),
        (1, 1),
        mode=lax.GatherScatterMode.PROMISE_IN_BOUNDS,
    )


def pick(tables, index, tiles):
    lane, tile = (index & (LANES - 1), index >> 7)
    found = None
    for h in tiles:
        got = take_lanes(tables[h], lane)
        found = got if found is None else jnp.where(tile == h, got, found)
    return found


def spread8(row, rows=8):
    return jnp.broadcast_to(row, (rows, row.shape[-1]))


def one_hot(index, sublane):
    length = sublane.shape[0]
    low = spread8(index & (length - 1), 16).astype(F32).astype(BF16)
    column = jnp.concatenate([low] * (length // 16), axis=0)
    return jnp.where(column == sublane, jnp.ones((), BF16), jnp.zeros((), BF16))


def contract(left, right):
    return lax.dot_general(
        left.astype(BF16), right, (((1,), (1,)), ((), ())), preferred_element_type=F32
    )


def halves(values):
    high = values.astype(BF16).astype(F32)
    return high, values - high


def sublanes(length):
    return lax.broadcasted_iota(jnp.int32, (length, LANES), 0).astype(F32).astype(BF16)


def folded(first, second, distance, mask):
    return jnp.where(
        mask,
        first + pltpu.roll(first, 8 - distance, 0),
        second + pltpu.roll(second, distance, 0),
    )


def product(kkt_ref, cols, target):
    row = lax.broadcasted_iota(jnp.int32, (8, LANES), 0)
    terms = [kkt_ref[8 * i : 8 * i + 8, cols] * target for i in range(8)]
    upper = row < 4
    quads = [
        jnp.where(upper, terms[i], terms[i + 4]) + pltpu.roll(jnp.where(upper, terms[i + 4], terms[i]), 4, 0)
        for i in range(4)
    ]
    even_two = (row & 2) == 0
    twos = [folded(quads[i], quads[i + 2], 2, even_two) for i in range(2)]
    return folded(twos[0], twos[1], 1, (row & 1) == 0)


def doubled(block):
    return block if block.shape[0] == 8 else jnp.concatenate([block, block], axis=0)


def tiles_of(states):
    return [states[:, h * LANES : (h + 1) * LANES] for h in range(states.shape[1] // LANES)]


def lanes(start):
    return pl.ds(pl.multiple_of(start, LANES), LANES)


def upper_half():
    return lax.broadcasted_iota(jnp.int32, (8, LANES), 0) < 4


def inner_ends_of(tables, index_ref, base, cols, t, upper):
    near = index_ref[0:1, cols] - base
    far = index_ref[1:2, cols] - base
    tiles = (0, 1) if t < 2 else (2, 3) if t > 2 else (0, 1, 2, 3)
    both = jnp.where(upper, spread8(near), spread8(far))
    return pick(tables, both, tiles), near, far, tiles


def fetching(kernel, spots):
    def wrapped(*refs):
        *refs, sems = refs
        buffers = refs[len(refs) - len(spots) :]
        refs = list(refs[: len(refs) - len(spots)])
        copies = []
        for k, ((place, first), buffer) in enumerate(zip(spots.items(), buffers)):
            source = refs[place].at[:, pl.ds(first, buffer.shape[1])]
            copies.append(pltpu.make_async_copy(source, buffer, sems.at[k]))
            copies[-1].start()
            refs[place] = buffer

        def ready():
            for copy in copies:
                copy.wait()

        kernel(ready, *refs)

    return wrapped


def fetched(*shapes):
    return [pltpu.VMEM(shape, kind) for shape, kind in shapes] + [pltpu.SemaphoreType.DMA((len(shapes),))]


def chunk_copies(sources, buffers, sems, chunk, width):
    spot = pl.ds(pl.multiple_of(chunk * width, LANES), width)
    return [
        pltpu.make_async_copy(source.at[:, spot], buffer.at[:, spot], sems.at[k, chunk])
        for k, (source, buffer) in enumerate(zip(sources, buffers))
    ]


def inner_kernel(first, ready, *refs):
    if first:
        s_ref, index_ref, lev_ref, kkt_hbm, act_hbm, lim_hbm, y_hbm, acc_ref, w_ref, *rest = refs
        kkt_ref, act_ref, lim_ref, y_ref, sems, out_sems = rest
        sources, buffers = ((kkt_hbm, act_hbm, lim_hbm), (kkt_ref, act_ref, lim_ref))
        old_ref = None
    else:
        s_ref, index_ref, lev_ref, kkt_hbm, act_hbm, lim_hbm, old_hbm, y_hbm, acc_ref, *rest = refs
        kkt_ref, act_ref, lim_ref, old_ref, y_ref, sems, out_sems = rest
        sources, buffers = ((kkt_hbm, act_hbm, lim_hbm, old_hbm), (kkt_ref, act_ref, lim_ref, old_ref))
        w_ref = None
    upper = upper_half()
    row16 = lax.broadcasted_iota(jnp.int32, (16, LANES), 0)
    sublane = sublanes(SPAN)
    bus_count = s_ref.shape[1]
    inner = index_ref.shape[1]
    groups = bus_count // (GROUP * BLK)
    buses, branches = (bus_count // groups, inner // groups)
    per_pair = branches // (GROUP // 2)

    @pl.loop(0, groups)
    def _(g):
        for copy in chunk_copies(sources, buffers, sems, g, branches):
            copy.start()

    ready()

    def group(g):
        for p in range(GROUP // 2):
            base = g * buses + p * PAIR
            tables = [doubled(s_ref[:, lanes(base + h * LANES)]) for h in range(4)]
            sums = [jnp.zeros((8, SPAN), F32)] * (PAIR // SPAN)
            weights = jnp.zeros((16, SPAN), F32)
            jobs = []
            for t in range(per_pair // LANES):
                cols = lanes(g * branches + p * per_pair + t * LANES)
                ends, near, far, tiles = inner_ends_of(tables, index_ref, base, cols, t, upper)
                penalty = 0.25 * lev_ref[0:1, cols].astype(F32)
                if first:
                    scaled, target = (None, ends)
                else:
                    scaled = old_ref[:, cols] - ends
                    target = ends - scaled
                flows = product(kkt_ref, cols, target)
                flows = jnp.where(act_ref[:, cols] == 1, lim_ref[:, cols], flows)
                y = flows if first else flows + scaled
                y_ref[:, cols] = y
                high, low = halves(spread8(penalty) * y)
                from_part = jnp.where(upper, high, pltpu.roll(low, 4, 0))
                to_part = jnp.where(upper, pltpu.roll(high, 4, 0), low)
                near_span, far_span = (near >> 6, far >> 6)
                near_tile, far_tile = (spread8(near_span), spread8(far_span))
                spans = [2 * h + half for h in tiles for half in range(2)]
                left = [
                    jnp.concatenate(
                        [
                            jnp.where(near_tile == h, from_part, 0.0),
                            jnp.where(far_tile == h, to_part, 0.0),
                        ],
                        axis=1,
                    )
                    for h in spans
                ]
                if first:
                    level = spread8(penalty, 16)
                    left.append(
                        jnp.concatenate(
                            [
                                jnp.where(spread8(near_span, 16) == row16, level, 0.0),
                                jnp.where(spread8(far_span, 16) == row16, level, 0.0),
                            ],
                            axis=1,
                        )
                    )
                right = jnp.concatenate([one_hot(near, sublane), one_hot(far, sublane)], axis=1)
                jobs.append((jnp.concatenate(left, axis=0).astype(BF16), right, spans))
            for left, right, spans in jobs:
                out = contract(left, right)
                for place, h in enumerate(spans):
                    sums[h] = sums[h] + out[8 * place : 8 * place + 8]
                if first:
                    weights = weights + out[8 * len(spans) :]
            for h in range(4):
                spot = lanes(base + h * LANES)
                acc_ref[:, spot] = jnp.concatenate([sums[2 * h], sums[2 * h + 1]], axis=1)
                if first:
                    w_ref[0:1, spot] = jnp.concatenate(
                        [weights[2 * h : 2 * h + 1], weights[2 * h + 1 : 2 * h + 2]], axis=1
                    )

    def out_copy(g):
        spot = pl.ds(pl.multiple_of(g * branches, LANES), branches)
        return pltpu.make_async_copy(y_ref.at[:, spot], y_hbm.at[:, spot], out_sems.at[g])

    @pl.loop(0, groups, step=2)
    def _(start):
        for g in range(2):
            for copy in chunk_copies(sources, buffers, sems, start + g, branches):
                copy.wait()
        for g in range(2):
            group(start + g)
        for g in range(2):
            out_copy(start + g).start()

    @pl.loop(0, groups)
    def _(g):
        out_copy(g).wait()


def list_places(list_ref, g, base):
    count = list_ref.shape[1] // 4
    return [list_ref[0:1, lanes(k * count + g * LANES)] - base for k in range(4)]


def list_picks(tables, places, upper):
    picks = []
    for k in (0, 2):
        both = jnp.where(upper, spread8(places[k]), spread8(places[k + 1]))
        picks.append(pick(tables, both, range(len(tables))))
    return picks


def even_sides():
    return lax.axis_index("gx") % 2 == 0, lax.axis_index("gy") % 2 == 0


def write_blocks(outs, kept, rows):
    even_x, even_y = even_sides()
    count = outs[0].shape[1]

    def block(k):
        return kept[rows, k * count : (k + 1) * count]

    for out, even, at_even, at_odd in (
        (outs[0], even_x, 1, 0),
        (outs[1], even_x, 0, 1),
        (outs[2], even_y, 3, 2),
        (outs[3], even_y, 2, 3),
    ):
        out[rows, :] = jnp.where(even, block(at_even), block(at_odd))


def write_ghosts(outs, picks, g):
    even_x, even_y = even_sides()
    spot = lanes(g * LANES)
    for out_even, out_odd, even, both in (
        (outs[0], outs[1], even_x, picks[0]),
        (outs[2], outs[3], even_y, picks[1]),
    ):
        out_even[0:4, spot] = jnp.where(even, both[:4], both[4:])
        out_odd[0:4, spot] = jnp.where(even, both[4:], both[:4])


def read_ghost(got, block, spot):
    even_x, even_y = even_sides()
    by_even = jnp.where(even_x, block == 1, block == 0) | jnp.where(even_y, block == 3, block == 2)
    return jnp.where(
        block < 2,
        jnp.where(by_even, got[0][0:4, spot], got[1][0:4, spot]),
        jnp.where(by_even, got[2][0:4, spot], got[3][0:4, spot]),
    )


def hv_states(s_ref, hv_bus_ref, work_ref):
    lane = lax.broadcasted_iota(jnp.int32, (1, LANES), 1)

    def body(t, carry):
        bus = hv_bus_ref[t]
        row = s_ref[2:3, lanes((bus >> 7) * LANES)]
        work_ref[pl.ds(t, 1), :] = jnp.where(lane == (bus & (LANES - 1)), row, 0.0)
        return carry

    lax.fori_loop(0, work_ref.shape[0], body, 0, unroll=32)
    return jnp.broadcast_to(jnp.sum(work_ref[...], axis=1, keepdims=True), work_ref.shape)


def as_row(values, width, offset):
    count = values.shape[0]
    wide = jnp.broadcast_to(values[:, :1], (count, width))
    lane = lax.broadcasted_iota(jnp.int32, (count, width), 1)
    own = lax.broadcasted_iota(jnp.int32, (count, width), 0)
    return jnp.sum(jnp.where(lane == own + offset, wide, 0.0), axis=0, keepdims=True)


def write_hv(out_ref, values, penalties):
    width = out_ref.shape[-1]
    row = as_row(values, width, 0) + as_row(penalties, width, values.shape[0])
    out_ref[...] = jnp.broadcast_to(row, out_ref.shape)


def start_kernel(
    bus_ref, level_ref, s_ref, list_ref, from_ref, kkt_ref, act_ref, lim_ref, lev_ref,
    xe_ref, xo_ref, ye_ref, yo_ref, z_ref, hv_ref, hv_own_ref, hv_pen_ref, work_ref, turn_ref, kept_ref,
):
    outs = (xe_ref, xo_ref, ye_ref, yo_ref)
    upper = upper_half()
    values = hv_states(s_ref, bus_ref, work_ref)
    hv_own_ref[...] = values

    def body(t, carry):
        hv_pen_ref[pl.ds(t, 1), :] = jnp.full((1, LANES), level_ref[t], jnp.int32).astype(F32) * 0.25
        return carry

    lax.fori_loop(0, hv_pen_ref.shape[0], body, 0, unroll=32)
    write_hv(hv_ref, values, hv_pen_ref[...])
    groups = s_ref.shape[1] // (GROUP * BLK)
    buses, cross = (GROUP * BLK, from_ref.shape[1] // groups)

    @pl.loop(0, groups, unroll=4)
    def _(g):
        base = g * buses
        tables = [doubled(s_ref[:, lanes(base + h * LANES)]) for h in range(buses // LANES)]
        picks = list_picks(tables, list_places(list_ref, g, base), upper)
        z_ref[0:8, lanes(g * LANES)] = picks[0]
        z_ref[8:16, lanes(g * LANES)] = picks[1]
        write_ghosts(outs, picks, g)
        for t in range(cross // LANES):
            cols = lanes(g * cross + t * LANES)
            index = spread8(from_ref[0:1, cols] - (base + t * PAIR))
            ends = pick(tables[4 * t : 4 * t + 4], index, range(4))
            fixed = act_ref[:, cols] == 1
            part = jnp.where(fixed, lim_ref[:, cols], product(kkt_ref, cols, jnp.where(upper, ends, 0.0)))
            for i in range(8):
                turn_ref[64 * t + 8 * i : 64 * t + 8 * i + 8, :] = kkt_ref[8 * i : 8 * i + 8, cols]
            block = [
                jnp.where(fixed, 0.0, turn_ref[pl.ds(64 * t + 4 + j, 8, stride=8), :])[4:] for j in range(4)
            ]
            kept_ref[0:8, cols] = part
            for j in range(4):
                kept_ref[8 + 4 * j : 12 + 4 * j, cols] = block[j]
            kept_ref[24:25, cols] = 0.25 * lev_ref[0:1, cols].astype(F32)

    for rows in (slice(4, 8), slice(8, 24), slice(24, 25)):
        write_blocks(outs, kept_ref, rows)


def far_hv(first, bus_ref, partner_ref, all_ref, own, penalty, scaled, sum_ref, weight_ref, work_ref, other_ref):
    count = work_ref.shape[0]
    width = all_ref.shape[-1]
    lane = lax.broadcasted_iota(jnp.int32, (1, LANES), 1)
    wide = lax.broadcasted_iota(jnp.int32, (1, width), 1)

    def narrow(row):
        return functools.reduce(jnp.add, [row[:, k : k + LANES] for k in range(0, width, LANES)])

    def fetch(t, carry):
        partner = partner_ref[t]
        device, place = (partner // count, partner % count)
        row = all_ref[pl.ds(device, 1), :]
        work_ref[pl.ds(t, 1), :] = narrow(jnp.where(wide == place, row, 0.0))
        other_ref[pl.ds(t, 1), :] = narrow(jnp.where(wide == place + count, row, 0.0))
        return carry

    lax.fori_loop(0, count, fetch, 0, unroll=32)
    far_value = jnp.sum(work_ref[...], axis=1, keepdims=True)
    far_penalty = jnp.sum(other_ref[...], axis=1, keepdims=True)
    flow = (penalty * own - far_penalty * far_value) / (penalty + far_penalty)
    y = flow if first else flow + scaled
    work_ref[...] = penalty * y
    other_ref[...] = penalty
    sum_ref[...] = jnp.zeros_like(sum_ref)
    if first:
        weight_ref[...] = jnp.zeros_like(weight_ref)

    def place_terms(t, carry):
        bus = bus_ref[t]
        spot = lanes((bus >> 7) * LANES)
        here = lane == (bus & (LANES - 1))
        sum_ref[0:1, spot] += jnp.where(here, work_ref[pl.ds(t, 1), :], 0.0)
        if first:
            weight_ref[0:1, spot] += jnp.where(here, other_ref[pl.ds(t, 1), :], 0.0)
        return carry

    lax.fori_loop(0, count, place_terms, 0, unroll=32)
    return y


def outer_kernel(first, *refs):
    if first:
        (
            bus_ref, partner_ref, all_ref, own_ref, hv_pen_ref, xe, xo, ye, yo, acc_ref, weight_in_ref,
            s_ref, list_ref, from_ref, kkt_ref, act_ref, lim_ref, lev_ref, z_ref, target_ref, prior_ref,
            new_ref, inv_ref, oxe, oxo, oye, oyo, yc_ref, ym_ref, zn_ref, hv_ref, hv_scaled_ref, hv_own_ref,
            sum_ref, hv_weight_ref, work_ref, other_ref, kept_ref,
        ) = refs
        now = (xe, xo, ye, yo)
        scaled = None
    else:
        (
            bus_ref, partner_ref, all_ref, own_ref, hv_pen_ref, scaled_ref, xe, xo, ye, yo, nxe, nxo, nye, nyo,
            acc_ref, inv_ref, s_ref, list_ref, from_ref, kkt_ref, act_ref, lim_ref, lev_ref, z_ref, yc_old_ref,
            ym_old_ref, target_ref, prior_ref,
            new_ref, state_ref, oxe, oxo, oye, oyo, yc_ref, hv_dual_ref,
            sum_ref, work_ref, other_ref,
        ) = refs
        now = (nxe, nxo, nye, nyo)
        hv_weight_ref = None
        scaled = scaled_ref[...]
    fixed_parts = (xe, xo, ye, yo)
    outs = (oxe, oxo, oye, oyo)
    upper = upper_half()
    row8 = lax.broadcasted_iota(jnp.int32, (8, LANES), 0)
    row16 = lax.broadcasted_iota(jnp.int32, (16, LANES), 0)
    power = (row8 == 2) | (row8 == 6)
    sublane = sublanes(LANES)
    even_x, even_y = even_sides()
    groups = s_ref.shape[1] // (GROUP * BLK)
    buses, cross = (GROUP * BLK, from_ref.shape[1] // groups)
    per_list = xe.shape[1] // cross
    count = buses // LANES
    hv_y = far_hv(
        first, bus_ref, partner_ref, all_ref, own_ref[...], hv_pen_ref[...], scaled, sum_ref, hv_weight_ref,
        work_ref, other_ref,
    )

    @pl.loop(0, groups, unroll=8)
    def _(g):
        base = g * buses
        tables = [doubled(s_ref[:, lanes(base + h * LANES)]) for h in range(count)]
        places = list_places(list_ref, g, base)
        sums = [None] * count
        weights = [None] * count
        outputs = []
        for t in range(cross // LANES):
            cols = lanes(g * cross + t * LANES)
            ghost = read_ghost(now, g // per_list, lanes((g % per_list) * cross + t * LANES))
            near = from_ref[0:1, cols] - (base + t * PAIR)
            ends = pick(tables[4 * t : 4 * t + 4], spread8(near), range(4))
            ends = jnp.where(upper, ends, doubled(ghost))
            penalty = 0.25 * lev_ref[0:1, cols].astype(F32)
            if first:
                scaled, target = (None, ends)
            else:
                scaled = yc_old_ref[:, cols] - ends
                target = ends - scaled
            flows = product(kkt_ref, cols, target)
            flows = jnp.where(act_ref[:, cols] == 1, lim_ref[:, cols], flows)
            y = flows if first else flows + scaled
            yc_ref[:, cols] = y
            outputs.append(y)
            high, low = halves(spread8(penalty) * y)
            part = jnp.where(upper, high, pltpu.roll(low, 4, 0))
            tile = spread8(near >> 7)
            left = [jnp.where(tile == h, part, 0.0) for h in range(4)]
            if first:
                left.append(jnp.where(spread8(near >> 7, 16) == row16, spread8(penalty, 16), 0.0))
            out = contract(jnp.concatenate(left, axis=0), one_hot(near, sublane))
            for h in range(4):
                sums[4 * t + h] = out[8 * h : 8 * h + 8]
                if first:
                    weights[4 * t + h] = out[32 + h : 33 + h]

        spot = lanes(g * LANES)
        lefts, rights = ([], [])
        for k, (even, pair) in enumerate(((even_x, 0), (even_x, 1), (even_y, 0), (even_y, 1))):
            start = 0 if k < 2 else 2
            from_even = even if pair == 0 else jnp.logical_not(even)

            def received(parts, rows):
                return jnp.where(from_even, parts[start][rows, spot], parts[start + 1][rows, spot])

            rows = slice(4 * k, 4 * k + 4)
            held = z_ref[rows, spot]
            if first:
                scaled, target = (None, held)
            else:
                scaled = ym_old_ref[rows, spot] - held
                target = held - scaled
            flows = received(now, slice(4, 8))
            for j in range(4):
                flows = flows + received(fixed_parts, slice(8 + 4 * j, 12 + 4 * j)) * spread8(target[j : j + 1], 4)
            penalty = received(fixed_parts, slice(24, 25))
            y = flows if first else flows + scaled
            if first:
                ym_ref[rows, spot] = y
            high, low = halves(spread8(penalty, 4) * y)
            part = jnp.concatenate([high, low], axis=0)
            tile = spread8(places[k] >> 7)
            left = [jnp.where(tile == h, part, 0.0) for h in range(count)]
            if first:
                left.append(jnp.where(spread8(places[k] >> 7, 16) == row16, spread8(penalty, 16), 0.0))
            lefts.append(jnp.concatenate(left, axis=0))
            rights.append(one_hot(places[k], sublane))
        out = contract(jnp.concatenate(lefts[:2], axis=1), jnp.concatenate(rights[:2], axis=1))
        out = out + contract(jnp.concatenate(lefts[2:], axis=1), jnp.concatenate(rights[2:], axis=1))

        fresh = []
        for h in range(count):
            cols = lanes(base + h * LANES)
            total = acc_ref[:, cols] + sums[h] + out[8 * h : 8 * h + 8]
            total = total + pltpu.roll(total, 4, 0)
            total = total + jnp.where(power, spread8(sum_ref[0:1, cols]), 0.0)
            prior = doubled(prior_ref[:, cols])
            total = total + prior * doubled(target_ref[:, cols])
            if first:
                weight = weight_in_ref[0:1, cols] + weights[h] + out[8 * count + h : 8 * count + h + 1]
                weight = spread8(weight) + jnp.where(power, spread8(hv_weight_ref[0:1, cols]), 0.0) + prior
                inverse = 1.0 / weight
                inv_ref[:, cols] = inverse
            else:
                inverse = inv_ref[:, cols]
            state = total * inverse
            new_ref[:, cols] = state
            if not first:
                state_ref[:, cols] = state[:4]
            fresh.append(state)

        picks = list_picks(fresh, places, upper)
        write_ghosts(outs, picks, g)
        if first:
            zn_ref[0:8, spot] = picks[0]
            zn_ref[8:16, spot] = picks[1]
            for t in range(cross // LANES):
                cols = lanes(g * cross + t * LANES)
                near = from_ref[0:1, cols] - (base + t * PAIR)
                ends = pick(fresh[4 * t : 4 * t + 4], spread8(near), range(4))
                target = 2.0 * ends - outputs[t]
                part = product(kkt_ref, cols, jnp.where(upper, target, 0.0))
                kept_ref[:, cols] = jnp.where(act_ref[:, cols] == 1, lim_ref[:, cols], part)

    if first:
        write_blocks(outs, kept_ref, slice(4, 8))
    reached = hv_states(new_ref, bus_ref, work_ref)
    left_over = hv_y - reached
    penalty = hv_pen_ref[...]
    if first:
        hv_scaled_ref[...] = left_over
        hv_own_ref[...] = reached - left_over
        write_hv(hv_ref, reached - left_over, penalty)
    else:
        row = as_row(penalty * left_over, LANES, 0)
        hv_dual_ref[...] = row[:, : hv_dual_ref.shape[1]]


def inner_dual_kernel(s_ref, index_ref, y_ref, lev_ref, dual_ref):
    upper = upper_half()
    groups = s_ref.shape[1] // (GROUP * BLK)
    branches = index_ref.shape[1] // groups
    per_pair = branches // (GROUP // 2)

    @pl.loop(0, groups, unroll=4)
    def _(g):
        for p in range(GROUP // 2):
            base = g * GROUP * BLK + p * PAIR
            tables = [s_ref[:, lanes(base + h * LANES)] for h in range(4)]
            for t in range(per_pair // LANES):
                cols = lanes(g * branches + p * per_pair + t * LANES)
                ends, _, _, _ = inner_ends_of(tables, index_ref, base, cols, t, upper)
                penalty = 0.25 * lev_ref[0:1, cols].astype(F32)
                dual_ref[:, cols] = spread8(penalty) * (y_ref[:, cols] - ends)


def outer_dual_kernel(dual_in_ref, xe, xo, ye, yo, s_ref, from_ref, y_ref, lev_ref, dual_ref):
    upper = upper_half()
    groups = s_ref.shape[1] // (GROUP * BLK)
    cross = from_ref.shape[1] // groups
    per_list = xe.shape[1] // cross

    @pl.loop(0, groups, unroll=8)
    def _(g):
        for t in range(cross // LANES):
            base = g * GROUP * BLK + t * PAIR
            cols = lanes(g * cross + t * LANES)
            ghost = read_ghost((xe, xo, ye, yo), g // per_list, lanes((g % per_list) * cross + t * LANES))
            near = from_ref[0:1, cols] - base
            tables = [s_ref[:, lanes(base + h * LANES)] for h in range(4)]
            ends = pick(tables, spread8(near), range(4))
            ends = jnp.where(upper, ends, doubled(ghost))
            penalty = 0.25 * lev_ref[0:1, cols].astype(F32)
            dual_ref[:, cols] = spread8(penalty) * (y_ref[:, cols] - ends)


def part(rows, width, index=0):
    return pl.BlockSpec((rows, width), lambda g: (0, index))


def scalars():
    return pl.BlockSpec(memory_space=pltpu.SMEM)


def in_place():
    return pl.BlockSpec(memory_space=pl.ANY)


def shape_of(*dims):
    return jax.ShapeDtypeStruct(dims, F32)


def params():
    return pltpu.CompilerParams(
        dimension_semantics=("arbitrary",), vmem_limit_bytes=24 * 1024 * 1024
    )


def cost(flops, moved):
    return pl.CostEstimate(flops=flops, bytes_accessed=moved, transcendentals=0)


def on_device(
    bus_start, bus_target, bus_weight, inner_ends, cross_from, boundary_lists, kkt_map, active_set, limits,
    penalty_level, hv_bus, hv_partner, hv_level,
):
    def hbm(x):
        return pltpu.with_memory_space_constraint(x, pltpu.HBM)

    bus_start, bus_target, bus_weight, inner_ends, boundary_lists, active_set, limits = map(
        hbm, (bus_start, bus_target, bus_weight, inner_ends, boundary_lists, active_set, limits)
    )
    hv_bus, hv_partner, hv_level = map(hbm, (hv_bus, hv_partner, hv_level))
    _, bus_count = bus_start.shape
    list_len = boundary_lists.shape[1] // 4
    inner = inner_ends.shape[1]
    cross = cross_from.shape[0]
    branches = kkt_map.shape[2]
    terms = hv_bus.shape[0]
    devices = lax.axis_size("gx") * lax.axis_size("gy")
    behind = inner // cross
    groups = bus_count // (GROUP * BLK)
    hv_width = max(LANES, 2 * terms)
    kkt = hbm(kkt_map.reshape(64, branches))
    from_row = hbm(cross_from.reshape(1, cross))
    level_row = hbm(penalty_level.reshape(1, branches))
    lists = part(1, 4 * list_len)
    level_in = part(1, inner)
    cross_args = (from_row, kkt, active_set, limits, level_row)
    cross_specs = [part(1, cross), part(64, cross, behind), part(8, cross, behind), part(8, cross, behind), part(1, cross, behind)]
    hv_block = (terms, LANES)
    hv_all_spec = part(devices, hv_width)
    hv_spec = part(*hv_block)
    state_spec, state4_spec, row_spec = (part(8, bus_count), part(4, bus_count), part(1, bus_count))
    held_spec = part(16, list_len)
    common = dict(grid=(1,), compiler_params=params())

    *sent, held, hv_rows, hv_own, hv_pen = pl.pallas_call(
        start_kernel,
        name="first_messages",
        in_specs=[scalars(), scalars(), state4_spec, lists] + cross_specs,
        out_shape=[shape_of(STATIC_ROWS, list_len)] * 4
        + [shape_of(16, list_len), shape_of(devices, hv_width), shape_of(*hv_block), shape_of(*hv_block)],
        out_specs=[part(STATIC_ROWS, list_len)] * 4 + [held_spec, hv_all_spec, hv_spec, hv_spec],
        scratch_shapes=[
            pltpu.VMEM(hv_block, F32),
            pltpu.VMEM((64 * (GROUP // 2), LANES), F32),
            pltpu.VMEM((STATIC_ROWS, cross), F32),
        ],
        cost_estimate=cost(10**6, 4 * 10**6),
        **common,
    )(hv_bus, hv_level, bus_start, boundary_lists, *cross_args)

    def exchange(messages):
        xe, xo, ye, yo = messages
        xo = swapped(xo, "gx", 1)
        yo = swapped(yo, "gy", 1)
        xe = swapped(xe, "gx", 0)
        ye = swapped(ye, "gy", 0)
        return (xe, xo, ye, yo)

    def buffers(count):
        kinds = [F32, jnp.int32, F32, F32][:count]
        return (
            [pltpu.VMEM((64 if k == 0 else 8, inner), kind) for k, kind in enumerate(kinds)]
            + [pltpu.VMEM((8, inner), F32)]
            + [pltpu.SemaphoreType.DMA((count, groups)), pltpu.SemaphoreType.DMA((groups,))]
        )

    inner_small = (((2, inner), jnp.int32), ((1, inner), jnp.int32))
    first_got = exchange(sent)
    hv_all = to_all(hv_rows)
    y_inner, sums, weights = pl.pallas_call(
        fetching(functools.partial(inner_kernel, True), {0: 0, 1: 0, 2: 0}),
        name="inner_first",
        in_specs=[in_place()] * 6,
        out_shape=[shape_of(8, inner), shape_of(8, bus_count), shape_of(1, bus_count)],
        out_specs=[in_place(), state_spec, row_spec],
        scratch_shapes=buffers(3) + fetched(((4, bus_count), F32), *inner_small),
        cost_estimate=cost(10**8, 10**7),
        **common,
    )(bus_start, inner_ends, level_row, kkt, active_set, limits)
    message = part(8, list_len)
    state, inverse, *rest = pl.pallas_call(
        functools.partial(outer_kernel, True),
        name="outer_first",
        in_specs=[scalars()] * 2
        + [hv_all_spec, hv_spec, hv_spec]
        + [part(STATIC_ROWS, list_len)] * 4
        + [state_spec, row_spec, state4_spec, lists]
        + cross_specs
        + [held_spec, state4_spec, state4_spec],
        out_shape=[shape_of(8, bus_count), shape_of(8, bus_count)]
        + [shape_of(8, list_len)] * 4
        + [shape_of(8, cross), pltpu.HBM((16, list_len), F32), pltpu.HBM((16, list_len), F32)]
        + [shape_of(devices, hv_width), pltpu.HBM(hv_block, F32), pltpu.HBM(hv_block, F32)],
        out_specs=[state_spec, state_spec]
        + [message] * 4
        + [part(8, cross), held_spec, held_spec]
        + [hv_all_spec, hv_spec, hv_spec],
        scratch_shapes=[pltpu.VMEM((1, bus_count), F32)] * 2 + [pltpu.VMEM(hv_block, F32)] * 2 + [pltpu.VMEM((8, cross), F32)],
        cost_estimate=cost(10**7, 5 * 10**6),
        **common,
    )(
        hv_bus, hv_partner, hv_all, hv_own, hv_pen, *first_got, sums, weights, bus_start, boundary_lists,
        *cross_args, held, bus_target, bus_weight,
    )
    sent, (y_cross, y_mirror, held, hv_rows, hv_scaled, hv_own) = (rest[:4], rest[4:])
    y_mirror, held, hv_scaled, hv_own = map(hbm, (y_mirror, held, hv_scaled, hv_own))

    second_got = exchange(sent)
    hv_all = to_all(hv_rows)
    y_inner, sums = pl.pallas_call(
        fetching(functools.partial(inner_kernel, False), {0: 0, 1: 0, 2: 0}),
        name="inner_second",
        in_specs=[in_place()] * 7,
        out_shape=[shape_of(8, inner), shape_of(8, bus_count)],
        out_specs=[in_place(), state_spec],
        scratch_shapes=buffers(4) + fetched(((8, bus_count), F32), *inner_small),
        cost_estimate=cost(10**8, 10**7),
        **common,
    )(state, inner_ends, level_row, kkt, active_set, limits, y_inner)
    last = part(4, list_len)
    state, bus_state, *rest = pl.pallas_call(
        functools.partial(outer_kernel, False),
        name="outer_second",
        in_specs=[scalars()] * 2
        + [hv_all_spec, hv_spec, hv_spec, hv_spec]
        + [part(STATIC_ROWS, list_len)] * 4
        + [message] * 4
        + [state_spec, state_spec, state_spec, lists]
        + cross_specs
        + [held_spec, part(8, cross), held_spec, state4_spec, state4_spec],
        out_shape=[shape_of(8, bus_count), shape_of(4, bus_count)]
        + [shape_of(4, list_len)] * 4
        + [shape_of(8, cross), shape_of(1, terms)],
        out_specs=[state_spec, state4_spec] + [last] * 4 + [part(8, cross), part(1, terms)],
        scratch_shapes=[pltpu.VMEM((1, bus_count), F32)] + [pltpu.VMEM(hv_block, F32)] * 2,
        cost_estimate=cost(10**7, 5 * 10**6),
        **common,
    )(
        hv_bus, hv_partner, hv_all, hv_own, hv_pen, hv_scaled, *first_got, *second_got, sums, inverse, state,
        boundary_lists, *cross_args, held, y_cross, y_mirror, bus_target, bus_weight,
    )
    sent, (y_cross, hv_dual) = (rest[:4], rest[4:])

    last_got = exchange(sent)
    duals = pl.pallas_call(
        inner_dual_kernel,
        name="inner_duals",
        in_specs=[state_spec, part(2, inner), part(8, inner), level_in],
        out_shape=shape_of(8, branches),
        out_specs=part(8, inner),
        cost_estimate=cost(10**7, 3 * 10**6),
        **common,
    )(state, inner_ends, y_inner, level_row)
    duals = pl.pallas_call(
        outer_dual_kernel,
        name="outer_duals",
        in_specs=[in_place()] + [last] * 4 + [state_spec, part(1, cross), part(8, cross), part(1, cross, behind)],
        out_shape=shape_of(8, branches),
        out_specs=part(8, cross, behind),
        input_output_aliases={0: 0},
        cost_estimate=cost(10**6, 10**6),
        **common,
    )(duals, *last_got, state, from_row, y_cross, level_row)
    return (bus_state, duals, hv_dual.reshape(terms))


def solution(mesh):
    return jax.shard_map(
        on_device,
        mesh=mesh,
        in_specs=(
            P(None, ("gx", "gy")),
            P(None, ("gx", "gy")),
            P(None, ("gx", "gy")),
            P(None, ("gx", "gy")),
            P(("gx", "gy")),
            P(("gx", "gy"), None),
            P(None, None, ("gx", "gy")),
            P(None, ("gx", "gy")),
            P(None, ("gx", "gy")),
            P(("gx", "gy")),
            P(("gx", "gy")),
            P(("gx", "gy")),
            P(("gx", "gy")),
        ),
        out_specs=(P(None, ("gx", "gy")), P(None, ("gx", "gy")), P(("gx", "gy"))),
        check_vma=False,
    )
```

```python
import functools

import jax
import jax.numpy as jnp
from jax import lax
from jax.experimental import pallas as pl
from jax.experimental.pallas import tpu as pltpu
from jax.sharding import PartitionSpec as P

F32 = jnp.float32
BF16 = jnp.bfloat16
BLK = 256
LANES = 128
GROUP = 8
PAIR = 2 * BLK
SPAN = 64
STATIC_ROWS = 25


def swapped(value, axis, first):
    count = lax.axis_size(axis)
    moves = []
    for low in range(first, count - 1, 2):
        moves += [(low, low + 1), (low + 1, low)]
    return lax.ppermute(value, axis, moves)


def to_all(rows):
    return lax.all_to_all(rows, ("gx", "gy"), split_axis=0, concat_axis=0, tiled=True)


def take_lanes(table, lane):
    return lax.gather(
        table,
        lane[..., None],
        lax.GatherDimensionNumbers(
            offset_dims=(),
            collapsed_slice_dims=(1,),
            start_index_map=(1,),
            operand_batching_dims=(0,),
            start_indices_batching_dims=(0,),
        ),
        (1, 1),
        mode=lax.GatherScatterMode.PROMISE_IN_BOUNDS,
    )


def pick(tables, index, tiles):
    lane, tile = (index & (LANES - 1), index >> 7)
    found = None
    for h in tiles:
        got = take_lanes(tables[h], lane)
        found = got if found is None else jnp.where(tile == h, got, found)
    return found


def spread8(row, rows=8):
    return jnp.broadcast_to(row, (rows, row.shape[-1]))


def one_hot(index, sublane):
    length = sublane.shape[0]
    low = spread8(index & (length - 1), 16).astype(F32).astype(BF16)
    column = jnp.concatenate([low] * (length // 16), axis=0)
    return jnp.where(column == sublane, jnp.ones((), BF16), jnp.zeros((), BF16))


def contract(left, right):
    return lax.dot_general(
        left.astype(BF16), right, (((1,), (1,)), ((), ())), preferred_element_type=F32
    )


def halves(values):
    high = values.astype(BF16).astype(F32)
    return high, values - high


def sublanes(length):
    return lax.broadcasted_iota(jnp.int32, (length, LANES), 0).astype(F32).astype(BF16)


def folded(first, second, distance, mask):
    return jnp.where(
        mask,
        first + pltpu.roll(first, 8 - distance, 0),
        second + pltpu.roll(second, distance, 0),
    )


def product(kkt_ref, cols, target):
    row = lax.broadcasted_iota(jnp.int32, (8, LANES), 0)
    terms = [kkt_ref[8 * i : 8 * i + 8, cols] * target for i in range(8)]
    upper = row < 4
    quads = [
        jnp.where(upper, terms[i], terms[i + 4]) + pltpu.roll(jnp.where(upper, terms[i + 4], terms[i]), 4, 0)
        for i in range(4)
    ]
    even_two = (row & 2) == 0
    twos = [folded(quads[i], quads[i + 2], 2, even_two) for i in range(2)]
    return folded(twos[0], twos[1], 1, (row & 1) == 0)


def doubled(block):
    return block if block.shape[0] == 8 else jnp.concatenate([block, block], axis=0)


def tiles_of(states):
    return [states[:, h * LANES : (h + 1) * LANES] for h in range(states.shape[1] // LANES)]


def lanes(start):
    return pl.ds(pl.multiple_of(start, LANES), LANES)


def upper_half():
    return lax.broadcasted_iota(jnp.int32, (8, LANES), 0) < 4


def inner_ends_of(tables, index_ref, base, cols, t, upper):
    near = index_ref[0:1, cols] - base
    far = index_ref[1:2, cols] - base
    tiles = (0, 1) if t < 2 else (2, 3) if t > 2 else (0, 1, 2, 3)
    both = jnp.where(upper, spread8(near), spread8(far))
    return pick(tables, both, tiles), near, far, tiles


def fetching(kernel, spots):
    def wrapped(*refs):
        *refs, sems = refs
        buffers = refs[len(refs) - len(spots) :]
        refs = list(refs[: len(refs) - len(spots)])
        copies = []
        for k, ((place, first), buffer) in enumerate(zip(spots.items(), buffers)):
            source = refs[place].at[:, pl.ds(first, buffer.shape[1])]
            copies.append(pltpu.make_async_copy(source, buffer, sems.at[k]))
            copies[-1].start()
            refs[place] = buffer

        def ready():
            for copy in copies:
                copy.wait()

        kernel(ready, *refs)

    return wrapped


def fetched(*shapes):
    return [pltpu.VMEM(shape, kind) for shape, kind in shapes] + [pltpu.SemaphoreType.DMA((len(shapes),))]


def chunk_copies(sources, buffers, sems, chunk, width):
    spot = pl.ds(pl.multiple_of(chunk * width, LANES), width)
    return [
        pltpu.make_async_copy(source.at[:, spot], buffer.at[:, spot], sems.at[k, chunk])
        for k, (source, buffer) in enumerate(zip(sources, buffers))
    ]


def inner_kernel(first, ready, *refs):
    if first:
        s_ref, index_ref, lev_ref, kkt_hbm, act_hbm, lim_hbm, y_hbm, acc_ref, w_ref, *rest = refs
        kkt_ref, act_ref, lim_ref, y_ref, sems, out_sems = rest
        sources, buffers = ((kkt_hbm, act_hbm, lim_hbm), (kkt_ref, act_ref, lim_ref))
        old_ref = None
    else:
        s_ref, index_ref, lev_ref, kkt_hbm, act_hbm, lim_hbm, old_hbm, y_hbm, acc_ref, *rest = refs
        kkt_ref, act_ref, lim_ref, old_ref, y_ref, sems, out_sems = rest
        sources, buffers = ((kkt_hbm, act_hbm, lim_hbm, old_hbm), (kkt_ref, act_ref, lim_ref, old_ref))
        w_ref = None
    upper = upper_half()
    row16 = lax.broadcasted_iota(jnp.int32, (16, LANES), 0)
    sublane = sublanes(SPAN)
    bus_count = s_ref.shape[1]
    inner = index_ref.shape[1]
    groups = bus_count // (GROUP * BLK)
    buses, branches = (bus_count // groups, inner // groups)
    per_pair = branches // (GROUP // 2)

    @pl.loop(0, groups)
    def _(g):
        for copy in chunk_copies(sources, buffers, sems, g, branches):
            copy.start()

    ready()

    def group(g):
        for p in range(GROUP // 2):
            base = g * buses + p * PAIR
            tables = [doubled(s_ref[:, lanes(base + h * LANES)]) for h in range(4)]
            sums = [jnp.zeros((8, SPAN), F32)] * (PAIR // SPAN)
            weights = jnp.zeros((16, SPAN), F32)
            jobs = []
            for t in range(per_pair // LANES):
                cols = lanes(g * branches + p * per_pair + t * LANES)
                ends, near, far, tiles = inner_ends_of(tables, index_ref, base, cols, t, upper)
                penalty = 0.25 * lev_ref[0:1, cols].astype(F32)
                if first:
                    scaled, target = (None, ends)
                else:
                    scaled = old_ref[:, cols] - ends
                    target = ends - scaled
                flows = product(kkt_ref, cols, target)
                flows = jnp.where(act_ref[:, cols] == 1, lim_ref[:, cols], flows)
                y = flows if first else flows + scaled
                y_ref[:, cols] = y
                high, low = halves(spread8(penalty) * y)
                from_part = jnp.where(upper, high, pltpu.roll(low, 4, 0))
                to_part = jnp.where(upper, pltpu.roll(high, 4, 0), low)
                near_span, far_span = (near >> 6, far >> 6)
                near_tile, far_tile = (spread8(near_span), spread8(far_span))
                spans = [2 * h + half for h in tiles for half in range(2)]
                left = [
                    jnp.concatenate(
                        [
                            jnp.where(near_tile == h, from_part, 0.0),
                            jnp.where(far_tile == h, to_part, 0.0),
                        ],
                        axis=1,
                    )
                    for h in spans
                ]
                if first:
                    level = spread8(penalty, 16)
                    left.append(
                        jnp.concatenate(
                            [
                                jnp.where(spread8(near_span, 16) == row16, level, 0.0),
                                jnp.where(spread8(far_span, 16) == row16, level, 0.0),
                            ],
                            axis=1,
                        )
                    )
                right = jnp.concatenate([one_hot(near, sublane), one_hot(far, sublane)], axis=1)
                jobs.append((jnp.concatenate(left, axis=0).astype(BF16), right, spans))
            for left, right, spans in jobs:
                out = contract(left, right)
                for place, h in enumerate(spans):
                    sums[h] = sums[h] + out[8 * place : 8 * place + 8]
                if first:
                    weights = weights + out[8 * len(spans) :]
            for h in range(4):
                spot = lanes(base + h * LANES)
                acc_ref[:, spot] = jnp.concatenate([sums[2 * h], sums[2 * h + 1]], axis=1)
                if first:
                    w_ref[0:1, spot] = jnp.concatenate(
                        [weights[2 * h : 2 * h + 1], weights[2 * h + 1 : 2 * h + 2]], axis=1
                    )

    def out_copy(g):
        spot = pl.ds(pl.multiple_of(g * branches, LANES), branches)
        return pltpu.make_async_copy(y_ref.at[:, spot], y_hbm.at[:, spot], out_sems.at[g])

    @pl.loop(0, groups, step=2)
    def _(start):
        for g in range(2):
            for copy in chunk_copies(sources, buffers, sems, start + g, branches):
                copy.wait()
        for g in range(2):
            group(start + g)
        for g in range(2):
            out_copy(start + g).start()

    @pl.loop(0, groups)
    def _(g):
        out_copy(g).wait()


def list_places(list_ref, g, base):
    count = list_ref.shape[1] // 4
    return [list_ref[0:1, lanes(k * count + g * LANES)] - base for k in range(4)]


def list_picks(tables, places, upper):
    picks = []
    for k in (0, 2):
        both = jnp.where(upper, spread8(places[k]), spread8(places[k + 1]))
        picks.append(pick(tables, both, range(len(tables))))
    return picks


def even_sides():
    return lax.axis_index("gx") % 2 == 0, lax.axis_index("gy") % 2 == 0


def write_blocks(outs, kept, rows):
    even_x, even_y = even_sides()
    count = outs[0].shape[1]

    def block(k):
        return kept[rows, k * count : (k + 1) * count]

    for out, even, at_even, at_odd in (
        (outs[0], even_x, 1, 0),
        (outs[1], even_x, 0, 1),
        (outs[2], even_y, 3, 2),
        (outs[3], even_y, 2, 3),
    ):
        out[rows, :] = jnp.where(even, block(at_even), block(at_odd))


def write_ghosts(outs, picks, g):
    even_x, even_y = even_sides()
    spot = lanes(g * LANES)
    for out_even, out_odd, even, both in (
        (outs[0], outs[1], even_x, picks[0]),
        (outs[2], outs[3], even_y, picks[1]),
    ):
        out_even[0:4, spot] = jnp.where(even, both[:4], both[4:])
        out_odd[0:4, spot] = jnp.where(even, both[4:], both[:4])


def read_ghost(got, block, spot):
    even_x, even_y = even_sides()
    by_even = jnp.where(even_x, block == 1, block == 0) | jnp.where(even_y, block == 3, block == 2)
    return jnp.where(
        block < 2,
        jnp.where(by_even, got[0][0:4, spot], got[1][0:4, spot]),
        jnp.where(by_even, got[2][0:4, spot], got[3][0:4, spot]),
    )


def hv_states(s_ref, hv_bus_ref, work_ref):
    lane = lax.broadcasted_iota(jnp.int32, (1, LANES), 1)

    def body(t, carry):
        bus = hv_bus_ref[t]
        row = s_ref[2:3, lanes((bus >> 7) * LANES)]
        work_ref[pl.ds(t, 1), :] = jnp.where(lane == (bus & (LANES - 1)), row, 0.0)
        return carry

    lax.fori_loop(0, work_ref.shape[0], body, 0, unroll=32)
    return jnp.broadcast_to(jnp.sum(work_ref[...], axis=1, keepdims=True), work_ref.shape)


def as_row(values, width, offset):
    count = values.shape[0]
    wide = jnp.broadcast_to(values[:, :1], (count, width))
    lane = lax.broadcasted_iota(jnp.int32, (count, width), 1)
    own = lax.broadcasted_iota(jnp.int32, (count, width), 0)
    return jnp.sum(jnp.where(lane == own + offset, wide, 0.0), axis=0, keepdims=True)


def write_hv(out_ref, values, penalties):
    width = out_ref.shape[-1]
    row = as_row(values, width, 0) + as_row(penalties, width, values.shape[0])
    out_ref[...] = jnp.broadcast_to(row, out_ref.shape)


def start_kernel(
    bus_ref, level_ref, s_ref, list_ref, from_ref, kkt_ref, act_ref, lim_ref, lev_ref,
    xe_ref, xo_ref, ye_ref, yo_ref, z_ref, hv_ref, hv_own_ref, hv_pen_ref, work_ref, turn_ref, kept_ref,
):
    outs = (xe_ref, xo_ref, ye_ref, yo_ref)
    upper = upper_half()
    values = hv_states(s_ref, bus_ref, work_ref)
    hv_own_ref[...] = values

    def body(t, carry):
        hv_pen_ref[pl.ds(t, 1), :] = jnp.full((1, LANES), level_ref[t], jnp.int32).astype(F32) * 0.25
        return carry

    lax.fori_loop(0, hv_pen_ref.shape[0], body, 0, unroll=32)
    write_hv(hv_ref, values, hv_pen_ref[...])
    groups = s_ref.shape[1] // (GROUP * BLK)
    buses, cross = (GROUP * BLK, from_ref.shape[1] // groups)

    @pl.loop(0, groups, unroll=8)
    def _(g):
        base = g * buses
        tables = [doubled(s_ref[:, lanes(base + h * LANES)]) for h in range(buses // LANES)]
        picks = list_picks(tables, list_places(list_ref, g, base), upper)
        z_ref[0:8, lanes(g * LANES)] = picks[0]
        z_ref[8:16, lanes(g * LANES)] = picks[1]
        write_ghosts(outs, picks, g)
        for t in range(cross // LANES):
            cols = lanes(g * cross + t * LANES)
            index = spread8(from_ref[0:1, cols] - (base + t * PAIR))
            ends = pick(tables[4 * t : 4 * t + 4], index, range(4))
            fixed = act_ref[:, cols] == 1
            part = jnp.where(fixed, lim_ref[:, cols], product(kkt_ref, cols, jnp.where(upper, ends, 0.0)))
            for i in range(8):
                turn_ref[64 * t + 8 * i : 64 * t + 8 * i + 8, :] = kkt_ref[8 * i : 8 * i + 8, cols]
            block = [
                jnp.where(fixed, 0.0, turn_ref[pl.ds(64 * t + 4 + j, 8, stride=8), :])[4:] for j in range(4)
            ]
            kept_ref[0:8, cols] = part
            for j in range(4):
                kept_ref[8 + 4 * j : 12 + 4 * j, cols] = block[j]
            kept_ref[24:25, cols] = 0.25 * lev_ref[0:1, cols].astype(F32)

    for rows in (slice(4, 8), slice(8, 24), slice(24, 25)):
        write_blocks(outs, kept_ref, rows)


def far_hv(first, bus_ref, partner_ref, all_ref, own, penalty, scaled, sum_ref, weight_ref, work_ref, other_ref):
    count = work_ref.shape[0]
    width = all_ref.shape[-1]
    lane = lax.broadcasted_iota(jnp.int32, (1, LANES), 1)
    wide = lax.broadcasted_iota(jnp.int32, (1, width), 1)

    def narrow(row):
        return functools.reduce(jnp.add, [row[:, k : k + LANES] for k in range(0, width, LANES)])

    def fetch(t, carry):
        partner = partner_ref[t]
        device, place = (partner // count, partner % count)
        row = all_ref[pl.ds(device, 1), :]
        work_ref[pl.ds(t, 1), :] = narrow(jnp.where(wide == place, row, 0.0))
        other_ref[pl.ds(t, 1), :] = narrow(jnp.where(wide == place + count, row, 0.0))
        return carry

    lax.fori_loop(0, count, fetch, 0, unroll=32)
    far_value = jnp.sum(work_ref[...], axis=1, keepdims=True)
    far_penalty = jnp.sum(other_ref[...], axis=1, keepdims=True)
    flow = (penalty * own - far_penalty * far_value) / (penalty + far_penalty)
    y = flow if first else flow + scaled
    work_ref[...] = penalty * y
    other_ref[...] = penalty
    sum_ref[...] = jnp.zeros_like(sum_ref)
    if first:
        weight_ref[...] = jnp.zeros_like(weight_ref)

    def place_terms(t, carry):
        bus = bus_ref[t]
        spot = lanes((bus >> 7) * LANES)
        here = lane == (bus & (LANES - 1))
        sum_ref[0:1, spot] += jnp.where(here, work_ref[pl.ds(t, 1), :], 0.0)
        if first:
            weight_ref[0:1, spot] += jnp.where(here, other_ref[pl.ds(t, 1), :], 0.0)
        return carry

    lax.fori_loop(0, count, place_terms, 0, unroll=32)
    return y


def outer_kernel(first, *refs):
    if first:
        (
            bus_ref, partner_ref, all_ref, own_ref, hv_pen_ref, xe, xo, ye, yo, acc_ref, weight_in_ref,
            s_ref, list_ref, from_ref, kkt_ref, act_ref, lim_ref, lev_ref, z_ref, target_ref, prior_ref,
            new_ref, inv_ref, oxe, oxo, oye, oyo, yc_ref, ym_ref, zn_ref, hv_ref, hv_scaled_ref, hv_own_ref,
            sum_ref, hv_weight_ref, work_ref, other_ref, kept_ref,
        ) = refs
        now = (xe, xo, ye, yo)
        scaled = None
    else:
        (
            bus_ref, partner_ref, all_ref, own_ref, hv_pen_ref, scaled_ref, xe, xo, ye, yo, nxe, nxo, nye, nyo,
            acc_ref, inv_ref, s_ref, list_ref, from_ref, kkt_ref, act_ref, lim_ref, lev_ref, z_ref, yc_old_ref,
            ym_old_ref, target_ref, prior_ref,
            new_ref, state_ref, oxe, oxo, oye, oyo, yc_ref, hv_dual_ref,
            sum_ref, work_ref, other_ref,
        ) = refs
        now = (nxe, nxo, nye, nyo)
        hv_weight_ref = None
        scaled = scaled_ref[...]
    fixed_parts = (xe, xo, ye, yo)
    outs = (oxe, oxo, oye, oyo)
    upper = upper_half()
    row8 = lax.broadcasted_iota(jnp.int32, (8, LANES), 0)
    row16 = lax.broadcasted_iota(jnp.int32, (16, LANES), 0)
    power = (row8 == 2) | (row8 == 6)
    sublane = sublanes(LANES)
    even_x, even_y = even_sides()
    groups = s_ref.shape[1] // (GROUP * BLK)
    buses, cross = (GROUP * BLK, from_ref.shape[1] // groups)
    per_list = xe.shape[1] // cross
    count = buses // LANES
    hv_y = far_hv(
        first, bus_ref, partner_ref, all_ref, own_ref[...], hv_pen_ref[...], scaled, sum_ref, hv_weight_ref,
        work_ref, other_ref,
    )

    @pl.loop(0, groups, unroll=8)
    def _(g):
        base = g * buses
        tables = [doubled(s_ref[:, lanes(base + h * LANES)]) for h in range(count)]
        places = list_places(list_ref, g, base)
        sums = [None] * count
        weights = [None] * count
        outputs = []
        for t in range(cross // LANES):
            cols = lanes(g * cross + t * LANES)
            ghost = read_ghost(now, g // per_list, lanes((g % per_list) * cross + t * LANES))
            near = from_ref[0:1, cols] - (base + t * PAIR)
            ends = pick(tables[4 * t : 4 * t + 4], spread8(near), range(4))
            ends = jnp.where(upper, ends, doubled(ghost))
            penalty = 0.25 * lev_ref[0:1, cols].astype(F32)
            if first:
                scaled, target = (None, ends)
            else:
                scaled = yc_old_ref[:, cols] - ends
                target = ends - scaled
            flows = product(kkt_ref, cols, target)
            flows = jnp.where(act_ref[:, cols] == 1, lim_ref[:, cols], flows)
            y = flows if first else flows + scaled
            yc_ref[:, cols] = y
            outputs.append(y)
            high, low = halves(spread8(penalty) * y)
            part = jnp.where(upper, high, pltpu.roll(low, 4, 0))
            tile = spread8(near >> 7)
            left = [jnp.where(tile == h, part, 0.0) for h in range(4)]
            if first:
                left.append(jnp.where(spread8(near >> 7, 16) == row16, spread8(penalty, 16), 0.0))
            out = contract(jnp.concatenate(left, axis=0), one_hot(near, sublane))
            for h in range(4):
                sums[4 * t + h] = out[8 * h : 8 * h + 8]
                if first:
                    weights[4 * t + h] = out[32 + h : 33 + h]

        spot = lanes(g * LANES)
        lefts, rights = ([], [])
        for k, (even, pair) in enumerate(((even_x, 0), (even_x, 1), (even_y, 0), (even_y, 1))):
            start = 0 if k < 2 else 2
            from_even = even if pair == 0 else jnp.logical_not(even)

            def received(parts, rows):
                return jnp.where(from_even, parts[start][rows, spot], parts[start + 1][rows, spot])

            rows = slice(4 * k, 4 * k + 4)
            held = z_ref[rows, spot]
            if first:
                scaled, target = (None, held)
            else:
                scaled = ym_old_ref[rows, spot] - held
                target = held - scaled
            flows = received(now, slice(4, 8))
            for j in range(4):
                flows = flows + received(fixed_parts, slice(8 + 4 * j, 12 + 4 * j)) * spread8(target[j : j + 1], 4)
            penalty = received(fixed_parts, slice(24, 25))
            y = flows if first else flows + scaled
            if first:
                ym_ref[rows, spot] = y
            high, low = halves(spread8(penalty, 4) * y)
            part = jnp.concatenate([high, low], axis=0)
            tile = spread8(places[k] >> 7)
            left = [jnp.where(tile == h, part, 0.0) for h in range(count)]
            if first:
                left.append(jnp.where(spread8(places[k] >> 7, 16) == row16, spread8(penalty, 16), 0.0))
            lefts.append(jnp.concatenate(left, axis=0))
            rights.append(one_hot(places[k], sublane))
        out = contract(jnp.concatenate(lefts[:2], axis=1), jnp.concatenate(rights[:2], axis=1))
        out = out + contract(jnp.concatenate(lefts[2:], axis=1), jnp.concatenate(rights[2:], axis=1))

        fresh = []
        for h in range(count):
            cols = lanes(base + h * LANES)
            total = acc_ref[:, cols] + sums[h] + out[8 * h : 8 * h + 8]
            total = total + pltpu.roll(total, 4, 0)
            total = total + jnp.where(power, spread8(sum_ref[0:1, cols]), 0.0)
            prior = doubled(prior_ref[:, cols])
            total = total + prior * doubled(target_ref[:, cols])
            if first:
                weight = weight_in_ref[0:1, cols] + weights[h] + out[8 * count + h : 8 * count + h + 1]
                weight = spread8(weight) + jnp.where(power, spread8(hv_weight_ref[0:1, cols]), 0.0) + prior
                inverse = 1.0 / weight
                inv_ref[:, cols] = inverse
            else:
                inverse = inv_ref[:, cols]
            state = total * inverse
            new_ref[:, cols] = state
            if not first:
                state_ref[:, cols] = state[:4]
            fresh.append(state)

        picks = list_picks(fresh, places, upper)
        write_ghosts(outs, picks, g)
        if first:
            zn_ref[0:8, spot] = picks[0]
            zn_ref[8:16, spot] = picks[1]
            for t in range(cross // LANES):
                cols = lanes(g * cross + t * LANES)
                near = from_ref[0:1, cols] - (base + t * PAIR)
                ends = pick(fresh[4 * t : 4 * t + 4], spread8(near), range(4))
                target = 2.0 * ends - outputs[t]
                part = product(kkt_ref, cols, jnp.where(upper, target, 0.0))
                kept_ref[:, cols] = jnp.where(act_ref[:, cols] == 1, lim_ref[:, cols], part)

    if first:
        write_blocks(outs, kept_ref, slice(4, 8))
    reached = hv_states(new_ref, bus_ref, work_ref)
    left_over = hv_y - reached
    penalty = hv_pen_ref[...]
    if first:
        hv_scaled_ref[...] = left_over
        hv_own_ref[...] = reached - left_over
        write_hv(hv_ref, reached - left_over, penalty)
    else:
        row = as_row(penalty * left_over, LANES, 0)
        hv_dual_ref[...] = row[:, : hv_dual_ref.shape[1]]


def inner_dual_kernel(s_ref, index_ref, y_ref, lev_ref, dual_ref):
    upper = upper_half()
    groups = s_ref.shape[1] // (GROUP * BLK)
    branches = index_ref.shape[1] // groups
    per_pair = branches // (GROUP // 2)

    @pl.loop(0, groups, unroll=8)
    def _(g):
        for p in range(GROUP // 2):
            base = g * GROUP * BLK + p * PAIR
            tables = [s_ref[:, lanes(base + h * LANES)] for h in range(4)]
            for t in range(per_pair // LANES):
                cols = lanes(g * branches + p * per_pair + t * LANES)
                ends, _, _, _ = inner_ends_of(tables, index_ref, base, cols, t, upper)
                penalty = 0.25 * lev_ref[0:1, cols].astype(F32)
                dual_ref[:, cols] = spread8(penalty) * (y_ref[:, cols] - ends)


def outer_dual_kernel(dual_in_ref, xe, xo, ye, yo, s_ref, from_ref, y_ref, lev_ref, dual_ref):
    upper = upper_half()
    groups = s_ref.shape[1] // (GROUP * BLK)
    cross = from_ref.shape[1] // groups
    per_list = xe.shape[1] // cross

    @pl.loop(0, groups, unroll=8)
    def _(g):
        for t in range(cross // LANES):
            base = g * GROUP * BLK + t * PAIR
            cols = lanes(g * cross + t * LANES)
            ghost = read_ghost((xe, xo, ye, yo), g // per_list, lanes((g % per_list) * cross + t * LANES))
            near = from_ref[0:1, cols] - base
            tables = [s_ref[:, lanes(base + h * LANES)] for h in range(4)]
            ends = pick(tables, spread8(near), range(4))
            ends = jnp.where(upper, ends, doubled(ghost))
            penalty = 0.25 * lev_ref[0:1, cols].astype(F32)
            dual_ref[:, cols] = spread8(penalty) * (y_ref[:, cols] - ends)


def part(rows, width, index=0):
    return pl.BlockSpec((rows, width), lambda g: (0, index))


def scalars():
    return pl.BlockSpec(memory_space=pltpu.SMEM)


def in_place():
    return pl.BlockSpec(memory_space=pl.ANY)


def shape_of(*dims):
    return jax.ShapeDtypeStruct(dims, F32)


def params():
    return pltpu.CompilerParams(
        dimension_semantics=("arbitrary",), vmem_limit_bytes=24 * 1024 * 1024
    )


def cost(flops, moved):
    return pl.CostEstimate(flops=flops, bytes_accessed=moved, transcendentals=0)


def on_device(
    bus_start, bus_target, bus_weight, inner_ends, cross_from, boundary_lists, kkt_map, active_set, limits,
    penalty_level, hv_bus, hv_partner, hv_level,
):
    def hbm(x):
        return pltpu.with_memory_space_constraint(x, pltpu.HBM)

    bus_start, bus_target, bus_weight, inner_ends, boundary_lists, active_set, limits = map(
        hbm, (bus_start, bus_target, bus_weight, inner_ends, boundary_lists, active_set, limits)
    )
    hv_bus, hv_partner, hv_level = map(hbm, (hv_bus, hv_partner, hv_level))
    _, bus_count = bus_start.shape
    list_len = boundary_lists.shape[1] // 4
    inner = inner_ends.shape[1]
    cross = cross_from.shape[0]
    branches = kkt_map.shape[2]
    terms = hv_bus.shape[0]
    devices = lax.axis_size("gx") * lax.axis_size("gy")
    behind = inner // cross
    groups = bus_count // (GROUP * BLK)
    hv_width = max(LANES, 2 * terms)
    kkt = hbm(kkt_map.reshape(64, branches))
    from_row = hbm(cross_from.reshape(1, cross))
    level_row = hbm(penalty_level.reshape(1, branches))
    lists = part(1, 4 * list_len)
    level_in = part(1, inner)
    cross_args = (from_row, kkt, active_set, limits, level_row)
    cross_specs = [part(1, cross), part(64, cross, behind), part(8, cross, behind), part(8, cross, behind), part(1, cross, behind)]
    hv_block = (terms, LANES)
    hv_all_spec = part(devices, hv_width)
    hv_spec = part(*hv_block)
    state_spec, state4_spec, row_spec = (part(8, bus_count), part(4, bus_count), part(1, bus_count))
    held_spec = part(16, list_len)
    common = dict(grid=(1,), compiler_params=params())

    *sent, held, hv_rows, hv_own, hv_pen = pl.pallas_call(
        start_kernel,
        name="first_messages",
        in_specs=[scalars(), scalars(), state4_spec, lists] + cross_specs,
        out_shape=[shape_of(STATIC_ROWS, list_len)] * 4
        + [shape_of(16, list_len), shape_of(devices, hv_width), shape_of(*hv_block), shape_of(*hv_block)],
        out_specs=[part(STATIC_ROWS, list_len)] * 4 + [held_spec, hv_all_spec, hv_spec, hv_spec],
        scratch_shapes=[
            pltpu.VMEM(hv_block, F32),
            pltpu.VMEM((64 * (GROUP // 2), LANES), F32),
            pltpu.VMEM((STATIC_ROWS, cross), F32),
        ],
        cost_estimate=cost(10**6, 4 * 10**6),
        **common,
    )(hv_bus, hv_level, bus_start, boundary_lists, *cross_args)

    def exchange(messages):
        xe, xo, ye, yo = messages
        xo = swapped(xo, "gx", 1)
        yo = swapped(yo, "gy", 1)
        xe = swapped(xe, "gx", 0)
        ye = swapped(ye, "gy", 0)
        return (xe, xo, ye, yo)

    def buffers(count):
        kinds = [F32, jnp.int32, F32, F32][:count]
        return (
            [pltpu.VMEM((64 if k == 0 else 8, inner), kind) for k, kind in enumerate(kinds)]
            + [pltpu.VMEM((8, inner), F32)]
            + [pltpu.SemaphoreType.DMA((count, groups)), pltpu.SemaphoreType.DMA((groups,))]
        )

    inner_small = (((2, inner), jnp.int32), ((1, inner), jnp.int32))
    first_got = exchange(sent)
    hv_all = to_all(hv_rows)
    y_inner, sums, weights = pl.pallas_call(
        fetching(functools.partial(inner_kernel, True), {0: 0, 1: 0, 2: 0}),
        name="inner_first",
        in_specs=[in_place()] * 6,
        out_shape=[shape_of(8, inner), shape_of(8, bus_count), shape_of(1, bus_count)],
        out_specs=[in_place(), state_spec, row_spec],
        scratch_shapes=buffers(3) + fetched(((4, bus_count), F32), *inner_small),
        cost_estimate=cost(10**8, 10**7),
        **common,
    )(bus_start, inner_ends, level_row, kkt, active_set, limits)
    message = part(8, list_len)
    state, inverse, *rest = pl.pallas_call(
        functools.partial(outer_kernel, True),
        name="outer_first",
        in_specs=[scalars()] * 2
        + [hv_all_spec, hv_spec, hv_spec]
        + [part(STATIC_ROWS, list_len)] * 4
        + [state_spec, row_spec, state4_spec, lists]
        + cross_specs
        + [held_spec, state4_spec, state4_spec],
        out_shape=[shape_of(8, bus_count), shape_of(8, bus_count)]
        + [shape_of(8, list_len)] * 4
        + [shape_of(8, cross), pltpu.HBM((16, list_len), F32), pltpu.HBM((16, list_len), F32)]
        + [shape_of(devices, hv_width), pltpu.HBM(hv_block, F32), pltpu.HBM(hv_block, F32)],
        out_specs=[state_spec, state_spec]
        + [message] * 4
        + [part(8, cross), held_spec, held_spec]
        + [hv_all_spec, hv_spec, hv_spec],
        scratch_shapes=[pltpu.VMEM((1, bus_count), F32)] * 2 + [pltpu.VMEM(hv_block, F32)] * 2 + [pltpu.VMEM((8, cross), F32)],
        cost_estimate=cost(10**7, 5 * 10**6),
        **common,
    )(
        hv_bus, hv_partner, hv_all, hv_own, hv_pen, *first_got, sums, weights, bus_start, boundary_lists,
        *cross_args, held, bus_target, bus_weight,
    )
    sent, (y_cross, y_mirror, held, hv_rows, hv_scaled, hv_own) = (rest[:4], rest[4:])
    y_mirror, held, hv_scaled, hv_own = map(hbm, (y_mirror, held, hv_scaled, hv_own))

    second_got = exchange(sent)
    hv_all = to_all(hv_rows)
    y_inner, sums = pl.pallas_call(
        fetching(functools.partial(inner_kernel, False), {0: 0, 1: 0, 2: 0}),
        name="inner_second",
        in_specs=[in_place()] * 7,
        out_shape=[shape_of(8, inner), shape_of(8, bus_count)],
        out_specs=[in_place(), state_spec],
        scratch_shapes=buffers(4) + fetched(((8, bus_count), F32), *inner_small),
        cost_estimate=cost(10**8, 10**7),
        **common,
    )(state, inner_ends, level_row, kkt, active_set, limits, y_inner)
    last = part(4, list_len)
    state, bus_state, *rest = pl.pallas_call(
        functools.partial(outer_kernel, False),
        name="outer_second",
        in_specs=[scalars()] * 2
        + [hv_all_spec, hv_spec, hv_spec, hv_spec]
        + [part(STATIC_ROWS, list_len)] * 4
        + [message] * 4
        + [state_spec, state_spec, state_spec, lists]
        + cross_specs
        + [held_spec, part(8, cross), held_spec, state4_spec, state4_spec],
        out_shape=[shape_of(8, bus_count), shape_of(4, bus_count)]
        + [shape_of(4, list_len)] * 4
        + [shape_of(8, cross), shape_of(1, terms)],
        out_specs=[state_spec, state4_spec] + [last] * 4 + [part(8, cross), part(1, terms)],
        scratch_shapes=[pltpu.VMEM((1, bus_count), F32)] + [pltpu.VMEM(hv_block, F32)] * 2,
        cost_estimate=cost(10**7, 5 * 10**6),
        **common,
    )(
        hv_bus, hv_partner, hv_all, hv_own, hv_pen, hv_scaled, *first_got, *second_got, sums, inverse, state,
        boundary_lists, *cross_args, held, y_cross, y_mirror, bus_target, bus_weight,
    )
    sent, (y_cross, hv_dual) = (rest[:4], rest[4:])

    last_got = exchange(sent)
    duals = pl.pallas_call(
        inner_dual_kernel,
        name="inner_duals",
        in_specs=[state_spec, part(2, inner), part(8, inner), level_in],
        out_shape=shape_of(8, branches),
        out_specs=part(8, inner),
        cost_estimate=cost(10**7, 3 * 10**6),
        **common,
    )(state, inner_ends, y_inner, level_row)
    duals = pl.pallas_call(
        outer_dual_kernel,
        name="outer_duals",
        in_specs=[in_place()] + [last] * 4 + [state_spec, part(1, cross), part(8, cross), part(1, cross, behind)],
        out_shape=shape_of(8, branches),
        out_specs=part(8, cross, behind),
        input_output_aliases={0: 0},
        cost_estimate=cost(10**6, 10**6),
        **common,
    )(duals, *last_got, state, from_row, y_cross, level_row)
    return (bus_state, duals, hv_dual.reshape(terms))


def solution(mesh):
    return jax.shard_map(
        on_device,
        mesh=mesh,
        in_specs=(
            P(None, ("gx", "gy")),
            P(None, ("gx", "gy")),
            P(None, ("gx", "gy")),
            P(None, ("gx", "gy")),
            P(("gx", "gy")),
            P(("gx", "gy"), None),
            P(None, None, ("gx", "gy")),
            P(None, ("gx", "gy")),
            P(None, ("gx", "gy")),
            P(("gx", "gy")),
            P(("gx", "gy")),
            P(("gx", "gy")),
            P(("gx", "gy")),
        ),
        out_specs=(P(None, ("gx", "gy")), P(None, ("gx", "gy")), P(("gx", "gy"))),
        check_vma=False,
    )
```
